32 devices in a mesh: rep: 2 (over y), shard: 16 (over z, x, core).
Axes of the slice: x: 2, y: 2, z: 4, core: 2. Of those that a mesh axis runs over, the one named last changes fastest.
Arguments:
- inputs: bfloat16 [32, 1024, 512], P(('rep', 'shard')), may hold values from -6 to 6
- segment_ids: int32 [32, 1024], P(('rep', 'shard')), may hold values from 0 to 3, never falling along the last dimension, each value on 1 to 800 neighbouring positions
- w_query: bfloat16 [512, 512], P('shard'), may hold values from -0.25 to 0.25
- w_key: bfloat16 [512, 512], P('shard'), may hold values from -0.25 to 0.25
- w_value: bfloat16 [512, 512], P('shard'), may hold values from -0.25 to 0.25
- w_out: bfloat16 [512, 512], P('shard'), may hold values from -3 to 3
- w_up: bfloat16 [512, 2048], P('shard'), may hold values from -0.25 to 0.25
- w_down: bfloat16 [2048, 512], P('shard'), may hold values from -0.125 to 0.125
- b_up: bfloat16 [2048], P('shard'), may hold values from -3 to 3
- b_down: bfloat16 [512], P('shard'), may hold values from -2 to 2
- gain_attn: bfloat16 [512], P('shard'), may hold values from 0.5 to 1.5
- shift_attn: bfloat16 [512], P('shard'), may hold values from -2 to 2
- gain_ffn: bfloat16 [512], P('shard'), may hold values from 0.5 to 1.5
- shift_ffn: bfloat16 [512], P('shard'), may hold values from -2 to 2
- cotangent: bfloat16 [32, 1024, 512], P(('rep', 'shard')), may hold values from -6 to 6
Outputs:
- output: bfloat16 [32, 1024, 512], P(('rep', 'shard'))
- grad_inputs: float32 [32, 1024, 512], P(('rep', 'shard'))
- grad_w_query: float32 [512, 512], P('shard')
- grad_w_key: float32 [512, 512], P('shard')
- grad_w_value: float32 [512, 512], P('shard')
- grad_w_out: float32 [512, 512], P('shard')
- grad_w_up: float32 [512, 2048], P('shard')
- grad_w_down: float32 [2048, 512], P('shard')
- grad_b_up: float32 [2048], P('shard')
- grad_b_down: float32 [512], P('shard')
- grad_gain_attn: float32 [512], P('shard')
- grad_shift_attn: float32 [512], P('shard')
- grad_gain_ffn: float32 [512], P('shard')
- grad_shift_ffn: float32 [512], P('shard')
The draws below stay inside these ranges and needn't reach their ends.
Inputs may be any that keep to these rules, and one draw needn't show every extreme that they name: `segment_ids`: within a sequence the ids never fall, each document is one run of equal ids, and the longest document has 800 tokens.
All inputs are finite; a program needn't handle non-finite values.
Results may differ from the reference program's by a relative error of at most 0.04.
Values may be sent and summed in bfloat16 or wider, within the bound.
A program may use at most 128 MiB of HBM per device.

```python
import math
import jax
import jax.numpy as jnp
import numpy as np
from jax import lax

D = 512
HEADS = 8
HEAD_DIM = 64
FF = 2048
SEQ = 1024
DOCS = 4
DOC_MOST = 800
SEQS = 32


def level_of(stream_key, shape, cuts, low, high):
    level, own = 1.0, jax.random.fold_in(stream_key, 6)
    for axis_at, parts in cuts:
        heights = jnp.exp(jax.random.uniform(jax.random.fold_in(own, axis_at), (parts,), jnp.float32, low / len(cuts), high / len(cuts)))
        level = level * jnp.repeat(heights, shape[axis_at] // parts).reshape([-1 if axis == axis_at else 1 for axis in range(len(shape))])
    return level


def length_profile(count, total, bound, lean):
    weights = [(1 << 20) // math.isqrt(grade ** lean) + 1 for grade in range(2, count + 1)]
    rest, holding = total - bound - (count - 1), [1] * (count - 1)
    while rest > 0:
        free = [i for i in range(count - 1) if holding[i] < bound]
        pool, left = sum([weights[i] for i in free]), rest
        for i in free:
            extra = min(bound - holding[i], max(1, left * weights[i] // pool), rest)
            holding[i] = holding[i] + extra
            rest = rest - extra
    return np.array([bound] + holding)


def uneven(key, count, total, limit, slope):
    if count == 2:
        one = jax.random.randint(key, (), max(1, total - limit), min(limit, total - 1) + 1)
        return jnp.stack([one, total - one])
    tallies = jnp.asarray(length_profile(count, total, limit, slope), jnp.int32)
    pairs = (count - 1) // 2
    source_of, receiver = tallies[1:1 + 2 * pairs:2], tallies[2:2 + 2 * pairs:2]
    room = jnp.minimum(source_of - 1, limit - receiver)
    shifted = jax.random.randint(jax.random.fold_in(key, 1), (pairs,), 0, 1 << 20) % (room + 1)
    tallies = tallies.at[1:1 + 2 * pairs:2].set(source_of - shifted).at[2:2 + 2 * pairs:2].set(receiver + shifted)
    return tallies[jax.random.permutation(jax.random.fold_in(key, 2), count)]


def gaussian(key, shape, spread, reach, split=(), held_as=jnp.bfloat16):
    values = jax.random.normal(key, shape, jnp.float32) * spread
    if len(split) > 0:
        values = level_of(key, shape, split, -0.22, 0.18) * values
    return jnp.clip(values, min=-reach, max=reach).astype(held_as)


def setup_inputs(seed: int = 0) -> dict:
    keys = jax.random.split(jax.random.key(seed), 16)
    inputs = gaussian(keys[0], (SEQS, SEQ, D), 1.0, 6.0, ((0, 32),))
    segment_ids = jax.vmap(lambda own: jnp.searchsorted(jnp.cumsum(uneven(own, DOCS, SEQ, DOC_MOST, 1)), jnp.arange(SEQ), side="right"))(jax.random.split(keys[1], SEQS)).reshape((SEQS, SEQ)).astype(jnp.int32)
    w_query = gaussian(keys[2], (D, D), D ** -0.5, 0.25, ((0, 16),))
    w_key = gaussian(keys[3], (D, D), D ** -0.5, 0.25, ((0, 16),))
    w_value = gaussian(keys[4], (D, D), D ** -0.5, 0.25, ((0, 16),))
    w_out = gaussian(keys[5], (D, D), (max(D // 128, 1)) ** -0.5, 3.0, ((0, 16),))
    w_up = gaussian(keys[6], (D, FF), D ** -0.5, 0.25, ((0, 16),))
    w_down = gaussian(keys[7], (FF, D), FF ** -0.5, 0.125, ((0, 16),))
    b_up = gaussian(keys[8], (FF,), 0.5, 3.0, ((0, 16),))
    b_down = gaussian(keys[9], (D,), 0.3, 2.0, ((0, 16),))
    gain_attn = jnp.clip(1.0 + 0.1 * jax.random.normal(keys[10], (D,), jnp.float32), 0.5, 1.5).astype(jnp.bfloat16)
    shift_attn = gaussian(keys[11], (D,), 0.3, 2.0, ((0, 16),))
    gain_ffn = jnp.clip(1.0 + 0.1 * jax.random.normal(keys[12], (D,), jnp.float32), 0.5, 1.5).astype(jnp.bfloat16)
    shift_ffn = gaussian(keys[13], (D,), 0.3, 2.0, ((0, 16),))
    cotangent = gaussian(keys[14], (SEQS, SEQ, D), 1.0, 6.0, ((0, 32),))
    return dict(inputs=inputs, segment_ids=segment_ids, w_query=w_query, w_key=w_key, w_value=w_value, w_out=w_out, w_up=w_up, w_down=w_down, b_up=b_up, b_down=b_down, gain_attn=gain_attn, shift_attn=shift_attn, gain_ffn=gain_ffn, shift_ffn=shift_ffn, cotangent=cotangent)


epsilon = 1e-05
highest = lax.Precision.HIGHEST

@jax.custom_vjp
def low(v):
    return lax.optimization_barrier(v.astype(jnp.bfloat16)).astype(jnp.float32)

@jax.custom_vjp
def low_back(v):
    return v

def low_keep(v):
    return (low(v), None)

def low_pass(kept, grad):
    return (grad,)

def back_keep(v):
    return (v, None)

def back_low(kept, grad):
    return (low(grad),)
low.defvjp(low_keep, low_pass)
low_back.defvjp(back_keep, back_low)

def layer_norm(hidden, gain, shift):
    centre = hidden - lax.optimization_barrier(jnp.mean(hidden, axis=-1, keepdims=True))
    scale = lax.rsqrt(lax.optimization_barrier(jnp.mean(centre * centre, axis=-1, keepdims=True)) + epsilon)
    return centre * scale * gain + shift

def project(left, right):
    return jnp.dot(left, right, preferred_element_type=jnp.float32, precision=highest)

def feature(values):
    return jax.nn.elu(values) + 1.0

def sequence_forward(hidden, segments, weights):
    w_query, w_key, w_value, w_out, w_up, w_down, b_up, b_down, gain_attn, shift_attn, gain_ffn, shift_ffn = weights
    length = hidden.shape[0]
    block_rows = min(512, length)
    normed = low(layer_norm(hidden, gain_attn, shift_attn))
    queries = low_back(project(normed, w_query))
    keys_raw = low_back(project(normed, w_key))
    values = low(low_back(project(normed, w_value)))
    query_feat = low(feature(queries)).reshape(length, HEADS, HEAD_DIM)
    key_feat = low(feature(keys_raw)).reshape(length, HEADS, HEAD_DIM)
    value_heads = values.reshape(length, HEADS, HEAD_DIM)
    positions = jnp.arange(length, dtype=jnp.int32)

    def attend(offset):
        query_block = lax.dynamic_slice_in_dim(query_feat, offset, block_rows, 0)
        segment_block = lax.dynamic_slice_in_dim(segments, offset, block_rows, 0)
        query_pos = offset + jnp.arange(block_rows, dtype=jnp.int32)
        visible = (segment_block[:, None] == segments[None, :]) & (positions[None, :] <= query_pos[:, None])
        scores = jnp.einsum('qhd,khd->hqk', query_block, key_feat, precision=highest)
        masked = low_back(jnp.where(visible[None], scores, 0.0))
        totals = lax.optimization_barrier(jnp.sum(masked, axis=-1))
        mixed = low_back(jnp.einsum('hqk,khd->qhd', low(masked), value_heads, precision=highest))
        return mixed / jnp.transpose(totals)[:, :, None]
    offsets = jnp.arange(length // block_rows, dtype=jnp.int32) * block_rows
    context = lax.map(jax.checkpoint(attend), offsets).reshape(length, HEADS * HEAD_DIM)
    attn_out = low_back(project(low(low_back(context)), w_out))
    after_attn = hidden + attn_out
    normed_ffn = low(layer_norm(after_attn, gain_ffn, shift_ffn))
    pre_act = low_back(project(normed_ffn, w_up) + b_up)
    return after_attn + project(low(jax.nn.gelu(pre_act)), w_down) + b_down

def reference(inputs, segment_ids, w_query, w_key, w_value, w_out, w_up, w_down, b_up, b_down, gain_attn, shift_attn, gain_ffn, shift_ffn, cotangent):
    weights = tuple((item.astype(jnp.float32) for item in (w_query, w_key, w_value, w_out, w_up, w_down, b_up, b_down, gain_attn, shift_attn, gain_ffn, shift_ffn)))
    hidden_all = inputs.astype(jnp.float32)

    def forward(hidden_in, params):

        def single(packed):
            return sequence_forward(packed[0], packed[1], params)
        return lax.map(jax.checkpoint(single), (hidden_in, segment_ids))
    result, pullback = jax.vjp(forward, hidden_all, weights)
    grad_inputs, gradients = pullback(cotangent.astype(jnp.float32))
    return (result.astype(jnp.bfloat16), grad_inputs, gradients[0], gradients[1], gradients[2], gradients[3], gradients[4], gradients[5], gradients[6], gradients[7], gradients[8], gradients[9], gradients[10], gradients[11])
```

```python
import functools

import jax
import jax.numpy as jnp
from jax import lax
from jax.experimental import pallas as pl
from jax.experimental.pallas import tpu as pltpu
from jax.sharding import PartitionSpec as P

HEADS = 8
HEAD_DIM = 64
WIDTH = 512

epsilon = 1e-05
MESH = pl.DeviceIdType.MESH


class Place:
    def __init__(self, reps, shards):
        self.reps, self.shards = reps, shards
        self.A = 4
        self.B = shards // 8
        self.r = lax.axis_index("rep")
        s = lax.axis_index("shard")
        self.s = s
        self.c = lax.rem(s, 2)
        self.b = lax.rem(s // 2, self.B)
        self.a = s // (2 * self.B)
        self.h = lax.rem(self.r, 2)

    def at(self, a=None, b=None, c=None, r=None):
        a = self.a if a is None else a
        b = self.b if b is None else b
        c = self.c if c is None else c
        r = self.r if r is None else r
        return (r, (a * self.B + b) * 2 + c)

    def sibling(self):
        return self.at(c=1 - self.c)

    def twin(self, bit=1):
        return self.at(r=self.r + bit - 2 * bit * lax.rem(self.r // bit, 2))

    def bits(self):
        bit, out = 2, []
        while bit < self.reps:
            out.append(bit)
            bit *= 2
        return out

    def partners(self, wide):
        out = [self.sibling(), self.twin()]
        out += [self.at(a=lax.rem(self.a + j, self.A)) for j in range(1, self.A)]
        out += [self.at(b=lax.rem(self.b + j, self.B)) for j in range(1, self.B)]
        if wide:
            out += [self.twin(bit) for bit in self.bits()]
        return out


def greet(partners):
    barrier = pltpu.get_barrier_semaphore()
    for device in partners:
        pl.semaphore_signal(barrier, inc=1, device_id=device, device_id_type=MESH)
    pl.semaphore_wait(barrier, len(partners))


def remote(src, dst, send, recv, device):
    return pltpu.make_async_remote_copy(
        src_ref=src, dst_ref=dst, send_sem=send, recv_sem=recv, device_id=device, device_id_type=MESH
    )


def guarded(cond, body):
    if cond is None:
        body()
    else:
        pl.when(cond)(body)


class Sends:
    def __init__(self):
        self.made = []

    def go(self, cond, make):
        guarded(cond, lambda: make().start())
        self.made.append((cond, make))

    def finish(self):
        for cond, make in self.made:
            guarded(cond, lambda: make().wait_send())
        self.made = []


class Gather:
    def __init__(self, place, full, lo, rows, send, recv, sends):
        self.p, self.full, self.lo, self.rows = place, full, lo, rows
        self.send, self.recv, self.sends = send, recv, sends

    def whole(self, a, b, c):
        return self.full.at[a, b, c, pl.ds(self.lo, self.rows)]

    def half(self, a, b, c, h):
        size = self.rows // 2
        return self.full.at[a, b, c, pl.ds(pl.multiple_of(self.lo + h * size, 16), size)]

    def push(self, cond, ref, a, b, kind, half_id, device):
        c = self.p.c
        self.sends.go(
            cond,
            lambda: remote(ref, ref, self.send.at[a, b, kind], self.recv.at[a, b, c, half_id], device),
        )

    def await_(self, cond, ref, a, b, c, half_id):
        guarded(
            cond,
            lambda: remote(
                ref, ref, self.send.at[a, b, 0], self.recv.at[a, b, c, half_id], self.p.sibling()
            ).wait_recv(),
        )

    def both(self, one, two):
        if one is None:
            return two
        return one if two is None else jnp.logical_and(one, two)

    def along_b(self, cond, a, b, step):
        p = self.p
        if step <= 0:
            self.push(
                self.both(cond, p.b > 0), self.half(a, b, p.c, p.h), a, b, 2, 0, p.at(b=p.b - 1)
            )
        if step >= 0:
            self.push(
                self.both(cond, p.b < p.B - 1), self.half(a, b, p.c, p.h), a, b, 3, 0, p.at(b=p.b + 1)
            )

    def column(self, cond, a, step):
        p = self.p
        block = self.whole(a, p.b, p.c)
        if step <= 0:
            self.push(self.both(cond, p.a > 0), block, a, p.b, 0, 0, p.at(a=p.a - 1))
        if step >= 0:
            self.push(self.both(cond, p.a < p.A - 1), block, a, p.b, 1, 0, p.at(a=p.a + 1))
        self.along_b(cond, a, p.b, 0)
        self.push(cond, block, a, p.b, 5, 0, p.sibling())

    def own(self):
        self.column(None, self.p.a, 0)

    def lines(self, k):
        p = self.p
        if k == 0:
            return [(None, p.a, 0)]
        return [(p.a - k >= 0, p.a - k, 1), (p.a + k < p.A, p.a + k, -1)]

    def columns(self, k):
        for cond, a, step in self.lines(k):
            self.await_(cond, self.whole(a, self.p.b, self.p.c), a, self.p.b, self.p.c, 0)
            self.column(cond, a, step)

    def rows_b(self, k):
        p = self.p
        for cond, a, _ in self.lines(k):
            for j in range(1, p.B):
                for step in (1, -1):
                    b = p.b - j * step
                    here = self.both(cond, (b >= 0) if step > 0 else (b < p.B))
                    ref = self.half(a, b, p.c, p.h)
                    self.await_(here, ref, a, b, p.c, 0)
                    self.along_b(here, a, b, step)
                    self.push(here, ref, a, b, 4, 1, p.twin())
                    self.push(here, ref, a, b, 5, 0, p.sibling())

    def rows_twin(self, k):
        p = self.p
        for cond, a, _ in self.lines(k):
            for j in range(1, p.B):
                b = lax.rem(p.b + j, p.B)
                ref = self.half(a, b, p.c, 1 - p.h)
                self.await_(cond, ref, a, b, p.c, 1)
                self.push(cond, ref, a, b, 6, 1, p.sibling())

    def rest(self):
        p = self.p
        for a in range(p.A):
            self.await_(None, self.whole(a, p.b, 1 - p.c), a, p.b, 1 - p.c, 0)
            for j in range(1, p.B):
                b = lax.rem(p.b + j, p.B)
                self.await_(None, self.half(a, b, 1 - p.c, p.h), a, b, 1 - p.c, 0)
                self.await_(None, self.half(a, b, 1 - p.c, 1 - p.h), a, b, 1 - p.c, 1)

    def steps(self):
        A = self.p.A
        out = [self.own]
        for k in range(1, A + 2):
            if k < A:
                out.append(functools.partial(self.columns, k))
            if k - 1 < A:
                out.append(functools.partial(self.rows_b, k - 1))
            if 0 <= k - 2 < A:
                out.append(functools.partial(self.rows_twin, k - 2))
        out.append(self.rest)
        return out


class SmallGather:
    def __init__(self, place, full, send, recv, sends):
        self.p, self.full, self.send, self.recv, self.sends = place, full, send, recv, sends

    def copy(self, ref, k, device):
        return remote(ref, ref, self.send.at[k], self.recv.at[k], device)

    def go(self, ref, k, device):
        self.sends.go(None, lambda: self.copy(ref, k, device))

    def own(self):
        p = self.p
        for j in range(1, p.A):
            self.go(self.full.at[p.a, p.b, p.c], j, p.at(a=lax.rem(p.a + j, p.A)))

    def second(self):
        p = self.p
        for j in range(1, p.A):
            self.copy(self.full.at[lax.rem(p.a + p.A - j, p.A), p.b, p.c], j, p.sibling()).wait_recv()
        for j in range(1, p.B):
            self.go(self.full.at[:, p.b, p.c], p.A + j, p.at(b=lax.rem(p.b + j, p.B)))

    def third(self):
        p = self.p
        for j in range(1, p.B):
            self.copy(
                self.full.at[:, lax.rem(p.b + p.B - j, p.B), p.c], p.A + j, p.sibling()
            ).wait_recv()
        self.go(self.full.at[:, :, p.c], 0, p.sibling())

    def last(self):
        p = self.p
        self.copy(self.full.at[:, :, 1 - p.c], 0, p.sibling()).wait_recv()


class Reduce:
    def __init__(self, place, part, bufs, lo, rows, at, lanes, send, recv, sends):
        self.p, self.part, self.lo, self.rows, self.at, self.lanes = place, part, lo, rows, at, lanes
        self.core, self.line_b, self.pair, self.line_a, self.wide, self.done = bufs
        self.send, self.recv, self.sends = send, recv, sends
        self.size = rows // 2

    def win(self):
        return (pl.ds(self.lo, self.rows), pl.ds(self.at, self.lanes))

    def halfwin(self, h):
        return (
            pl.ds(pl.multiple_of(self.lo + h * self.size, 16), self.size),
            pl.ds(self.at, self.lanes),
        )

    def copy(self, src, dst, k, device):
        return remote(src, dst, self.send.at[k], self.recv.at[k], device)

    def go(self, src, dst, k, device):
        self.sends.go(None, lambda: self.copy(src, dst, k, device))

    def start(self):
        p = self.p
        for j in list(range(1, p.B)) + [0]:
            b = lax.rem(p.b + j, p.B)
            self.go(
                self.part.at[(slice(None), b, 1 - p.c) + self.win()],
                self.core.at[(slice(None), j) + self.win()],
                j,
                p.sibling(),
            )

    def after_core(self):
        p, base = self.p, self.p.B
        for j in list(range(1, p.B)) + [0]:
            b = lax.rem(p.b + j, p.B)
            mine = (slice(None), b, p.c) + self.win()
            got = (slice(None), j) + self.win()
            self.copy(self.core.at[got], self.core.at[got], j, p.sibling()).wait_recv()
            self.part[mine] = self.part[mine] + self.core[got]
            if j > 0:
                self.go(
                    self.part.at[mine],
                    self.line_b.at[(j - 1, slice(None)) + self.win()],
                    base + j,
                    p.at(b=b),
                )

    def after_b(self):
        p, base = self.p, self.p.B
        mine = (slice(None), p.b, p.c) + self.win()
        total = self.part[mine].astype(jnp.float32)
        for j in range(1, p.B):
            got = (j - 1, slice(None)) + self.win()
            self.copy(self.line_b.at[got], self.line_b.at[got], base + j, p.sibling()).wait_recv()
            total = total + self.line_b[got].astype(jnp.float32)
        self.part[mine] = total.astype(jnp.bfloat16)
        give = (slice(None),) + self.halfwin(1 - p.h)
        self.go(
            self.part.at[(slice(None), p.b, p.c) + self.halfwin(1 - p.h)],
            self.pair.at[give],
            2 * base,
            p.twin(),
        )

    def after_pair(self):
        p, base = self.p, 2 * self.p.B
        got = (slice(None),) + self.halfwin(p.h)
        self.copy(self.pair.at[got], self.pair.at[got], base, p.twin()).wait_recv()
        mine = (slice(None), p.b, p.c) + self.halfwin(p.h)
        self.part[mine] = self.part[mine] + self.pair[got]
        for j in range(1, p.A):
            a = lax.rem(p.a + j, p.A)
            self.go(
                self.part.at[(a, p.b, p.c) + self.halfwin(p.h)],
                self.line_a.at[(j - 1,) + self.halfwin(p.h)],
                base + j,
                p.at(a=a),
            )

    def after_a(self):
        p, base = self.p, 2 * self.p.B
        mine = self.halfwin(p.h)
        total = self.part[(p.a, p.b, p.c) + mine].astype(jnp.float32)
        for j in range(1, p.A):
            got = (j - 1,) + mine
            self.copy(self.line_a.at[got], self.line_a.at[got], base + j, p.sibling()).wait_recv()
            total = total + self.line_a[got].astype(jnp.float32)
        for i, bit in enumerate(p.bits()):
            k = base + p.A + 1 + i
            self.wide[(2 * i,) + mine] = total.astype(jnp.bfloat16)
            src, dst = self.wide.at[(2 * i,) + mine], self.wide.at[(2 * i + 1,) + mine]
            self.go(src, dst, k, p.twin(bit))
            self.copy(src, dst, k, p.twin(bit)).wait_recv()
            total = self.wide[(2 * i,) + mine].astype(jnp.float32) + self.wide[
                (2 * i + 1,) + mine
            ].astype(jnp.float32)
        self.done[mine] = total.astype(jnp.bfloat16)
        self.go(self.done.at[mine], self.done.at[mine], base + p.A, p.twin())

    def finish(self):
        p = self.p
        got = self.halfwin(1 - p.h)
        self.copy(self.done.at[got], self.done.at[got], 2 * p.B + p.A, p.twin()).wait_recv()

    def steps(self):
        return [self.start, self.after_core, self.after_b, self.after_pair, self.after_a, self.finish]

    @staticmethod
    def n_sems(reps, shards):
        wide = max(reps.bit_length() - 2, 0)
        return 2 * (shards // 8) + 4 + 1 + wide


class SmallReduce:
    def __init__(self, place, slots, send, recv, sends):
        self.p, self.slots, self.send, self.recv, self.sends = place, slots, send, recv, sends
        self.now, self.free, self.k = 0, 1, 0

    def exchange(self, devices):
        self.fresh = []
        for device in devices:
            self.fresh.append((self.free, self.k))
            now, free, k = self.now, self.free, self.k
            self.sends.go(
                None,
                lambda now=now, free=free, k=k, device=device: remote(
                    self.slots.at[now], self.slots.at[free], self.send.at[k], self.recv.at[k], device
                ),
            )
            self.free, self.k = self.free + 1, self.k + 1

    def add(self):
        total = self.slots[self.now]
        for slot, k in self.fresh:
            remote(
                self.slots.at[slot],
                self.slots.at[slot],
                self.send.at[k],
                self.recv.at[k],
                self.p.sibling(),
            ).wait_recv()
            total = total + self.slots[slot]
        self.slots[self.free] = total
        self.now, self.free = self.free, self.free + 1

    def steps(self):
        p = self.p
        stages = [
            [p.sibling()],
            [p.at(b=lax.rem(p.b + j, p.B)) for j in range(1, p.B)],
            [p.twin()],
            [p.at(a=lax.rem(p.a + j, p.A)) for j in range(1, p.A)],
        ] + [[p.twin(bit)] for bit in p.bits()]
        out = [lambda: self.exchange(stages[0])]
        for stage in stages[1:]:
            out.append(lambda stage=stage: (self.add(), self.exchange(stage)))
        out.append(self.add)
        return out

    @staticmethod
    def counts(reps, shards):
        wide = max(reps.bit_length() - 2, 0)
        copies = 1 + (shards // 8 - 1) + 1 + 3 + wide
        return copies, 1 + copies + 4 + wide


def gather_kernel(reps, shards, q, k, v, o, up, down, small, full, smalls, send, recv, send0, recv0, local):
    p = Place(reps, shards)
    rows = q.shape[0]
    mine = full.at[p.a, p.b, p.c]
    pieces = [(ref, mine.at[pl.ds(i * rows, rows)]) for i, ref in enumerate((q, k, v, o))]
    pieces += [
        (up.at[:, pl.ds(i * WIDTH, WIDTH)], mine.at[pl.ds((4 + i) * rows, rows)]) for i in range(4)
    ]
    pieces += [(down, mine.at[pl.ds(8 * rows, 4 * rows)]), (small, smalls.at[p.a, p.b, p.c])]
    copies = [pltpu.make_async_copy(src, dst, local.at[i]) for i, (src, dst) in enumerate(pieces)]
    for copy in copies:
        copy.start()
    greet(p.partners(False))
    for copy in copies:
        copy.wait()
    sends = Sends()
    tiny = SmallGather(p, smalls, send0, recv0, sends)
    first = Gather(p, full, 0, 4 * rows, send.at[0], recv.at[0], sends)
    second = Gather(p, full, 4 * rows, 8 * rows, send.at[1], recv.at[1], sends)
    tiny.own()
    one, two = first.steps(), second.steps()
    for i in range(len(one)):
        one[i]()
        if i == 3:
            tiny.second()
        if i == 6:
            tiny.third()
    tiny.last()
    for step in two:
        step()
    sends.finish()


def gather_all(reps, shards, weights, small):
    rows = weights[0].shape[0]
    A, B = 4, shards // 8
    n_local = 10
    return pl.pallas_call(
        functools.partial(gather_kernel, reps, shards),
        out_shape=(
            jax.ShapeDtypeStruct((A, B, 2, 12 * rows, WIDTH), jnp.bfloat16),
            jax.ShapeDtypeStruct((A, B, 2, 8, 128), jnp.float32),
        ),
        in_specs=[pl.BlockSpec(memory_space=pltpu.VMEM)] * 7,
        out_specs=(pl.BlockSpec(memory_space=pltpu.VMEM),) * 2,
        scratch_shapes=[
            pltpu.SemaphoreType.DMA((2, A, B, 7)),
            pltpu.SemaphoreType.DMA((2, A, B, 2, 2)),
            pltpu.SemaphoreType.DMA((A + B,)),
            pltpu.SemaphoreType.DMA((A + B,)),
            pltpu.SemaphoreType.DMA((n_local,)),
        ],
        compiler_params=pltpu.CompilerParams(
            collective_id=1, has_side_effects=True, vmem_limit_bytes=40 << 20
        ),
        name="gather_weights",
    )(*weights, small)


def reduce_kernel(reps, shards, grads, tiny, out, tiny_out, part, *scratch):
    core, line_b, pair, line_a, wide, done, slots, send, recv, send0, recv0, local = scratch
    p = Place(reps, shards)
    load = pltpu.make_async_copy(grads, part, local.at[0])
    load.start()
    load0 = pltpu.make_async_copy(tiny, slots.at[0], local.at[1])
    load0.start()
    greet(p.partners(True))
    load.wait()
    load0.wait()
    rows = part.shape[3] // 12
    sends = Sends()
    bufs = (core, line_b, pair, line_a, wide, done)
    jobs = [
        Reduce(p, part, bufs, lo * rows, n * rows, 0, WIDTH, send.at[i], recv.at[i], sends)
        for i, (lo, n) in enumerate(((0, 4), (4, 4), (8, 4)))
    ]
    small = SmallReduce(p, slots, send0, recv0, sends)
    all_steps = [job.steps() for job in jobs]
    small_steps = small.steps()
    small_steps[0]()
    count = len(all_steps[0])
    for t in range(count + len(jobs) - 1):
        for i, steps in enumerate(all_steps):
            if 0 <= t - i < count:
                steps[t - i]()
        if 1 <= t + 1 < len(small_steps):
            small_steps[t + 1]()
    out[...] = done[...].astype(jnp.float32)
    tiny_out[...] = slots[small.now]
    sends.finish()


def reduce_all(reps, shards, grads, tiny):
    A, B = 4, shards // 8
    rows = grads.shape[3]
    wide = max(2 * (reps.bit_length() - 2), 1)
    jobs = 3
    per_job = Reduce.n_sems(reps, shards)
    copies, slots = SmallReduce.counts(reps, shards)
    return pl.pallas_call(
        functools.partial(reduce_kernel, reps, shards),
        out_shape=(
            jax.ShapeDtypeStruct((rows, WIDTH), jnp.float32),
            jax.ShapeDtypeStruct(tiny.shape, jnp.float32),
        ),
        in_specs=[pl.BlockSpec(memory_space=pl.ANY)] * 2,
        out_specs=(pl.BlockSpec(memory_space=pltpu.VMEM),) * 2,
        scratch_shapes=[
            pltpu.VMEM(grads.shape, jnp.bfloat16),
            pltpu.VMEM((A, B, rows, WIDTH), jnp.bfloat16),
            pltpu.VMEM((B - 1, A, rows, WIDTH), jnp.bfloat16),
            pltpu.VMEM((A, rows, WIDTH), jnp.bfloat16),
            pltpu.VMEM((A - 1, rows, WIDTH), jnp.bfloat16),
            pltpu.VMEM((wide, rows, WIDTH), jnp.bfloat16),
            pltpu.VMEM((rows, WIDTH), jnp.bfloat16),
            pltpu.VMEM((slots,) + tiny.shape, jnp.float32),
            pltpu.SemaphoreType.DMA((jobs, per_job)),
            pltpu.SemaphoreType.DMA((jobs, per_job)),
            pltpu.SemaphoreType.DMA((copies,)),
            pltpu.SemaphoreType.DMA((copies,)),
            pltpu.SemaphoreType.DMA((2,)),
        ],
        compiler_params=pltpu.CompilerParams(
            collective_id=2, has_side_effects=True, vmem_limit_bytes=50 << 20
        ),
        name="reduce_grads",
    )(grads, tiny)


def layer_norm(hidden, gain, shift):
    centre = hidden - jnp.mean(hidden, axis=-1, keepdims=True)
    scale = lax.rsqrt(jnp.mean(centre * centre, axis=-1, keepdims=True) + epsilon)
    normal = centre * scale
    return (normal * gain + shift, normal, scale)


def norm_back(grad_out, normal, scale, gain):
    grad_normal = grad_out * gain
    grad_hidden = scale * (
        grad_normal
        - jnp.mean(grad_normal, axis=-1, keepdims=True)
        - normal * jnp.mean(grad_normal * normal, axis=-1, keepdims=True)
    )
    return (grad_hidden, jnp.sum(grad_out * normal, axis=0), jnp.sum(grad_out, axis=0))


def feature(values):
    return jax.nn.elu(values) + 1.0


def causal_visible(segments, offset, block_rows):
    length = segments.shape[0]
    query_pos = offset + jnp.arange(block_rows, dtype=jnp.int32)
    key_pos = jnp.arange(length, dtype=jnp.int32)
    query_seg = segments[offset : offset + block_rows]
    return (query_seg[:, None] == segments[None, :]) & (key_pos[None, :] <= query_pos[:, None])


def attend_forward(packed):
    query_feat, key_feat, values, segments = packed
    length = query_feat.shape[0]
    block_rows = min(512, length)
    contexts = []
    totals_all = []
    for offset in range(0, length, block_rows):
        visible = causal_visible(segments, offset, block_rows)
        scores = jnp.einsum(
            "qhd,khd->hqk",
            query_feat[offset : offset + block_rows],
            key_feat,
            preferred_element_type=jnp.float32,
        )
        masked = jnp.where(visible[None], scores, 0.0)
        totals = jnp.transpose(jnp.sum(masked, axis=-1))
        mixed = jnp.einsum(
            "hqk,khd->qhd", masked.astype(jnp.bfloat16), values, preferred_element_type=jnp.float32
        )
        contexts.append(mixed / totals[:, :, None])
        totals_all.append(totals)
    return (jnp.concatenate(contexts, axis=0), jnp.concatenate(totals_all, axis=0))


def attend_backward(packed):
    query_feat, key_feat, values, segments, grad_mixed, grad_totals = packed
    length = query_feat.shape[0]
    block_rows = min(512, length)
    query_parts = []
    grad_keys = jnp.zeros(key_feat.shape, jnp.float32)
    grad_values = jnp.zeros(values.shape, jnp.float32)
    for offset in range(0, length, block_rows):
        visible = causal_visible(segments, offset, block_rows)
        query_block = query_feat[offset : offset + block_rows]
        mixed_block = grad_mixed[offset : offset + block_rows]
        scores = jnp.einsum(
            "qhd,khd->hqk", query_block, key_feat, preferred_element_type=jnp.float32
        )
        rounded = jnp.where(visible[None], scores, 0.0).astype(jnp.bfloat16)
        grad_weights = jnp.einsum(
            "qhd,khd->hqk", mixed_block, values, preferred_element_type=jnp.float32
        )
        grad_weights = (
            grad_weights + jnp.transpose(grad_totals[offset : offset + block_rows])[:, :, None]
        ).astype(jnp.bfloat16)
        grad_scores = jnp.where(visible[None], grad_weights, jnp.zeros((), jnp.bfloat16))
        query_parts.append(
            jnp.einsum("hqk,khd->qhd", grad_scores, key_feat, preferred_element_type=jnp.float32)
        )
        grad_keys = grad_keys + jnp.einsum(
            "hqk,qhd->khd", grad_scores, query_block, preferred_element_type=jnp.float32
        )
        grad_values = grad_values + jnp.einsum(
            "hqk,qhd->khd", rounded, mixed_block, preferred_element_type=jnp.float32
        )
    return (jnp.concatenate(query_parts, axis=0), grad_keys, grad_values)


def on_device(
    reps,
    shards,
    inputs,
    segment_ids,
    w_query,
    w_key,
    w_value,
    w_out,
    w_up,
    w_down,
    b_up,
    b_down,
    gain_attn,
    shift_attn,
    gain_ffn,
    shift_ffn,
    cotangent,
):
    sequences, length, model_width = inputs.shape
    row_count = sequences * length
    rows = w_query.shape[0]
    A, B = 4, shards // 8

    def padded(vec):
        return jnp.pad(vec.astype(jnp.float32), (0, 128 - vec.shape[0]))[None]

    small = jnp.concatenate(
        [padded(v) for v in (b_up, b_down, gain_attn, shift_attn, gain_ffn, shift_ffn)]
        + [jnp.zeros((2, 128), jnp.float32)],
        axis=0,
    )
    full, smalls = gather_all(reps, shards, (w_query, w_key, w_value, w_out, w_up, w_down), small)
    full = full.reshape(shards, 12 * rows, WIDTH)
    full_query, full_key, full_value, full_out = (
        full[:, i * rows : (i + 1) * rows].reshape(model_width, WIDTH) for i in range(4)
    )
    full_up = jnp.concatenate(
        [full[:, i * rows : (i + 1) * rows].reshape(model_width, WIDTH) for i in range(4, 8)], axis=1
    )
    full_down = full[:, 8 * rows :].reshape(shards * 4 * rows, WIDTH)
    smalls = smalls.reshape(shards, 8, 128)
    bias_up = smalls[:, 0, : b_up.shape[0]].reshape(-1)
    bias_down, gain_one, shift_one, gain_two, shift_two = (
        smalls[:, i, :rows].reshape(-1) for i in range(1, 6)
    )
    hidden_in = inputs.reshape(row_count, model_width).astype(jnp.float32)
    normed_one, normal_one, scale_one = layer_norm(hidden_in, gain_one, shift_one)
    normed_attn = normed_one.astype(jnp.bfloat16)
    queries = jnp.dot(normed_attn, full_query, preferred_element_type=jnp.float32)
    keys_raw = jnp.dot(normed_attn, full_key, preferred_element_type=jnp.float32)
    values = jnp.dot(normed_attn, full_value, preferred_element_type=jnp.float32).astype(
        jnp.bfloat16
    )
    query_feat, query_pull = jax.vjp(feature, queries)
    key_feat, key_pull = jax.vjp(feature, keys_raw)
    head_shape = (sequences, length, HEADS, HEAD_DIM)
    query_heads = query_feat.astype(jnp.bfloat16).reshape(head_shape)
    key_heads = key_feat.astype(jnp.bfloat16).reshape(head_shape)
    value_heads = values.reshape(head_shape)
    context, totals = lax.map(attend_forward, (query_heads, key_heads, value_heads, segment_ids))
    context_low = context.reshape(row_count, model_width).astype(jnp.bfloat16)
    after_attn = hidden_in + jnp.dot(context_low, full_out, preferred_element_type=jnp.float32)
    normed_two, normal_two, scale_two = layer_norm(after_attn, gain_two, shift_two)
    normed_ffn = normed_two.astype(jnp.bfloat16)
    pre_act = jnp.dot(normed_ffn, full_up, preferred_element_type=jnp.float32) + bias_up
    activated, gelu_pull = jax.vjp(jax.nn.gelu, pre_act)
    hidden = activated.astype(jnp.bfloat16)
    result = (
        after_attn + jnp.dot(hidden, full_down, preferred_element_type=jnp.float32) + bias_down
    )
    output = result.astype(jnp.bfloat16).reshape(inputs.shape)
    upstream = cotangent.reshape(row_count, model_width)
    upstream_f = upstream.astype(jnp.float32)
    grad_down = jnp.einsum("tf,td->fd", hidden, upstream, preferred_element_type=jnp.float32)
    grad_bias_down = jnp.sum(upstream_f, axis=0)
    grad_hidden = jnp.einsum("td,fd->tf", upstream, full_down, preferred_element_type=jnp.float32)
    grad_pre = gelu_pull(grad_hidden)[0].astype(jnp.bfloat16)
    grad_bias_up = jnp.sum(grad_pre.astype(jnp.float32), axis=0)
    grad_up = jnp.einsum("td,tf->df", normed_ffn, grad_pre, preferred_element_type=jnp.float32)
    grad_normed_two = jnp.einsum("tf,df->td", grad_pre, full_up, preferred_element_type=jnp.float32)
    grad_part, grad_gain_two, grad_shift_two = norm_back(
        grad_normed_two, normal_two, scale_two, gain_two
    )
    grad_after = upstream_f + grad_part
    grad_attn_out = grad_after.astype(jnp.bfloat16)
    grad_out = jnp.einsum(
        "td,te->de", context_low, grad_attn_out, preferred_element_type=jnp.float32
    )
    grad_context = jnp.einsum(
        "te,de->td", grad_attn_out, full_out, preferred_element_type=jnp.float32
    ).astype(jnp.bfloat16)
    grad_context = grad_context.astype(jnp.float32).reshape(head_shape)
    grad_totals = -jnp.sum(grad_context * context, axis=-1) / totals
    grad_mixed = (grad_context / totals[..., None]).astype(jnp.bfloat16)
    grad_qfeat, grad_kfeat, grad_vals = lax.map(
        attend_backward, (query_heads, key_heads, value_heads, segment_ids, grad_mixed, grad_totals)
    )
    grad_queries = query_pull(grad_qfeat.reshape(row_count, model_width))[0].astype(jnp.bfloat16)
    grad_keys = key_pull(grad_kfeat.reshape(row_count, model_width))[0].astype(jnp.bfloat16)
    grad_values = grad_vals.reshape(row_count, model_width).astype(jnp.bfloat16)
    grad_query_w = jnp.einsum(
        "td,te->de", normed_attn, grad_queries, preferred_element_type=jnp.float32
    )
    grad_key_w = jnp.einsum("td,te->de", normed_attn, grad_keys, preferred_element_type=jnp.float32)
    grad_value_w = jnp.einsum(
        "td,te->de", normed_attn, grad_values, preferred_element_type=jnp.float32
    )
    grad_normed_one = jnp.einsum(
        "te,de->td", grad_queries, full_query, preferred_element_type=jnp.float32
    )
    grad_normed_one = grad_normed_one + jnp.einsum(
        "te,de->td", grad_keys, full_key, preferred_element_type=jnp.float32
    )
    grad_normed_one = grad_normed_one + jnp.einsum(
        "te,de->td", grad_values, full_value, preferred_element_type=jnp.float32
    )
    grad_first, grad_gain_one, grad_shift_one = norm_back(
        grad_normed_one, normal_one, scale_one, gain_one
    )
    grad_inputs = (grad_after + grad_first).reshape(inputs.shape)

    def blocks(grad):
        return grad.astype(jnp.bfloat16).reshape(shards, -1, WIDTH)

    packed = jnp.concatenate(
        [blocks(g) for g in (grad_query_w, grad_key_w, grad_value_w, grad_out)]
        + [blocks(grad_up[:, i * WIDTH : (i + 1) * WIDTH]) for i in range(4)]
        + [blocks(grad_down)],
        axis=1,
    ).reshape(A, B, 2, 12 * rows, WIDTH)
    tiny = jnp.concatenate(
        [
            grad_bias_up.reshape(4, WIDTH),
            jnp.stack(
                [grad_bias_down, grad_gain_one, grad_shift_one, grad_gain_two, grad_shift_two]
            ),
            jnp.zeros((7, WIDTH), jnp.float32),
        ],
        axis=0,
    )
    owned, total = reduce_all(reps, shards, packed, tiny)
    here = lax.axis_index("shard")
    owned_up = jnp.concatenate(
        [owned[i * rows : (i + 1) * rows] for i in range(4, 8)], axis=1
    )
    n_up = b_up.shape[0]
    owned_bup = lax.dynamic_slice(total[:4].reshape(-1), (here * n_up,), (n_up,))
    vecs = [lax.dynamic_slice(total[4 + i], (here * rows,), (rows,)) for i in range(5)]
    return (
        output,
        grad_inputs,
        owned[:rows],
        owned[rows : 2 * rows],
        owned[2 * rows : 3 * rows],
        owned[3 * rows : 4 * rows],
        owned_up,
        owned[8 * rows :],
        owned_bup,
        *vecs,
    )


def solution(mesh):
    reps, shards = mesh.shape["rep"], mesh.shape["shard"]
    placed = (
        P(("rep", "shard"), None, None),
        P(("rep", "shard"), None),
        P("shard", None),
        P("shard", None),
        P("shard", None),
        P("shard", None),
        P("shard", None),
        P("shard", None),
        P("shard"),
        P("shard"),
        P("shard"),
        P("shard"),
        P("shard"),
        P("shard"),
        P(("rep", "shard"), None, None),
    )
    return jax.shard_map(
        functools.partial(on_device, reps, shards),
        mesh=mesh,
        in_specs=placed,
        out_specs=(
            P(("rep", "shard"), None, None),
            P(("rep", "shard"), None, None),
            P("shard", None),
            P("shard", None),
            P("shard", None),
            P("shard", None),
            P("shard", None),
            P("shard", None),
            P("shard"),
            P("shard"),
            P("shard"),
            P("shard"),
            P("shard"),
            P("shard"),
        ),
        check_vma=False,
    )
```

```python
import functools
import types

import jax
import jax.numpy as jnp
from jax import lax
from jax.experimental import pallas as pl
from jax.experimental.pallas import tpu as pltpu
from jax.sharding import PartitionSpec as P

WIDTH = 512
CHUNK = 256
HEAD_DIM = 64
GROUP = 256
PER_GROUP = GROUP // HEAD_DIM
GROUPS = WIDTH // GROUP

epsilon = 1e-05
MESH = pl.DeviceIdType.MESH
F32 = jnp.float32
BF16 = jnp.bfloat16


class Place:
    def __init__(self, reps, shards):
        self.reps, self.shards = reps, shards
        self.A = 4
        self.B = shards // 8
        self.r = lax.axis_index("rep")
        s = lax.axis_index("shard")
        self.s = s
        self.c = lax.rem(s, 2)
        self.b = lax.rem(s // 2, self.B)
        self.a = s // (2 * self.B)
        self.h = lax.rem(self.r, 2)

    def at(self, a=None, b=None, c=None, r=None):
        a = self.a if a is None else a
        b = self.b if b is None else b
        c = self.c if c is None else c
        r = self.r if r is None else r
        return (r, (a * self.B + b) * 2 + c)

    def next_a(self, j):
        return lax.rem(self.a + j, self.A)

    def next_b(self, j):
        return lax.rem(self.b + j, self.B)

    def sibling(self):
        return self.at(c=1 - self.c)

    def twin(self, bit=1):
        return self.at(r=self.r + bit - 2 * bit * lax.rem(self.r // bit, 2))

    def bits(self):
        bit, out = 2, []
        while bit < self.reps:
            out.append(bit)
            bit *= 2
        return out

    def partners(self):
        out = [self.sibling(), self.twin()]
        out += [self.at(a=self.next_a(j)) for j in range(1, self.A)]
        out += [self.at(b=self.next_b(j)) for j in range(1, self.B)]
        return out + [self.twin(bit) for bit in self.bits()]


def greet(partners):
    barrier = pltpu.get_barrier_semaphore()
    for device in partners:
        pl.semaphore_signal(barrier, inc=1, device_id=device, device_id_type=MESH)
    pl.semaphore_wait(barrier, len(partners))


def remote(src, dst, send, recv, device):
    return pltpu.make_async_remote_copy(
        src_ref=src, dst_ref=dst, send_sem=send, recv_sem=recv, device_id=device, device_id_type=MESH
    )


def both(one, two):
    if one is None:
        return two
    return one if two is None else jnp.logical_and(one, two)


class Sends:
    def __init__(self):
        self.made = []

    @staticmethod
    def act(copy, do):
        cond, make = copy()
        if cond is None:
            do(make())
        else:
            pl.when(cond)(lambda: do(make()))

    def go(self, copy):
        self.act(copy, lambda made: made.start())
        self.made.append(copy)

    def arrived(self, copy):
        self.act(copy, lambda made: made.wait_recv())

    def finish(self):
        for copy in self.made:
            self.act(copy, lambda made: made.wait_send())
        self.made = []


class Gather:
    def __init__(self, place, full, lo, rows, send, recv, sends):
        self.p, self.full, self.lo, self.rows = place, full, lo, rows
        self.send, self.recv, self.sends = send, recv, sends

    def whole(self, a, b, c):
        return self.full.at[a, b, c, pl.ds(self.lo, self.rows)]

    def half(self, a, b, c, h):
        size = self.rows // 2
        return self.full.at[a, b, c, pl.ds(pl.multiple_of(self.lo + h * size, 16), size)]

    def line(self, k, way):
        p = self.p
        if k == 0:
            return None, p.a
        return ((p.a - k >= 0), p.a - k) if way > 0 else ((p.a + k < p.A), p.a + k)

    def cross(self, j, way):
        p = self.p
        if j == 0:
            return None, p.b
        return ((p.b - j >= 0), p.b - j) if way > 0 else ((p.b + j < p.B), p.b + j)

    def copy(self, ref, a, b, c, kind, half_id, device):
        return remote(ref, ref, self.send.at[a, b, kind], self.recv.at[a, b, c, half_id], device)

    def to_a(self, k, way, step):
        p = self.p

        def copy():
            cond, a = self.line(k, way)
            cond = both(cond, (p.a < p.A - 1) if step > 0 else (p.a > 0))
            ref = self.whole(a, p.b, p.c)
            return cond, lambda: self.copy(
                ref, a, p.b, p.c, 1 if step > 0 else 0, 0, p.at(a=p.a + step)
            )

        self.sends.go(copy)

    def to_b(self, k, way, j, across, step):
        p = self.p

        def copy():
            cond, a = self.line(k, way)
            more, b = self.cross(j, across)
            cond = both(both(cond, more), (p.b < p.B - 1) if step > 0 else (p.b > 0))
            ref = self.half(a, b, p.c, p.h)
            return cond, lambda: self.copy(
                ref, a, b, p.c, 3 if step > 0 else 2, 0, p.at(b=p.b + step)
            )

        self.sends.go(copy)

    def column(self, k, way):
        p = self.p
        for step in (1, -1):
            if k == 0 or step == way:
                self.to_a(k, way, step)
        for step in (1, -1):
            self.to_b(k, way, 0, 0, step)

        def copy():
            cond, a = self.line(k, way)
            return cond, lambda: self.copy(
                self.whole(a, p.b, p.c), a, p.b, p.c, 5, 0, p.sibling()
            )

        self.sends.go(copy)

    def own(self):
        self.column(0, 1)

    def ways(self, k):
        return (1,) if k == 0 else (1, -1)

    def columns(self, k):
        p = self.p
        for way in self.ways(k):

            def copy():
                cond, a = self.line(k, way)
                return cond, lambda: self.copy(
                    self.whole(a, p.b, p.c), a, p.b, p.c, 0, 0, p.sibling()
                )

            self.sends.arrived(copy)
            self.column(k, way)

    def rows_b(self, k):
        p = self.p
        for way in self.ways(k):
            for j in range(1, p.B):
                for across in (1, -1):

                    def copy(kind, half_id, device, way=way, j=j, across=across):
                        cond, a = self.line(k, way)
                        more, b = self.cross(j, across)
                        ref = self.half(a, b, p.c, p.h)
                        return both(cond, more), lambda: self.copy(
                            ref, a, b, p.c, kind, half_id, device()
                        )

                    self.sends.arrived(functools.partial(copy, 0, 0, p.sibling))
                    if p.B > 2:
                        self.to_b(k, way, j, across, across)
                    self.sends.go(functools.partial(copy, 4, 1, p.twin))
                    self.sends.go(functools.partial(copy, 5, 0, p.sibling))

    def rows_twin(self, k):
        p = self.p
        for way in self.ways(k):
            for j in range(1, p.B):

                def copy(kind, way=way, j=j):
                    cond, a = self.line(k, way)
                    b = p.next_b(j)
                    ref = self.half(a, b, p.c, 1 - p.h)
                    return cond, lambda: self.copy(ref, a, b, p.c, kind, 1, p.sibling())

                self.sends.arrived(functools.partial(copy, 0))
                self.sends.go(functools.partial(copy, 6))

    def rest(self):
        p = self.p
        other = 1 - p.c
        for a in range(p.A):
            self.copy(self.whole(a, p.b, other), a, p.b, other, 0, 0, p.sibling()).wait_recv()
            for j in range(1, p.B):
                b = p.next_b(j)
                for i, h in enumerate((p.h, 1 - p.h)):
                    self.copy(self.half(a, b, other, h), a, b, other, 0, i, p.sibling()).wait_recv()


class SmallGather:
    def __init__(self, place, full, send, recv, sends):
        self.p, self.full, self.send, self.recv, self.sends = place, full, send, recv, sends

    def copy(self, ref, k, device):
        return remote(ref, ref, self.send.at[k], self.recv.at[k], device)

    def own(self):
        p = self.p
        for j in range(1, p.A):
            self.sends.go(
                lambda j=j: (
                    None,
                    lambda: self.copy(self.full.at[p.a, p.b, p.c], j, p.at(a=p.next_a(j))),
                )
            )

    def second(self):
        p = self.p
        for j in range(1, p.A):
            self.copy(self.full.at[p.next_a(p.A - j), p.b, p.c], j, p.sibling()).wait_recv()
        for j in range(1, p.B):
            self.sends.go(
                lambda j=j: (
                    None,
                    lambda: self.copy(self.full.at[:, p.b, p.c], p.A + j, p.at(b=p.next_b(j))),
                )
            )

    def third(self):
        p = self.p
        for j in range(1, p.B):
            self.copy(self.full.at[:, p.next_b(p.B - j), p.c], p.A + j, p.sibling()).wait_recv()
        self.sends.go(lambda: (None, lambda: self.copy(self.full.at[:, :, p.c], 0, p.sibling())))

    def last(self):
        p = self.p
        self.copy(self.full.at[:, :, 1 - p.c], 0, p.sibling()).wait_recv()


class Reduce:
    def __init__(self, place, part, bufs, lo, rows, at, lanes, send, recv, sends, pair_first=False):
        self.p, self.part, self.lo, self.rows, self.at, self.lanes = place, part, lo, rows, at, lanes
        self.core, self.line_b, self.pair, self.line_a, self.wide, self.done = bufs
        self.send, self.recv, self.sends = send, recv, sends
        self.pair_first = pair_first

    def win(self):
        return (pl.ds(self.lo, self.rows), pl.ds(self.at, self.lanes))

    def half(self, h):
        size = self.lanes // 2
        return (
            pl.ds(self.lo, self.rows),
            pl.ds(pl.multiple_of(self.at + h * size, 128), size),
        )

    def go(self, copy):
        self.sends.go(lambda: (None, lambda: self.copy(*copy())))

    def copy(self, src, dst, k, device):
        return remote(src, dst, self.send.at[k], self.recv.at[k], device)

    def arrived(self, ref, k):
        self.copy(ref, ref, k, self.p.sibling()).wait_recv()

    def order(self):
        return list(range(1, self.p.B)) + [0]

    def start(self):
        p = self.p
        for j in self.order():
            self.go(
                lambda j=j: (
                    self.part.at[(slice(None), p.next_b(j), 1 - p.c) + self.win()],
                    self.core.at[(slice(None), j) + self.win()],
                    j,
                    p.sibling(),
                )
            )

    def after_core(self):
        p = self.p
        for j in self.order():
            mine = (slice(None), p.next_b(j), p.c) + self.win()
            got = (slice(None), j) + self.win()
            self.arrived(self.core.at[got], j)
            self.part[mine] = self.part[mine] + self.core[got]
            if self.pair_first:
                self.to_pair(j)
            elif j > 0:
                self.to_b(j, self.win)

    def to_b(self, j, win):
        p = self.p
        self.go(
            lambda: (
                self.part.at[(slice(None), p.next_b(j), p.c) + win()],
                self.line_b.at[(j - 1, slice(None)) + win()],
                p.B + j,
                p.at(b=p.next_b(j)),
            )
        )

    def to_pair(self, j):
        p = self.p
        self.go(
            lambda: (
                self.part.at[(slice(None), p.next_b(j), p.c) + self.half(1 - p.h)],
                self.pair.at[(slice(None), j) + self.half(1 - p.h)],
                2 * p.B + j,
                p.twin(),
            )
        )

    def to_a(self):
        p = self.p
        for j in range(1, p.A):
            self.go(
                lambda j=j: (
                    self.part.at[(p.next_a(j), p.b, p.c) + self.half(p.h)],
                    self.line_a.at[(j - 1,) + self.half(p.h)],
                    3 * p.B + j,
                    p.at(a=p.next_a(j)),
                )
            )

    def add_b(self, win):
        p = self.p
        mine = (slice(None), p.b, p.c) + win
        total = self.part[mine].astype(F32)
        for j in range(1, p.B):
            got = (j - 1, slice(None)) + win
            self.arrived(self.line_b.at[got], p.B + j)
            total = total + self.line_b[got].astype(F32)
        self.part[mine] = total.astype(BF16)

    def add_pair(self, j):
        p = self.p
        got = (slice(None), j) + self.half(p.h)
        mine = (slice(None), p.next_b(j), p.c) + self.half(p.h)
        self.arrived(self.pair.at[got], 2 * p.B + j)
        self.part[mine] = self.part[mine] + self.pair[got]

    def second(self):
        p = self.p
        if self.pair_first:
            for j in self.order():
                self.add_pair(j)
                if j > 0:
                    self.to_b(j, lambda: self.half(p.h))
        else:
            self.add_b(self.win())
            self.to_pair(0)

    def third(self):
        p = self.p
        if self.pair_first:
            self.add_b(self.half(p.h))
        else:
            self.add_pair(0)
        self.to_a()

    def after_a(self):
        p, base = self.p, 3 * self.p.B
        mine = self.half(p.h)
        total = self.part[(p.a, p.b, p.c) + mine].astype(F32)
        for j in range(1, p.A):
            got = (j - 1,) + mine
            self.arrived(self.line_a.at[got], base + j)
            total = total + self.line_a[got].astype(F32)
        for i, bit in enumerate(p.bits()):
            k = base + p.A + 1 + i
            self.wide[(2 * i,) + mine] = total.astype(BF16)

            def copy(i=i, k=k, bit=bit):
                here = self.half(p.h)
                return (
                    self.wide.at[(2 * i,) + here],
                    self.wide.at[(2 * i + 1,) + here],
                    k,
                    p.twin(bit),
                )

            self.go(copy)
            self.arrived(self.wide.at[(2 * i + 1,) + mine], k)
            total = self.wide[(2 * i,) + mine].astype(F32)
            total = total + self.wide[(2 * i + 1,) + mine].astype(F32)
        self.done[mine] = total.astype(BF16)
        self.go(
            lambda: (
                self.done.at[self.half(p.h)],
                self.done.at[self.half(p.h)],
                base + p.A,
                p.twin(),
            )
        )

    def finish(self):
        p = self.p
        self.arrived(self.done.at[self.half(1 - p.h)], 3 * p.B + p.A)

    def steps(self):
        return [self.start, self.after_core, self.second, self.third, self.after_a, self.finish]

    @staticmethod
    def n_sems(reps, shards):
        return 3 * (shards // 8) + 4 + 1 + max(reps.bit_length() - 2, 0)


class SmallReduce:
    def __init__(self, place, slots, send, recv, sends):
        self.p, self.slots, self.send, self.recv, self.sends = place, slots, send, recv, sends
        self.now, self.free, self.k = 0, 1, 0

    def copy(self, src, dst, k, device):
        return remote(self.slots.at[src], self.slots.at[dst], self.send.at[k], self.recv.at[k], device)

    def exchange(self, devices):
        self.fresh = []
        for device in devices:
            src, dst, k = self.now, self.free, self.k
            self.fresh.append((dst, k))
            self.sends.go(
                lambda src=src, dst=dst, k=k, device=device: (
                    None,
                    lambda: self.copy(src, dst, k, device()),
                )
            )
            self.free, self.k = self.free + 1, self.k + 1

    def add(self):
        total = self.slots[self.now]
        for slot, k in self.fresh:
            self.copy(slot, slot, k, self.p.sibling()).wait_recv()
            total = total + self.slots[slot]
        self.slots[self.free] = total
        self.now, self.free = self.free, self.free + 1

    def steps(self):
        p = self.p
        stages = [
            [p.sibling],
            [lambda j=j: p.at(b=p.next_b(j)) for j in range(1, p.B)],
            [p.twin],
            [lambda j=j: p.at(a=p.next_a(j)) for j in range(1, p.A)],
        ] + [[functools.partial(p.twin, bit)] for bit in p.bits()]
        out = [lambda: self.exchange(stages[0])]
        for stage in stages[1:]:
            out.append(lambda stage=stage: (self.add(), self.exchange(stage)))
        out.append(self.add)
        return out

    @staticmethod
    def counts(reps, shards):
        wide = max(reps.bit_length() - 2, 0)
        copies = 1 + (shards // 8 - 1) + 1 + 3 + wide
        return copies, 1 + copies + 4 + wide


def dot(lhs, rhs):
    return lax.dot_general(lhs, rhs, (((1,), (0,)), ((), ())), preferred_element_type=F32)


def dot_nt(lhs, rhs):
    return lax.dot_general(lhs, rhs, (((1,), (1,)), ((), ())), preferred_element_type=F32)


def dot_tn(lhs, rhs):
    return lax.dot_general(lhs, rhs, (((0,), (0,)), ((), ())), preferred_element_type=F32)


def iota(shape, axis):
    return lax.broadcasted_iota(jnp.int32, shape, axis)


def mean_last(value):
    return jnp.sum(value, axis=-1, keepdims=True) * (1.0 / value.shape[-1])


def column_sum(value):
    return jnp.sum(value, axis=0, keepdims=True)


def twice(value):
    return jnp.concatenate([value, value], axis=1)


def feature(value):
    return jnp.where(value > 0, value + 1.0, jnp.exp(jnp.minimum(value, 0.0)))


def layer_kernel(reps, shards, length, n):
    p = Place(reps, shards)
    A, B = p.A, p.B
    rows_w = n.w_query.shape[0]
    R = rows_w
    chunks = length // CHUNK
    full, part, smalls, slots, vecs = n.full, n.part, n.smalls, n.slots, n.vecs

    mine = full.at[p.a, p.b, p.c]
    pieces = [
        (ref, mine.at[pl.ds(i * R, R)])
        for i, ref in enumerate((n.w_query, n.w_key, n.w_value, n.w_out))
    ]
    pieces += [
        (n.w_up.at[:, pl.ds(i * WIDTH, WIDTH)], mine.at[pl.ds((4 + i) * R, R)]) for i in range(4)
    ]
    pieces += [(n.w_down, mine.at[pl.ds(8 * R, 4 * R)])]
    local = [
        pltpu.make_async_copy(src, dst, n.sem_local.at[i]) for i, (src, dst) in enumerate(pieces)
    ]
    for copy in local:
        copy.start()
    smalls[p.a, p.b, p.c] = n.small[...]
    greet(p.partners())
    for copy in local:
        copy.wait()

    sends = Sends()
    tiny = SmallGather(p, smalls, n.send0, n.recv0, sends)
    first = Gather(p, full, 0, 4 * R, n.send1.at[0], n.recv1.at[0], sends)
    later = Gather(p, full, 4 * R, 8 * R, n.send1.at[1], n.recv1.at[1], sends)
    bufs = (n.core, n.line_b, n.pair, n.line_a, n.wide, n.done)

    def job(i, lo, rows, at, lanes, pair_first=False):
        return Reduce(
            p, part, bufs, lo, rows, at, lanes, n.send2.at[i], n.recv2.at[i], sends, pair_first
        )

    jobs = [
        job(0, 4 * R, 2 * R, 0, WIDTH),
        job(1, 6 * R, 2 * R, 0, WIDTH),
        job(2, 8 * R, 4 * R, 0, WIDTH, True),
        job(3, 3 * R, R, 0, WIDTH),
        job(4, 0, 3 * R, 0, GROUP),
        job(5, 0, 3 * R, GROUP, GROUP),
    ]
    J = [j.steps() for j in jobs]
    small_sum = SmallReduce(p, slots, n.send3, n.recv3, sends)
    T = small_sum.steps()

    def rows_of(t):
        return pl.ds(pl.multiple_of(t * CHUNK, CHUNK), CHUNK)

    def per_chunk(events, body, down=False):
        def step(i, carry):
            body(chunks - 1 - i if down else i)
            for at, calls in enumerate(events):
                if calls:

                    @pl.when(i == at)
                    def _():
                        for call in calls:
                            call()

            return carry

        lax.fori_loop(0, chunks, step, 0)

    tiny.own()
    first.own()

    seg_row = n.segment_ids[...].astype(F32)
    seg_rows = n.seg_rows
    seg_rows[0:8, :] = jnp.full((8, 128), -1.0, F32)
    seg_rows[pl.ds(8, length), :] = jnp.broadcast_to(seg_row, (128, length)).T
    seg_rows[pl.ds(8 + length, 8), :] = jnp.full((8, 128), -2.0, F32)
    heads, mask, mask_t = n.heads, n.mask, n.mask_t
    for i in range(PER_GROUP):
        heads[i] = jnp.where(iota((CHUNK, GROUP), 1) // HEAD_DIM == i, 1.0, 0.0).astype(BF16)
    same_head = (iota((GROUP, GROUP), 0) // HEAD_DIM) == (iota((GROUP, GROUP), 1) // HEAD_DIM)
    n.ones[...] = jnp.where(same_head, 1.0, 0.0).astype(BF16)
    later_row = iota((CHUNK, CHUNK), 0) >= iota((CHUNK, CHUNK), 1)
    later_col = iota((CHUNK, CHUNK), 0) <= iota((CHUNK, CHUNK), 1)
    for t in range(chunks):
        same = twice(seg_rows[pl.ds(8 + t * CHUNK, CHUNK), :]) == seg_row[
            :, t * CHUNK : (t + 1) * CHUNK
        ]
        mask[t] = jnp.where(same & later_row, 1.0, 0.0).astype(BF16)
        mask_t[t] = jnp.where(same & later_col, 1.0, 0.0).astype(BF16)

    def seg_chunk(t):
        return seg_rows[pl.ds(pl.multiple_of(8 + t * CHUNK, 8), CHUNK), :]

    def seg_at(t, row):
        return seg_rows[pl.ds(8 + t * CHUNK + row, 1), :]

    def flags(one, two):
        return twice(jnp.where(one == two, 1.0, 0.0))

    first.columns(1)
    tiny.second()
    first.rows_b(0)

    def norm_one(t):
        at = rows_of(t)
        h = n.inputs[at].astype(F32)
        centre = h - mean_last(h)
        scale = lax.rsqrt(mean_last(centre * centre) + epsilon)
        n.normal_one[at] = centre * scale
        n.scale_one[at] = jnp.broadcast_to(scale, (CHUNK, 128))

    per_chunk([], norm_one)
    first.columns(2)
    first.rows_b(1)
    first.rows_twin(0)
    tiny.third()
    first.columns(3)
    first.rows_b(2)
    first.rows_twin(1)
    later.own()
    first.rows_b(3)
    first.rows_twin(2)
    tiny.last()

    blocks = smalls[...].reshape(shards * 8, 128).astype(BF16)
    lane = iota((128, WIDTH), 1)
    row = iota((128, WIDTH), 0)
    block = iota((shards, 8, WIDTH), 0)
    at_lane = iota((shards, 8, WIDTH), 2)
    spread = jnp.where(lane % R == row, 1.0, 0.0).astype(BF16)
    laid = dot(blocks, spread).reshape(shards, 8, WIDTH)
    vecs[0:8] = jnp.sum(jnp.where(at_lane // R == block, laid, 0.0), axis=0)
    spread = jnp.where(lane % (4 * R) == row, 1.0, 0.0).astype(BF16)
    laid = dot(blocks, spread).reshape(shards, 8, WIDTH)
    for i in range(4):
        picked = jnp.where((at_lane + i * WIDTH) // (4 * R) == block, laid, 0.0)
        vecs[8 + i : 9 + i] = jnp.sum(picked, axis=0)[0:1]
    b_down, gain_one, shift_one, gain_two, shift_two = (vecs[i : i + 1] for i in range(1, 6))

    first.rows_twin(3)
    first.rest()

    def weight(i):
        return full[:, :, :, i * R : (i + 1) * R, :].reshape(WIDTH, WIDTH)

    def weight_down(i):
        return full[i, :, :, 8 * R : 12 * R, :].reshape(WIDTH, WIDTH)

    lanes = [slice(g * GROUP, (g + 1) * GROUP) for g in range(GROUPS)]
    state, state_now, keys_now = n.state, n.state_now, n.keys_now
    state_now[...] = jnp.zeros(state_now.shape, F32)
    keys_now[...] = jnp.zeros(keys_now.shape, F32)
    slots[0] = jnp.zeros(slots.shape[1:], F32)

    def forward(t):
        at = rows_of(t)
        normed = (n.normal_one[at] * gain_one + shift_one).astype(BF16)
        n.normed_attn[at] = normed
        n.query[at] = feature(dot(normed, weight(0))).astype(BF16)
        n.key[at] = feature(dot(normed, weight(1))).astype(BF16)
        n.value[at] = dot(normed, weight(2)).astype(BF16)
        seg = seg_chunk(t)
        before = flags(seg, seg_at(t, -1))
        ending = flags(seg, seg_at(t, CHUNK - 1)).astype(BF16)
        carry = flags(seg_at(t, CHUNK - 1), seg_at(t, -1))
        before_low = before.astype(BF16)
        for g in range(GROUPS):
            q, k, v = (ref[at, lanes[g]] for ref in (n.query, n.key, n.value))
            old = state_now[g].astype(BF16)
            state[g, t] = old
            mixed = dot(q * before_low, old)
            for i in range(PER_GROUP):
                scores = dot_nt(q * heads[i], k).astype(BF16) * mask[t]
                mixed = mixed + dot(scores, v * heads[i])
            sums = dot(mask[t], k) + before * keys_now[g, 0:1]
            n.key_sums[at, lanes[g]] = sums
            totals = dot((q.astype(F32) * sums).astype(BF16), n.ones[...])
            inverse = 1.0 / totals
            n.inverse[at, lanes[g]] = inverse
            n.context[at, lanes[g]] = (mixed * inverse).astype(BF16)
            ended = k * ending
            state_now[g] = state_now[g] * carry + dot_tn(ended, v) * n.ones[...].astype(F32)
            keys_now[g, 0:1] = keys_now[g, 0:1] * carry + column_sum(ended.astype(F32))
        after = n.inputs[at].astype(F32) + dot(n.context[at], weight(3))
        centre = after - mean_last(after)
        scale = lax.rsqrt(mean_last(centre * centre) + epsilon)
        normal = centre * scale
        n.normal_two[at] = normal
        n.scale_two[at] = jnp.broadcast_to(scale, (CHUNK, 128))
        n.normed_ffn[at] = (normal * gain_two + shift_two).astype(BF16)
        n.result[at] = after + b_down

    per_chunk(
        [
            [lambda: later.columns(1), lambda: later.rows_b(0)],
            [lambda: later.columns(2), lambda: later.rows_b(1), lambda: later.rows_twin(0)],
            [lambda: later.columns(3), lambda: later.rows_b(2), lambda: later.rows_twin(1)],
            [lambda: later.rows_b(3), lambda: later.rows_twin(2)],
        ],
        forward,
    )
    later.rows_twin(3)
    later.rest()

    c0 = 0.7978845608028654
    c1 = c0 * 0.044715
    n.grad_normed[...] = jnp.zeros(n.grad_normed.shape, F32)

    def ffn(i, events):
        bias = vecs[8 + i : 9 + i]

        def body(t):
            at = rows_of(t)
            pre = dot(n.normed_ffn[at], weight(4 + i)) + bias
            square = pre * pre
            half = 0.5 + 0.5 * jnp.tanh(pre * (c0 + c1 * square))
            hidden = pre * half
            slope = half + (2.0 * hidden) * (1.0 - half) * (c0 + (3.0 * c1) * square)
            low = hidden.astype(BF16)
            n.hidden[at] = low
            n.result[at] = n.result[at] + dot(low, weight_down(i))
            grad = (dot_nt(n.cotangent[at], weight_down(i)) * slope).astype(BF16)
            n.grad_pre[at] = grad
            slots[0, i : i + 1] += column_sum(grad.astype(F32))
            n.grad_normed[at] = n.grad_normed[at] + dot_nt(grad, weight(4 + i))

        per_chunk(events, body)
        for m in range(2):
            cut = slice(m * 256, (m + 1) * 256)
            grad = dot_tn(n.hidden[:, cut], n.cotangent[...]).astype(BF16)
            part[i, m * B // 2 : (m + 1) * B // 2, :, 8 * R : 12 * R, :] = grad.reshape(
                B // 2, 2, 4 * R, WIDTH
            )
            grad = dot_tn(n.normed_ffn[:, cut], n.grad_pre[...]).astype(BF16)
            part[2 * m : 2 * m + 2, :, :, (4 + i) * R : (5 + i) * R, :] = grad.reshape(
                2, B, 2, R, WIDTH
            )

    ffn(0, [])
    ffn(1, [])
    J[0][0]()
    ffn(2, [[], [], [J[0][1]], []])
    ffn(3, [[], [], [J[0][2]], []])
    J[1][0]()
    J[2][0]()
    J[0][3]()

    def norm_two_back(t):
        at = rows_of(t)
        n.output[at] = n.result[at].astype(BF16)
        grad = n.grad_normed[at]
        normal = n.normal_two[at]
        up = n.cotangent[at].astype(F32)
        slots[0, 4:5] += column_sum(up)
        slots[0, 7:8] += column_sum(grad * normal)
        slots[0, 8:9] += column_sum(grad)
        e = grad * gain_two
        back = e - mean_last(e) - normal * mean_last(e * normal)
        after = up + n.scale_two[at][:, 0:1] * back
        n.grad_normed[at] = after
        low = after.astype(BF16)
        n.grad_attn[at] = low
        grad_context = dot_nt(low, weight(3)).astype(BF16).astype(F32)
        inverse = n.inverse[at]
        n.grad_mixed[at] = (grad_context * inverse).astype(BF16)
        turned = (grad_context * n.context[at].astype(F32)).astype(BF16)
        for g in range(GROUPS):
            n.grad_totals[at, lanes[g]] = -dot(turned[:, lanes[g]], n.ones[...]) * inverse[
                :, lanes[g]
            ]

    per_chunk([[], [J[1][1], J[2][1]], [], []], norm_two_back)
    for m in range(2):
        grad = dot_tn(n.context[:, m * 256 : (m + 1) * 256], n.grad_attn[...]).astype(BF16)
        part[2 * m : 2 * m + 2, :, :, 3 * R : 4 * R, :] = grad.reshape(2, B, 2, R, WIDTH)
    J[3][0]()
    J[0][4]()

    def backward(g):
        state_now[g] = jnp.zeros((GROUP, GROUP), F32)
        keys_now[g] = jnp.zeros((8, GROUP), F32)

        def body(t):
            at = rows_of(t)
            seg = seg_chunk(t)
            before = flags(seg, seg_at(t, -1)).astype(BF16)
            after = flags(seg, seg_at(t, CHUNK))
            opening = flags(seg, seg_at(t, 0)).astype(BF16)
            carry = flags(seg_at(t, 0), seg_at(t, CHUNK))
            q, k, v, gm = (
                ref[at, lanes[g]] for ref in (n.query, n.key, n.value, n.grad_mixed)
            )
            totals = n.grad_totals[at, lanes[g]]
            old = state_now[g].astype(BF16)
            weighted = totals * q.astype(F32)
            gq = dot_nt(gm * before, state[g, t]) + totals * n.key_sums[at, lanes[g]]
            gk = after * (dot_nt(v, old) + keys_now[g, 0:1]) + dot(mask_t[t], weighted.astype(BF16))
            gv = after * dot(k, old)
            for i in range(PER_GROUP):
                head = heads[i]
                gm_head = gm * head
                back = dot_nt(gm_head, v).astype(BF16) * mask[t]
                gq = gq + dot(back, k * head)
                back = dot_nt(v * head, gm).astype(BF16) * mask_t[t]
                gk = gk + dot(back, q * head)
                back = dot_nt(k * head, q).astype(BF16) * mask_t[t]
                gv = gv + dot(back, gm_head)
            n.grad_query[at, lanes[g]] = (gq * jnp.minimum(q.astype(F32), 1.0)).astype(BF16)
            n.grad_key[at, lanes[g]] = (gk * jnp.minimum(k.astype(F32), 1.0)).astype(BF16)
            n.grad_value[at, lanes[g]] = gv.astype(BF16)
            opened = q * opening
            state_now[g] = state_now[g] * carry + dot_tn(opened, gm) * n.ones[...].astype(F32)
            keys_now[g, 0:1] = keys_now[g, 0:1] * carry + column_sum(
                weighted * opening.astype(F32)
            )

        return body

    def weight_grads(g):
        for i, ref in enumerate((n.grad_query, n.grad_key, n.grad_value)):
            grad = dot_tn(n.normed_attn[...], ref[:, lanes[g]]).astype(BF16)
            part[:, :, :, i * R : (i + 1) * R, lanes[g]] = grad.reshape(A, B, 2, R, GROUP)

    per_chunk([[J[0][5], J[1][2], J[2][2]], [], [J[3][1]], []], backward(0), down=True)
    weight_grads(0)
    J[4][0]()
    J[1][3]()
    J[2][3]()
    per_chunk([[J[4][1], J[3][2]], [J[1][4]], [J[2][4], J[3][3]], [J[4][2]]], backward(1), down=True)
    weight_grads(1)
    J[5][0]()
    J[1][5]()
    J[3][4]()

    def norm_one_back(t):
        at = rows_of(t)
        grad = dot_nt(n.grad_query[at], weight(0))
        grad = grad + dot_nt(n.grad_key[at], weight(1))
        grad = grad + dot_nt(n.grad_value[at], weight(2))
        normal = n.normal_one[at]
        slots[0, 5:6] += column_sum(grad * normal)
        slots[0, 6:7] += column_sum(grad)
        e = grad * gain_one
        back = e - mean_last(e) - normal * mean_last(e * normal)
        n.grad_inputs[at] = n.grad_normed[at] + n.scale_one[at][:, 0:1] * back

    per_chunk([[J[2][5], J[4][3]], [J[5][1]], [J[3][5]], []], norm_one_back)
    T[0]()
    J[4][4]()
    T[1]()
    J[5][2]()
    T[2]()
    J[4][5]()
    J[5][3]()
    T[3]()
    J[5][4]()
    for step in T[4:]:
        step()

    total = slots[small_sum.now]
    high = total.astype(BF16)
    low = (total - high.astype(F32)).astype(BF16)
    row, lane = iota((WIDTH, 128), 0), iota((WIDTH, 128), 1)
    pick = jnp.where((row == lane + p.s * R) & (lane < R), 1.0, 0.0).astype(BF16)
    n.tiny_out[0:16] = dot(high, pick) + dot(low, pick)
    picked = jnp.zeros((16, 128), F32)
    for i in range(4):
        wanted = (row + i * WIDTH == lane + p.s * (4 * R)) & (lane < 4 * R)
        pick = jnp.where(wanted, 1.0, 0.0).astype(BF16)
        keep = iota((16, 128), 0) == i
        picked = picked + jnp.where(keep, dot(high, pick) + dot(low, pick), 0.0)
    n.tiny_out[16:17] = column_sum(picked)

    J[5][5]()
    done = n.done
    for i, ref in enumerate((n.out_query, n.out_key, n.out_value, n.out_out)):
        ref[...] = done[i * R : (i + 1) * R].astype(F32)
    for i in range(4):
        n.out_up[:, i * WIDTH : (i + 1) * WIDTH] = done[(4 + i) * R : (5 + i) * R].astype(F32)
    n.out_down[...] = done[8 * R : 12 * R].astype(F32)
    sends.finish()


def layer(reps, shards, inputs, segment_ids, weights, small, cotangent):
    length = inputs.shape[0]
    A, B = 4, shards // 8
    R = weights[0].shape[0]
    rows = 12 * R
    bits = max(reps.bit_length() - 2, 0)
    copies, n_slots = SmallReduce.counts(reps, shards)
    n_sems = Reduce.n_sems(reps, shards)
    w_query, w_key, w_value, w_out, w_up, w_down = weights
    ins = dict(
        inputs=inputs,
        segment_ids=segment_ids,
        w_query=w_query,
        w_key=w_key,
        w_value=w_value,
        w_out=w_out,
        w_up=w_up,
        w_down=w_down,
        small=small,
        cotangent=cotangent,
    )
    outs = dict(
        output=((length, WIDTH), BF16),
        grad_inputs=((length, WIDTH), F32),
        out_query=((R, WIDTH), F32),
        out_key=((R, WIDTH), F32),
        out_value=((R, WIDTH), F32),
        out_out=((R, WIDTH), F32),
        out_up=((R, 4 * WIDTH), F32),
        out_down=((4 * R, WIDTH), F32),
        tiny_out=((24, 128), F32),
    )
    tall = (length, WIDTH)
    buffers = dict(
        full=((A, B, 2, rows, WIDTH), BF16),
        part=((A, B, 2, rows, WIDTH), BF16),
        core=((A, B, rows, WIDTH), BF16),
        line_b=((B - 1, A, rows, WIDTH), BF16),
        pair=((A, B, rows, WIDTH), BF16),
        line_a=((A - 1, rows, WIDTH), BF16),
        wide=((max(2 * bits, 1), rows if bits else 16, WIDTH), BF16),
        done=((rows, WIDTH), BF16),
        smalls=((A, B, 2, 8, 128), F32),
        slots=((n_slots, 16, WIDTH), F32),
        vecs=((16, WIDTH), F32),
        seg_rows=((length + 16, 128), F32),
        heads=((PER_GROUP, CHUNK, GROUP), BF16),
        ones=((GROUP, GROUP), BF16),
        mask=((length // CHUNK, CHUNK, CHUNK), BF16),
        mask_t=((length // CHUNK, CHUNK, CHUNK), BF16),
        normal_one=(tall, F32),
        scale_one=((length, 128), F32),
        normed_attn=(tall, BF16),
        query=(tall, BF16),
        key=(tall, BF16),
        value=(tall, BF16),
        key_sums=(tall, F32),
        inverse=(tall, F32),
        context=(tall, BF16),
        state=((GROUPS, length // CHUNK, GROUP, GROUP), BF16),
        state_now=((GROUPS, GROUP, GROUP), F32),
        keys_now=((GROUPS, 8, GROUP), F32),
        normal_two=(tall, F32),
        scale_two=((length, 128), F32),
        normed_ffn=(tall, BF16),
        hidden=(tall, BF16),
        grad_pre=(tall, BF16),
        grad_normed=(tall, F32),
        grad_attn=(tall, BF16),
        grad_mixed=(tall, BF16),
        grad_totals=(tall, F32),
    )
    sems = dict(
        sem_local=(9,),
        send0=(A + B,),
        recv0=(A + B,),
        send1=(2, A, B, 7),
        recv1=(2, A, B, 2, 2),
        send2=(6, n_sems),
        recv2=(6, n_sems),
        send3=(copies,),
        recv3=(copies,),
    )
    names = list(ins) + list(outs) + list(buffers) + list(sems)

    def kernel(*refs):
        n = types.SimpleNamespace(**dict(zip(names, refs, strict=True)))
        n.result = n.grad_inputs
        n.grad_query, n.grad_key, n.grad_value = n.hidden, n.grad_pre, n.normed_ffn
        layer_kernel(reps, shards, length, n)

    vmem = pl.BlockSpec(memory_space=pltpu.VMEM)
    flops = 2 * 3 * length * WIDTH * WIDTH * 12 + 20 * length * length * WIDTH
    results = pl.pallas_call(
        kernel,
        out_shape=tuple(jax.ShapeDtypeStruct(*spec) for spec in outs.values()),
        in_specs=[vmem] * len(ins),
        out_specs=(vmem,) * len(outs),
        scratch_shapes=[pltpu.VMEM(*spec) for spec in buffers.values()]
        + [pltpu.SemaphoreType.DMA(shape) for shape in sems.values()],
        compiler_params=pltpu.CompilerParams(
            collective_id=1, has_side_effects=True, vmem_limit_bytes=63 << 20
        ),
        cost_estimate=pl.CostEstimate(flops=flops, bytes_accessed=8 << 20, transcendentals=0),
        name="layer",
    )(*ins.values())
    return dict(zip(outs, results, strict=True))


def on_device(
    reps,
    shards,
    inputs,
    segment_ids,
    w_query,
    w_key,
    w_value,
    w_out,
    w_up,
    w_down,
    b_up,
    b_down,
    gain_attn,
    shift_attn,
    gain_ffn,
    shift_ffn,
    cotangent,
):
    sequences, length, width = inputs.shape
    R = w_query.shape[0]

    def padded(vec):
        return jnp.pad(vec.astype(F32), (0, 128 - vec.shape[0]))[None]

    small = jnp.concatenate(
        [padded(v) for v in (b_up, b_down, gain_attn, shift_attn, gain_ffn, shift_ffn)]
        + [jnp.zeros((2, 128), F32)],
        axis=0,
    )
    got = layer(
        reps,
        shards,
        inputs.reshape(sequences * length, width),
        segment_ids,
        (w_query, w_key, w_value, w_out, w_up, w_down),
        small,
        cotangent.reshape(sequences * length, width),
    )
    tiny = got["tiny_out"]
    return (
        got["output"].reshape(inputs.shape),
        got["grad_inputs"].reshape(inputs.shape),
        got["out_query"],
        got["out_key"],
        got["out_value"],
        got["out_out"],
        got["out_up"],
        got["out_down"],
        tiny[16, : 4 * R],
        *(tiny[i, :R] for i in range(4, 9)),
    )


def solution(mesh):
    reps, shards = mesh.shape["rep"], mesh.shape["shard"]
    token = P(("rep", "shard"), None, None)
    matrix, vector = P("shard", None), P("shard")
    return jax.shard_map(
        functools.partial(on_device, reps, shards),
        mesh=mesh,
        in_specs=(token, P(("rep", "shard"), None)) + (matrix,) * 6 + (vector,) * 6 + (token,),
        out_specs=(token, token) + (matrix,) * 6 + (vector,) * 6,
        check_vma=False,
    )
```

```python
import functools
import types

import jax
import jax.numpy as jnp
from jax import lax
from jax.experimental import pallas as pl
from jax.experimental.pallas import tpu as pltpu
from jax.sharding import PartitionSpec as P

WIDTH = 512
CHUNK = 256
HEAD_DIM = 64
GROUP = 256
PER_GROUP = GROUP // HEAD_DIM
GROUPS = WIDTH // GROUP

epsilon = 1e-05
MESH = pl.DeviceIdType.MESH
F32 = jnp.float32
BF16 = jnp.bfloat16


class Place:
    def __init__(self, reps, shards):
        self.reps, self.shards = reps, shards
        self.A = 4
        self.B = shards // 8
        self.r = lax.axis_index("rep")
        s = lax.axis_index("shard")
        self.s = s
        self.c = lax.rem(s, 2)
        self.b = lax.rem(s // 2, self.B)
        self.a = s // (2 * self.B)
        self.h = lax.rem(self.r, 2)

    def at(self, a=None, b=None, c=None, r=None):
        a = self.a if a is None else a
        b = self.b if b is None else b
        c = self.c if c is None else c
        r = self.r if r is None else r
        return (r, (a * self.B + b) * 2 + c)

    def near(self, k):
        high = self.a // 2
        return (1 - self.a + 4 * high, 2 - high, 3 * (1 - high))[k]

    def next_a(self, j):
        return lax.rem(self.a + j, self.A)

    def next_b(self, j):
        return lax.rem(self.b + j, self.B)

    def sibling(self):
        return self.at(c=1 - self.c)

    def twin(self, bit=1):
        return self.at(r=self.r + bit - 2 * bit * lax.rem(self.r // bit, 2))

    def bits(self):
        bit, out = 2, []
        while bit < self.reps:
            out.append(bit)
            bit *= 2
        return out

    def partners(self):
        out = [self.sibling(), self.twin()]
        out += [self.at(a=self.next_a(j)) for j in range(1, self.A)]
        out += [self.at(b=self.next_b(j)) for j in range(1, self.B)]
        return out + [self.twin(bit) for bit in self.bits()]


def greet(partners):
    barrier = pltpu.get_barrier_semaphore()
    for device in partners:
        pl.semaphore_signal(barrier, inc=1, device_id=device, device_id_type=MESH)
    pl.semaphore_wait(barrier, len(partners))


def remote(src, dst, send, recv, device):
    return pltpu.make_async_remote_copy(
        src_ref=src, dst_ref=dst, send_sem=send, recv_sem=recv, device_id=device, device_id_type=MESH
    )


def both(one, two):
    if one is None:
        return two
    return one if two is None else jnp.logical_and(one, two)


class Sends:
    def __init__(self):
        self.made = []

    @staticmethod
    def act(copy, do):
        cond, make = copy()
        if cond is None:
            do(make())
        else:
            pl.when(cond)(lambda: do(make()))

    def go(self, copy):
        self.act(copy, lambda made: made.start())
        self.made.append(copy)

    def arrived(self, copy):
        self.act(copy, lambda made: made.wait_recv())

    def finish(self):
        for copy in self.made:
            self.act(copy, lambda made: made.wait_send())
        self.made = []


class Gather:
    def __init__(self, place, full, window, send, recv, base, sends):
        self.p, self.full = place, full
        self.lo, self.rows, self.left, self.lanes = window
        self.send, self.recv, self.base, self.sends = send, recv, base, sends

    def whole(self, a, b, c):
        return self.full.at[a, b, c, pl.ds(self.lo, self.rows), pl.ds(self.left, self.lanes)]

    def half(self, a, b, c, h):
        size = self.lanes // 2
        lanes = pl.ds(pl.multiple_of(self.left + h * size, 128), size)
        return self.full.at[a, b, c, pl.ds(self.lo, self.rows), lanes]

    def copy(self, ref, k, device, other=None):
        return remote(ref, ref, self.send.at[k], self.recv.at[k if other is None else other], device)

    def go(self, make):
        self.sends.go(lambda: (None, make))

    def slot(self, kind, k=0, j=0):
        more = self.p.B - 1
        j = max(j - 1, 0)
        base = (0, 4, 4 + more, 4 + 4 * more, 7 + 4 * more, 7 + 7 * more)
        base += (8 + 7 * more, 8 + 8 * more, 11 + 8 * more)
        return self.base + base[kind] + (k * more if kind in (2, 4) else k) + j

    def own(self):
        p = self.p
        for k in (2, 1, 0):
            self.go(
                lambda k=k: self.copy(
                    self.half(p.a, p.b, p.c, p.h) if k else self.whole(p.a, p.b, p.c),
                    self.slot(0, k),
                    p.at(a=p.near(k)),
                    self.slot(0, p.a),
                )
            )
        for j in range(1, p.B):
            self.go(
                lambda j=j: self.copy(
                    self.whole(p.a, p.b, p.c), self.slot(1, 0, j), p.at(b=p.next_b(j))
                )
            )
        self.go(lambda: self.copy(self.whole(p.a, p.b, p.c), self.slot(5), p.sibling()))

    def line_a(self, k):
        p = self.p
        place = (p.near(k), p.b, p.c)
        ref = self.half(*place, p.h) if k else self.whole(*place)
        self.copy(ref, self.slot(0, p.near(k)), p.sibling()).wait_recv()

        def mine():
            return self.half(p.near(k), p.b, p.c, p.h)

        for j in range(1, p.B):
            self.go(lambda j=j: self.copy(mine(), self.slot(2, k, j), p.at(b=p.next_b(j))))
        if k:
            self.go(lambda: self.copy(mine(), self.slot(3, k), p.twin()))

    def line_b_own(self):
        p = self.p
        for j in range(1, p.B):
            b = p.next_b(p.B - j)
            self.copy(self.whole(p.a, b, p.c), self.slot(1, 0, j), p.sibling()).wait_recv()
            self.go(
                lambda j=j: self.copy(
                    self.whole(p.a, p.next_b(p.B - j), p.c), self.slot(6, 0, j), p.sibling()
                )
            )

    def line_b(self, k):
        p = self.p
        for j in range(1, p.B):
            b = p.next_b(p.B - j)
            ref = self.half(p.near(k), b, p.c, p.h)
            self.copy(ref, self.slot(2, k, j), p.sibling()).wait_recv()
            self.go(
                lambda j=j: self.copy(
                    self.half(p.near(k), p.next_b(p.B - j), p.c, p.h), self.slot(4, k, j), p.twin()
                )
            )
        self.go(
            lambda: self.copy(
                self.half(p.near(k), slice(None), p.c, p.h), self.slot(7, k), p.sibling()
            )
        )

    def twin(self, k):
        p = self.p
        for j in range(0 if k else 1, p.B):
            ref = self.half(p.near(k), p.next_b(p.B - j), p.c, 1 - p.h)
            kind = 4 if j else 3
            self.copy(ref, self.slot(kind, k, j), p.sibling()).wait_recv()
        self.go(
            lambda: self.copy(
                self.half(p.near(k), slice(None), p.c, 1 - p.h), self.slot(8, k), p.sibling()
            )
        )

    def rest(self):
        p = self.p
        other = 1 - p.c
        self.copy(self.whole(p.a, p.b, other), self.slot(5), p.sibling()).wait_recv()
        for j in range(1, p.B):
            ref = self.whole(p.a, p.next_b(p.B - j), other)
            self.copy(ref, self.slot(6, 0, j), p.sibling()).wait_recv()
        for k in range(3):
            for kind, h in ((7, p.h), (8, 1 - p.h)):
                ref = self.half(p.near(k), slice(None), other, h)
                self.copy(ref, self.slot(kind, k), p.sibling()).wait_recv()

    @staticmethod
    def n_sems(shards):
        return 14 + 8 * (shards // 8 - 1)


class SmallGather:
    def __init__(self, place, full, send, recv, sends):
        self.p, self.full, self.send, self.recv, self.sends = place, full, send, recv, sends

    def copy(self, ref, k, device):
        return remote(ref, ref, self.send.at[k], self.recv.at[k], device)

    def own(self):
        p = self.p
        for j in range(1, p.A):
            self.sends.go(
                lambda j=j: (
                    None,
                    lambda: self.copy(self.full.at[p.a, p.b, p.c], j, p.at(a=p.next_a(j))),
                )
            )

    def second(self):
        p = self.p
        for j in range(1, p.A):
            self.copy(self.full.at[p.next_a(p.A - j), p.b, p.c], j, p.sibling()).wait_recv()
        for j in range(1, p.B):
            self.sends.go(
                lambda j=j: (
                    None,
                    lambda: self.copy(self.full.at[:, p.b, p.c], p.A + j, p.at(b=p.next_b(j))),
                )
            )

    def third(self):
        p = self.p
        for j in range(1, p.B):
            self.copy(self.full.at[:, p.next_b(p.B - j), p.c], p.A + j, p.sibling()).wait_recv()
        self.sends.go(lambda: (None, lambda: self.copy(self.full.at[:, :, p.c], 0, p.sibling())))

    def last(self):
        p = self.p
        self.copy(self.full.at[:, :, 1 - p.c], 0, p.sibling()).wait_recv()


class Reduce:
    def __init__(self, place, part, bufs, window, sems, base, sends, pair_first=False, span=None, end=None):
        self.p, self.part = place, part
        self.lo, self.rows, self.at, self.lanes = window
        self.core, self.line_b, self.pair, self.line_a, self.wide, self.done = bufs
        self.send, self.recv = sems
        self.sends = sends
        self.pair_first = pair_first
        self.first, self.last = span or (0, place.A)
        self.end = end or self
        self.base = base

    def slot(self, kind, j=0):
        B = self.p.B
        twins = B if self.pair_first else 1
        base = (0, B - 1, 2 * B - 1, 2 * B - 2 + twins, 2 * B + 2 + twins, 2 * B + 3 + twins)
        return self.base + base[kind] + j

    def n_sems(self):
        last = self.slot(3, 1) if self.end is not self else self.slot(5, len(self.p.bits()))
        return last - self.base

    def span(self):
        return slice(self.first, self.last)

    def win(self):
        return (pl.ds(self.lo, self.rows), pl.ds(self.at, self.lanes))

    def half(self, h):
        size = self.lanes // 2
        return (
            pl.ds(self.lo, self.rows),
            pl.ds(pl.multiple_of(self.at + h * size, 128), size),
        )

    def go(self, copy, when=lambda: None):
        self.sends.go(lambda: (when(), lambda: self.copy(*copy())))

    def copy(self, src, dst, k, device):
        return remote(src, dst, self.send.at[k], self.recv.at[k], device)

    def arrived(self, ref, k):
        self.copy(ref, ref, k, self.p.sibling()).wait_recv()

    def order(self):
        return list(range(1, self.p.B)) + [0]

    def start(self):
        p = self.p
        for j in self.order():
            self.go(
                lambda j=j: (
                    self.part.at[(self.span(), p.next_b(j), 1 - p.c) + self.win()],
                    self.core.at[(self.span(), j) + self.win()],
                    self.slot(0, j),
                    p.sibling(),
                )
            )

    def after_core(self):
        p = self.p
        for j in self.order():
            mine = (self.span(), p.next_b(j), p.c) + self.win()
            got = (self.span(), j) + self.win()
            self.arrived(self.core.at[got], self.slot(0, j))
            self.part[mine] = self.part[mine] + self.core[got]
            if self.pair_first:
                self.to_pair(j)
            elif j > 0:
                self.to_b(j, self.win)

    def to_b(self, j, win):
        p = self.p
        self.go(
            lambda: (
                self.part.at[(self.span(), p.next_b(j), p.c) + win()],
                self.line_b.at[(j - 1, self.span()) + win()],
                self.slot(1, j),
                p.at(b=p.next_b(j)),
            )
        )

    def to_pair(self, j):
        p = self.p
        self.go(
            lambda: (
                self.part.at[(self.span(), p.next_b(j), p.c) + self.half(1 - p.h)],
                self.pair.at[(self.span(), j) + self.half(1 - p.h)],
                self.slot(2, j),
                p.twin(),
            )
        )

    def to_a(self):
        p, end = self.p, self.end
        partial = self.last - self.first < p.A
        for j in range(1, p.A):

            def when(j=j):
                a = p.next_a(j)
                return both(a >= self.first, a < self.last) if partial else None

            end.go(
                lambda j=j: (
                    self.part.at[(p.next_a(j), p.b, p.c) + self.half(p.h)],
                    self.line_a.at[(j - 1,) + self.half(p.h)],
                    end.slot(3, j),
                    p.at(a=p.next_a(j)),
                ),
                when,
            )

    def add_b(self, win):
        p = self.p
        mine = (self.span(), p.b, p.c) + win
        total = self.part[mine].astype(F32)
        for j in range(1, p.B):
            got = (j - 1, self.span()) + win
            self.arrived(self.line_b.at[got], self.slot(1, j))
            total = total + self.line_b[got].astype(F32)
        self.part[mine] = total.astype(BF16)

    def add_pair(self, j):
        p = self.p
        got = (self.span(), j) + self.half(p.h)
        mine = (self.span(), p.next_b(j), p.c) + self.half(p.h)
        self.arrived(self.pair.at[got], self.slot(2, j))
        self.part[mine] = self.part[mine] + self.pair[got]

    def second(self):
        p = self.p
        if self.pair_first:
            for j in self.order():
                self.add_pair(j)
                if j > 0:
                    self.to_b(j, lambda: self.half(p.h))
        else:
            self.add_b(self.win())
            self.to_pair(0)

    def third(self):
        p = self.p
        if self.pair_first:
            self.add_b(self.half(p.h))
        else:
            self.add_pair(0)
        self.to_a()

    def after_a(self):
        p = self.p
        mine = self.half(p.h)
        total = self.part[(p.a, p.b, p.c) + mine].astype(F32)
        for j in range(1, p.A):
            got = (j - 1,) + mine
            self.arrived(self.line_a.at[got], self.slot(3, j))
            total = total + self.line_a[got].astype(F32)
        for i, bit in enumerate(p.bits()):
            k = self.slot(5, i)
            self.wide[(2 * i,) + mine] = total.astype(BF16)

            def copy(i=i, k=k, bit=bit):
                here = self.half(p.h)
                return (
                    self.wide.at[(2 * i,) + here],
                    self.wide.at[(2 * i + 1,) + here],
                    k,
                    p.twin(bit),
                )

            self.go(copy)
            self.arrived(self.wide.at[(2 * i + 1,) + mine], k)
            total = self.wide[(2 * i,) + mine].astype(F32)
            total = total + self.wide[(2 * i + 1,) + mine].astype(F32)
        self.done[mine] = total.astype(BF16)
        self.go(
            lambda: (
                self.done.at[self.half(p.h)],
                self.done.at[self.half(p.h)],
                self.slot(4),
                p.twin(),
            )
        )

    def finish(self):
        p = self.p
        self.arrived(self.done.at[self.half(1 - p.h)], self.slot(4))

    def steps(self):
        return [self.start, self.after_core, self.second, self.third, self.after_a, self.finish]


class SmallReduce:
    def __init__(self, place, slots, send, recv, sends):
        self.p, self.slots, self.send, self.recv, self.sends = place, slots, send, recv, sends
        self.now, self.free, self.k = 0, 1, 0

    def copy(self, src, dst, k, device):
        return remote(self.slots.at[src], self.slots.at[dst], self.send.at[k], self.recv.at[k], device)

    def exchange(self, devices):
        self.fresh = []
        for device in devices:
            src, dst, k = self.now, self.free, self.k
            self.fresh.append((dst, k))
            self.sends.go(
                lambda src=src, dst=dst, k=k, device=device: (
                    None,
                    lambda: self.copy(src, dst, k, device()),
                )
            )
            self.free, self.k = self.free + 1, self.k + 1

    def add(self):
        total = self.slots[self.now]
        for slot, k in self.fresh:
            self.copy(slot, slot, k, self.p.sibling()).wait_recv()
            total = total + self.slots[slot]
        self.slots[self.free] = total
        self.now, self.free = self.free, self.free + 1

    def steps(self):
        p = self.p
        stages = [
            [p.sibling],
            [lambda j=j: p.at(b=p.next_b(j)) for j in range(1, p.B)],
            [p.twin],
            [lambda j=j: p.at(a=p.next_a(j)) for j in range(1, p.A)],
        ] + [[functools.partial(p.twin, bit)] for bit in p.bits()]
        out = [lambda: self.exchange(stages[0])]
        for stage in stages[1:]:
            out.append(lambda stage=stage: (self.add(), self.exchange(stage)))
        out.append(self.add)
        return out

    @staticmethod
    def counts(reps, shards):
        wide = max(reps.bit_length() - 2, 0)
        copies = 1 + (shards // 8 - 1) + 1 + 3 + wide
        return copies, 1 + copies + 4 + wide


def dot(lhs, rhs):
    return lax.dot_general(lhs, rhs, (((1,), (0,)), ((), ())), preferred_element_type=F32)


def dot_nt(lhs, rhs):
    return lax.dot_general(lhs, rhs, (((1,), (1,)), ((), ())), preferred_element_type=F32)


def dot_tn(lhs, rhs):
    return lax.dot_general(lhs, rhs, (((0,), (0,)), ((), ())), preferred_element_type=F32)


def iota(shape, axis):
    return lax.broadcasted_iota(jnp.int32, shape, axis)


def mean_last(value):
    return jnp.sum(value, axis=-1, keepdims=True) * (1.0 / value.shape[-1])


def column_sum(value):
    return jnp.sum(value, axis=0, keepdims=True)


def twice(value):
    return jnp.concatenate([value, value], axis=1)


def feature(value):
    return jnp.where(value > 0, value + 1.0, jnp.exp(jnp.minimum(value, 0.0)))


def layer_kernel(reps, shards, length, n):
    p = Place(reps, shards)
    A, B = p.A, p.B
    rows_w = n.w_query.shape[0]
    R = rows_w
    chunks = length // CHUNK
    full, part, smalls, slots, vecs = n.full, n.part, n.smalls, n.slots, n.vecs

    mine = full.at[p.a, p.b, p.c]
    pieces = [
        (ref, mine.at[pl.ds(i * R, R)])
        for i, ref in enumerate((n.w_query, n.w_key, n.w_value, n.w_out))
    ]
    pieces += [
        (n.w_up.at[:, pl.ds(i * WIDTH, WIDTH)], mine.at[pl.ds((4 + i) * R, R)]) for i in range(4)
    ]
    pieces += [(n.w_down, mine.at[pl.ds(8 * R, 4 * R)])]
    pieces += [(n.inputs_far, n.inputs), (n.cotangent_far, n.cotangent)]
    local = [
        pltpu.make_async_copy(src, dst, n.sem_local.at[i]) for i, (src, dst) in enumerate(pieces)
    ]
    for copy in local:
        copy.start()
    smalls[p.a, p.b, p.c] = jnp.zeros((8, 128), F32)
    vectors = (n.b_up, n.b_down, n.gain_attn, n.shift_attn, n.gain_ffn, n.shift_ffn)
    for i, ref in enumerate(vectors):
        size = ref.shape[0]
        smalls[p.a, p.b, p.c, i : i + 1, 0:size] = ref[...].astype(F32).reshape(1, size)
    greet(p.partners())
    for copy in local[:9]:
        copy.wait()

    sends = Sends()
    tiny = SmallGather(p, smalls, n.send0, n.recv0, sends)
    windows = ((0 * R, 3 * R, 0, 512), (3 * R, 5 * R, 0, 512), (8 * R, 4 * R, 0, 512))
    gather_0, gather_1, gather_2 = (
        Gather(p, full, window, n.send1, n.recv1, i * Gather.n_sems(shards), sends)
        for i, window in enumerate(windows)
    )
    bufs = (n.core, n.line_b, n.pair, n.line_a, n.wide, n.done)

    made = []

    def job(lo, rows, at=0, lanes=WIDTH, **more):
        base = sum(one.n_sems() for one in made)
        window = (lo * R, rows * R, at, lanes)
        made.append(Reduce(p, part, bufs, window, (n.send1, n.recv2), base, sends, **more))
        return made[-1]

    up_one = job(4, 2)
    up_two = job(6, 2)
    down_one = job(8, 4, pair_first=True, span=(0, 2))
    down_two = job(8, 4, pair_first=True, span=(2, 4), end=down_one)
    out_all = job(3, 1)
    attn_one = job(0, 3, 0, 256)
    attn_two = job(0, 1, 256, 256)
    attn_three = job(1, 2, 256, 256, pair_first=True)
    assert sum(one.n_sems() for one in made) <= n.recv2.shape[0]
    small_sum = SmallReduce(p, slots, n.send3, n.recv3, sends)
    T = small_sum.steps()

    def rows_of(t):
        return pl.ds(pl.multiple_of(t * CHUNK, CHUNK), CHUNK)

    def per_chunk(events, body, down=False):
        def step(i, carry):
            body(chunks - 1 - i if down else i)
            for at, calls in enumerate(events):
                if calls:

                    @pl.when(i == at)
                    def _():
                        for call in calls:
                            call()

            return carry

        lax.fori_loop(0, chunks, step, 0)

    gather_0.own()
    gather_0.line_b_own()
    gather_1.own()
    gather_0.line_a(1)
    gather_0.line_a(2)
    gather_0.line_a(0)
    gather_0.line_b(0)
    gather_0.line_b(2)
    gather_1.line_b_own()
    gather_2.own()

    seg_row = n.segment_ids[...].astype(F32)
    seg_rows = n.seg_rows
    seg_rows[0:8, :] = jnp.full((8, 128), -1.0, F32)
    seg_rows[pl.ds(8, length), :] = jnp.broadcast_to(seg_row, (128, length)).T
    seg_rows[pl.ds(8 + length, 8), :] = jnp.full((8, 128), -2.0, F32)
    heads, mask, mask_t = n.heads, n.mask, n.mask_t
    for i in range(PER_GROUP):
        heads[i] = jnp.where(iota((CHUNK, GROUP), 1) // HEAD_DIM == i, 1.0, 0.0).astype(BF16)
    same_head = (iota((GROUP, GROUP), 0) // HEAD_DIM) == (iota((GROUP, GROUP), 1) // HEAD_DIM)
    n.ones[...] = jnp.where(same_head, 1.0, 0.0).astype(BF16)
    later_row = iota((CHUNK, CHUNK), 0) >= iota((CHUNK, CHUNK), 1)
    later_col = iota((CHUNK, CHUNK), 0) <= iota((CHUNK, CHUNK), 1)
    for t in range(chunks):
        same = twice(seg_rows[pl.ds(8 + t * CHUNK, CHUNK), :]) == seg_row[
            :, t * CHUNK : (t + 1) * CHUNK
        ]
        mask[t] = jnp.where(same & later_row, 1.0, 0.0).astype(BF16)
        mask_t[t] = jnp.where(same & later_col, 1.0, 0.0).astype(BF16)

    def seg_chunk(t):
        return seg_rows[pl.ds(pl.multiple_of(8 + t * CHUNK, 8), CHUNK), :]

    def seg_at(t, row):
        return seg_rows[pl.ds(8 + t * CHUNK + row, 1), :]

    def flags(one, two):
        return twice(jnp.where(one == two, 1.0, 0.0))

    tiny.own()
    gather_0.line_b(1)
    gather_1.line_a(2)

    local[9].wait()
    def norm_one(t):
        at = rows_of(t)
        h = n.inputs[at].astype(F32)
        centre = h - mean_last(h)
        scale = lax.rsqrt(mean_last(centre * centre) + epsilon)
        n.normal_one[at] = (centre * scale).astype(BF16)
        n.scale_one[at] = jnp.broadcast_to(scale, (CHUNK, 128))

    per_chunk([], norm_one)
    gather_1.line_a(1)
    tiny.second()
    gather_0.twin(2)
    gather_1.line_b(2)
    gather_1.line_a(0)
    gather_1.line_b(1)
    gather_0.twin(0)
    gather_0.twin(1)
    gather_0.rest()
    tiny.third()
    tiny.last()
    gather_2.line_a(0)
    gather_2.line_b_own()
    gather_2.line_a(2)
    gather_1.line_b(0)

    blocks = smalls[...].reshape(shards * 8, 128).astype(BF16)
    lane = iota((128, WIDTH), 1)
    row = iota((128, WIDTH), 0)
    block = iota((shards, 8, WIDTH), 0)
    at_lane = iota((shards, 8, WIDTH), 2)
    spread = jnp.where(lane % R == row, 1.0, 0.0).astype(BF16)
    laid = dot(blocks, spread).reshape(shards, 8, WIDTH)
    vecs[0:8] = jnp.sum(jnp.where(at_lane // R == block, laid, 0.0), axis=0)
    spread = jnp.where(lane % (4 * R) == row, 1.0, 0.0).astype(BF16)
    laid = dot(blocks, spread).reshape(shards, 8, WIDTH)
    for i in range(4):
        picked = jnp.where((at_lane + i * WIDTH) // (4 * R) == block, laid, 0.0)
        vecs[8 + i : 9 + i] = jnp.sum(picked, axis=0)[0:1]
    b_down, gain_one, shift_one, gain_two, shift_two = (vecs[i : i + 1] for i in range(1, 6))


    def weight(i):
        return full[:, :, :, i * R : (i + 1) * R, :].reshape(WIDTH, WIDTH)

    def weight_down(i):
        return full[i, :, :, 8 * R : 12 * R, :].reshape(WIDTH, WIDTH)

    lanes = [slice(g * GROUP, (g + 1) * GROUP) for g in range(GROUPS)]
    state, state_now, keys_now = n.state, n.state_now, n.keys_now
    state_now[...] = jnp.zeros(state_now.shape, F32)
    keys_now[...] = jnp.zeros(keys_now.shape, F32)
    slots[0] = jnp.zeros(slots.shape[1:], F32)

    def forward(g):
        cut = lanes[g]

        def weight_part(i):
            return full[:, :, :, i * R : (i + 1) * R, cut].reshape(WIDTH, GROUP)

        def body(t):
            at = rows_of(t)
            if g == 0:
                normed = (n.normal_one[at].astype(F32) * gain_one + shift_one).astype(BF16)
                n.normed_attn[at] = normed
            else:
                normed = n.normed_attn[at]
            q = feature(dot(normed, weight_part(0))).astype(BF16)
            k = feature(dot(normed, weight_part(1))).astype(BF16)
            v = dot(normed, weight_part(2)).astype(BF16)
            n.query[at, cut], n.key[at, cut], n.value[at, cut] = q, k, v
            seg = seg_chunk(t)
            before = flags(seg, seg_at(t, -1))
            ending = flags(seg, seg_at(t, CHUNK - 1)).astype(BF16)
            carry = flags(seg_at(t, CHUNK - 1), seg_at(t, -1))
            old = state_now[g].astype(BF16)
            state[g, t] = old
            mixed = dot(q * before.astype(BF16), old)
            for i in range(PER_GROUP):
                scores = dot_nt(q * heads[i], k).astype(BF16) * mask[t]
                mixed = mixed + dot(scores, v * heads[i])
            sums = dot(mask[t], k) + before * keys_now[g, 0:1]
            n.key_sums[at, cut] = sums
            totals = dot((q.astype(F32) * sums).astype(BF16), n.ones[...])
            inverse = 1.0 / totals
            n.inverse[at, cut] = inverse
            n.context[at, cut] = (mixed * inverse).astype(BF16)
            ended = k * ending
            state_now[g] = state_now[g] * carry + dot_tn(ended, v) * n.ones[...].astype(F32)
            keys_now[g, 0:1] = keys_now[g, 0:1] * carry + column_sum(ended.astype(F32))

        return body

    per_chunk([[], [], [(lambda: gather_2.line_a(1)), (lambda: gather_1.twin(1))], []], forward(0))
    gather_2.line_b(0)
    gather_2.line_b(2)
    gather_1.twin(2)
    per_chunk([[], [(lambda: gather_1.twin(0))], [], []], forward(1))
    gather_1.rest()
    gather_2.line_b(1)

    c0 = 0.7978845608028654
    c1 = c0 * 0.044715

    def hidden_units(which):
        def body(t):
            at = rows_of(t)
            if which == 0:
                after = n.inputs[at].astype(F32) + dot(n.context[at], weight(3))
                centre = after - mean_last(after)
                scale = lax.rsqrt(mean_last(centre * centre) + epsilon)
                normal = centre * scale
                n.normal_two[at] = normal.astype(BF16)
                n.scale_two[at] = jnp.broadcast_to(scale, (CHUNK, 128))
                normed = (normal * gain_two + shift_two).astype(BF16)
                n.normed_ffn[at] = normed
                n.result[at] = after + b_down
                n.grad_normed[at] = jnp.zeros((CHUNK, WIDTH), F32)
            else:
                normed = n.normed_ffn[at]
            for i in (2 * which, 2 * which + 1):
                pre = dot(normed, weight(4 + i)) + vecs[8 + i : 9 + i]
                square = pre * pre
                half = 0.5 + 0.5 * jnp.tanh(pre * (c0 + c1 * square))
                hidden = pre * half
                slope = half + (2.0 * hidden) * (1.0 - half) * (c0 + (3.0 * c1) * square)
                cut = slice(i * WIDTH, (i + 1) * WIDTH)
                n.hidden[at, cut] = hidden.astype(BF16)
                n.grad_pre[at, cut] = slope.astype(BF16)

        return body

    per_chunk([[], [], [(lambda: gather_2.twin(1)), (lambda: gather_2.twin(0))], []], hidden_units(0))
    per_chunk([[(lambda: gather_2.twin(2))], [gather_2.rest], [], []], hidden_units(1))
    local[10].wait()
    sends.finish()

    def ffn(i, events):
        cut = slice(i * WIDTH, (i + 1) * WIDTH)

        def body(t):
            at = rows_of(t)
            n.result[at] = n.result[at] + dot(n.hidden[at, cut], weight_down(i))
            grad = dot_nt(n.cotangent[at], weight_down(i)) * n.grad_pre[at, cut].astype(F32)
            grad = grad.astype(BF16)
            n.grad_pre[at, cut] = grad
            slots[0, i : i + 1] += column_sum(grad.astype(F32))
            n.grad_normed[at] = n.grad_normed[at] + dot_nt(grad, weight(4 + i))

        per_chunk(events, body)
        for m in range(2):
            some = slice(i * WIDTH + m * 256, i * WIDTH + (m + 1) * 256)
            grad = dot_tn(n.hidden[:, some], n.cotangent[...]).astype(BF16)
            part[i, m * B // 2 : (m + 1) * B // 2, :, 8 * R : 12 * R, :] = grad.reshape(
                B // 2, 2, 4 * R, WIDTH
            )
            some = slice(m * 256, (m + 1) * 256)
            grad = dot_tn(n.normed_ffn[:, some], n.grad_pre[:, cut]).astype(BF16)
            part[2 * m : 2 * m + 2, :, :, (4 + i) * R : (5 + i) * R, :] = grad.reshape(
                2, B, 2, R, WIDTH
            )

    ffn(0, [[], [], [], []])
    ffn(1, [[], [], [], []])
    down_one.start()
    ffn(2, [[], [], [up_one.start, down_one.after_core], []])
    ffn(3, [[], [], [up_one.after_core], []])
    up_two.start()
    down_two.start()

    def norm_two_back(t):
        at = rows_of(t)
        n.output[at] = n.result[at].astype(BF16)
        grad = n.grad_normed[at]
        normal = n.normal_two[at].astype(F32)
        up = n.cotangent[at].astype(F32)
        slots[0, 4:5] += column_sum(up)
        slots[0, 7:8] += column_sum(grad * normal)
        slots[0, 8:9] += column_sum(grad)
        e = grad * gain_two
        back = e - mean_last(e) - normal * mean_last(e * normal)
        after = up + n.scale_two[at][:, 0:1] * back
        n.grad_normed[at] = after
        low = after.astype(BF16)
        n.grad_attn[at] = low
        grad_context = dot_nt(low, weight(3)).astype(BF16).astype(F32)
        inverse = n.inverse[at]
        n.grad_mixed[at] = (grad_context * inverse).astype(BF16)
        turned = (grad_context * n.context[at].astype(F32)).astype(BF16)
        for g in range(GROUPS):
            n.grad_totals[at, lanes[g]] = -dot(turned[:, lanes[g]], n.ones[...]) * inverse[
                :, lanes[g]
            ]

    per_chunk([[], [], [], []], norm_two_back)
    down_two.after_core()
    down_one.second()
    store = pltpu.make_async_copy(n.output, n.output_far, n.sem_local.at[11])
    store.start()
    for m in range(2):
        grad = dot_tn(n.context[:, m * 256 : (m + 1) * 256], n.grad_attn[...]).astype(BF16)
        part[2 * m : 2 * m + 2, :, :, 3 * R : 4 * R, :] = grad.reshape(2, B, 2, R, WIDTH)
    up_two.after_core()

    def backward(g):
        state_now[g] = jnp.zeros((GROUP, GROUP), F32)
        keys_now[g] = jnp.zeros((8, GROUP), F32)

        def body(t):
            at = rows_of(t)
            seg = seg_chunk(t)
            before = flags(seg, seg_at(t, -1)).astype(BF16)
            after = flags(seg, seg_at(t, CHUNK))
            opening = flags(seg, seg_at(t, 0)).astype(BF16)
            carry = flags(seg_at(t, 0), seg_at(t, CHUNK))
            q, k, v, gm = (
                ref[at, lanes[g]] for ref in (n.query, n.key, n.value, n.grad_mixed)
            )
            totals = n.grad_totals[at, lanes[g]]
            old = state_now[g].astype(BF16)
            weighted = totals * q.astype(F32)
            gq = dot_nt(gm * before, state[g, t]) + totals * n.key_sums[at, lanes[g]]
            gk = after * (dot_nt(v, old) + keys_now[g, 0:1]) + dot(mask_t[t], weighted.astype(BF16))
            gv = after * dot(k, old)
            for i in range(PER_GROUP):
                head = heads[i]
                gm_head = gm * head
                back = dot_nt(gm_head, v).astype(BF16) * mask[t]
                gq = gq + dot(back, k * head)
                back = dot_nt(v * head, gm).astype(BF16) * mask_t[t]
                gk = gk + dot(back, q * head)
                back = dot_nt(k * head, q).astype(BF16) * mask_t[t]
                gv = gv + dot(back, gm_head)
            n.grad_query[at, lanes[g]] = (gq * jnp.minimum(q.astype(F32), 1.0)).astype(BF16)
            n.grad_key[at, lanes[g]] = (gk * jnp.minimum(k.astype(F32), 1.0)).astype(BF16)
            n.grad_value[at, lanes[g]] = gv.astype(BF16)
            opened = q * opening
            state_now[g] = state_now[g] * carry + dot_tn(opened, gm) * n.ones[...].astype(F32)
            keys_now[g, 0:1] = keys_now[g, 0:1] * carry + column_sum(
                weighted * opening.astype(F32)
            )

        return body

    def weight_grads(g):
        for i, ref in enumerate((n.grad_query, n.grad_key, n.grad_value)):
            grad = dot_tn(n.normed_attn[...], ref[:, lanes[g]]).astype(BF16)
            part[:, :, :, i * R : (i + 1) * R, lanes[g]] = grad.reshape(A, B, 2, R, GROUP)

    per_chunk([[], [], [], []], backward(0), down=True)
    down_one.third()
    weight_grads(0)
    per_chunk([[down_two.second, attn_one.start, up_one.second], [attn_one.after_core], [out_all.start], []], backward(1), down=True)
    up_two.second()
    down_two.third()
    weight_grads(1)
    out_all.after_core()
    attn_three.start()

    def norm_one_back(t):
        at = rows_of(t)
        grad = dot_nt(n.grad_query[at], weight(0))
        grad = grad + dot_nt(n.grad_key[at], weight(1))
        grad = grad + dot_nt(n.grad_value[at], weight(2))
        normal = n.normal_one[at].astype(F32)
        slots[0, 5:6] += column_sum(grad * normal)
        slots[0, 6:7] += column_sum(grad)
        e = grad * gain_one
        back = e - mean_last(e) - normal * mean_last(e * normal)
        n.grad_inputs[at] = n.grad_normed[at] + n.scale_one[at][:, 0:1] * back

    per_chunk([[attn_three.after_core], [up_two.third], [out_all.second, attn_one.second, attn_two.start, attn_two.after_core], []], norm_one_back)
    store_more = pltpu.make_async_copy(n.grad_inputs, n.grad_inputs_far, n.sem_local.at[12])
    store_more.start()
    up_one.third()
    out_all.third()
    down_one.after_a()
    attn_two.second()
    attn_three.second()
    T[0]()
    T[1]()
    attn_one.third()
    attn_two.third()
    T[2]()
    attn_three.third()
    up_one.after_a()
    T[3]()
    attn_two.after_a()
    up_two.after_a()
    out_all.after_a()
    attn_one.after_a()
    attn_three.after_a()
    attn_one.finish()
    attn_two.finish()
    up_two.finish()
    attn_three.finish()
    T[4]()
    down_one.finish()

    total = slots[small_sum.now]
    high = total.astype(BF16)
    low = (total - high.astype(F32)).astype(BF16)
    row, lane = iota((WIDTH, 128), 0), iota((WIDTH, 128), 1)
    pick = jnp.where((row == lane + p.s * R) & (lane < R), 1.0, 0.0).astype(BF16)
    n.tiny_out[0:16] = dot(high, pick) + dot(low, pick)
    picked = jnp.zeros((16, 128), F32)
    for i in range(4):
        wanted = (row + i * WIDTH == lane + p.s * (4 * R)) & (lane < 4 * R)
        pick = jnp.where(wanted, 1.0, 0.0).astype(BF16)
        keep = iota((16, 128), 0) == i
        picked = picked + jnp.where(keep, dot(high, pick) + dot(low, pick), 0.0)
    n.tiny_out[16:17] = column_sum(picked)

    out_all.finish()
    up_one.finish()
    store.wait()
    store_more.wait()
    sends.finish()


PIECES = 4


def final_kernel(output, grad_inputs, done, tiny, *refs):
    out, grad, query, key, value, out_w, up, down = refs[:8]
    held_out, held_grad, sem = refs[-3:]
    rows = output.shape[0] // PIECES
    into, back = [], []
    for i in range(PIECES):
        cut = pl.ds(i * rows, rows)
        for k, (src, held, dst) in enumerate(
            ((grad_inputs, held_grad, grad), (output, held_out, out))
        ):
            into.append(pltpu.make_async_copy(src.at[cut], held.at[cut], sem.at[0, k, i]))
            back.append(pltpu.make_async_copy(held.at[cut], dst.at[cut], sem.at[1, k, i]))
    for copy in into:
        copy.start()
    R = query.shape[0]
    for i, ref in enumerate((query, key, value, out_w)):
        ref[...] = done[i * R : (i + 1) * R].astype(F32)
    for i in range(4):
        up[:, i * WIDTH : (i + 1) * WIDTH] = done[(4 + i) * R : (5 + i) * R].astype(F32)
    down[...] = done[8 * R : 12 * R].astype(F32)
    for ref, row in zip(refs[8:14], (16, 4, 5, 6, 7, 8), strict=True):
        ref[...] = tiny[row, : ref.shape[0]]
    for one, two in zip(into, back, strict=True):
        one.wait()
        two.start()
    for copy in back:
        copy.wait()


def final(output, grad_inputs, done, tiny):
    R = done.shape[0] // 12
    vmem, far = pl.BlockSpec(memory_space=pltpu.VMEM), pl.BlockSpec(memory_space=pl.ANY)
    shapes = [(output.shape, BF16), (grad_inputs.shape, F32)] + [((R, WIDTH), F32)] * 4
    shapes += [((R, 4 * WIDTH), F32), ((4 * R, WIDTH), F32), ((4 * R,), F32)] + [((R,), F32)] * 5
    return pl.pallas_call(
        final_kernel,
        out_shape=tuple(jax.ShapeDtypeStruct(*shape) for shape in shapes),
        in_specs=[far, far, vmem, vmem],
        out_specs=(far, far) + (vmem,) * 12,
        scratch_shapes=[
            pltpu.VMEM(output.shape, BF16),
            pltpu.VMEM(grad_inputs.shape, F32),
            pltpu.SemaphoreType.DMA((2, 2, PIECES)),
        ],
        name="final",
    )(output, grad_inputs, done, tiny)


def layer(reps, shards, inputs, segment_ids, weights, vectors, cotangent):
    length = inputs.shape[0]
    A, B = 4, shards // 8
    R = weights[0].shape[0]
    rows = 12 * R
    bits = max(reps.bit_length() - 2, 0)
    copies, n_slots = SmallReduce.counts(reps, shards)
    sums = 5 * (2 * B + A + bits) + 2 * (3 * B - 1 + A + bits) + 1 * (3 * B - 1)
    groups = 3
    w_query, w_key, w_value, w_out, w_up, w_down = weights
    b_up, b_down, gain_attn, shift_attn, gain_ffn, shift_ffn = vectors
    far_ins = dict(
        inputs_far=inputs,
        cotangent_far=cotangent,
        w_query=w_query,
        w_key=w_key,
        w_value=w_value,
        w_out=w_out,
        w_up=w_up,
        w_down=w_down,
    )
    ins = dict(
        segment_ids=segment_ids,
        b_up=b_up,
        b_down=b_down,
        gain_attn=gain_attn,
        shift_attn=shift_attn,
        gain_ffn=gain_ffn,
        shift_ffn=shift_ffn,
    )
    far_outs = dict(
        output_far=((length, WIDTH), BF16),
        grad_inputs_far=((length, WIDTH), F32),
    )
    outs = dict(
        done=((rows, WIDTH), BF16),
        tiny_out=((24, 128), F32),
    )
    tall = (length, WIDTH)
    buffers = dict(
        inputs=(tall, BF16),
        cotangent=(tall, BF16),
        output=(tall, BF16),
        grad_inputs=(tall, F32),
        full=((A, B, 2, rows, WIDTH), BF16),
        part=((A, B, 2, rows, WIDTH), BF16),
        core=((A, B, rows, WIDTH), BF16),
        line_b=((B - 1, A, rows, WIDTH), BF16),
        pair=((A, B, rows, WIDTH), BF16),
        line_a=((A - 1, rows, WIDTH), BF16),
        wide=((max(2 * bits, 1), rows if bits else 16, WIDTH), BF16),
        smalls=((A, B, 2, 8, 128), F32),
        slots=((n_slots, 16, WIDTH), F32),
        vecs=((16, WIDTH), F32),
        seg_rows=((length + 16, 128), F32),
        heads=((PER_GROUP, CHUNK, GROUP), BF16),
        ones=((GROUP, GROUP), BF16),
        mask=((length // CHUNK, CHUNK, CHUNK), BF16),
        mask_t=((length // CHUNK, CHUNK, CHUNK), BF16),
        normal_one=(tall, BF16),
        scale_one=((length, 128), F32),
        normed_attn=(tall, BF16),
        query=(tall, BF16),
        key=(tall, BF16),
        value=(tall, BF16),
        key_sums=(tall, F32),
        inverse=(tall, F32),
        context=(tall, BF16),
        state=((GROUPS, length // CHUNK, GROUP, GROUP), BF16),
        state_now=((GROUPS, GROUP, GROUP), F32),
        keys_now=((GROUPS, 8, GROUP), F32),
        normal_two=(tall, BF16),
        scale_two=((length, 128), F32),
        normed_ffn=(tall, BF16),
        hidden=((length, 4 * WIDTH), BF16),
        grad_pre=((length, 4 * WIDTH), BF16),
        grad_normed=(tall, F32),
        grad_attn=(tall, BF16),
        grad_mixed=(tall, BF16),
        grad_totals=(tall, F32),
    )
    sems = dict(
        sem_local=(13,),
        send0=(A + B,),
        recv0=(A + B,),
        send1=(max(groups * Gather.n_sems(shards), sums),),
        recv1=(groups * Gather.n_sems(shards),),
        recv2=(sums,),
        send3=(copies,),
        recv3=(copies,),
    )
    names = [*far_ins, *ins, *far_outs, *outs, *buffers, *sems]

    def kernel(*refs):
        n = types.SimpleNamespace(**dict(zip(names, refs, strict=True)))
        n.result = n.grad_inputs
        n.grad_query, n.grad_key, n.grad_value = (
            n.hidden.at[:, pl.ds(i * WIDTH, WIDTH)] for i in range(3)
        )
        layer_kernel(reps, shards, length, n)

    vmem, far = pl.BlockSpec(memory_space=pltpu.VMEM), pl.BlockSpec(memory_space=pl.ANY)
    flops = 2 * 3 * length * WIDTH * WIDTH * 12 + 20 * length * length * WIDTH
    return pl.pallas_call(
        kernel,
        out_shape=tuple(
            jax.ShapeDtypeStruct(*spec) for spec in [*far_outs.values(), *outs.values()]
        ),
        in_specs=[far] * len(far_ins) + [vmem] * len(ins),
        out_specs=(far,) * len(far_outs) + (vmem,) * len(outs),
        scratch_shapes=[pltpu.VMEM(*spec) for spec in buffers.values()]
        + [pltpu.SemaphoreType.DMA(shape) for shape in sems.values()],
        compiler_params=pltpu.CompilerParams(
            collective_id=1, has_side_effects=True, vmem_limit_bytes=63 << 20
        ),
        cost_estimate=pl.CostEstimate(flops=flops, bytes_accessed=8 << 20, transcendentals=0),
        name="layer",
    )(*far_ins.values(), *ins.values())


def on_device(
    reps,
    shards,
    inputs,
    segment_ids,
    w_query,
    w_key,
    w_value,
    w_out,
    w_up,
    w_down,
    b_up,
    b_down,
    gain_attn,
    shift_attn,
    gain_ffn,
    shift_ffn,
    cotangent,
):
    sequences, length, width = inputs.shape
    output, grad_inputs, done, tiny = layer(
        reps,
        shards,
        inputs.reshape(sequences * length, width),
        segment_ids,
        (w_query, w_key, w_value, w_out, w_up, w_down),
        (b_up, b_down, gain_attn, shift_attn, gain_ffn, shift_ffn),
        cotangent.reshape(sequences * length, width),
    )
    output, grad_inputs, *grads = final(output, grad_inputs, done, tiny)
    return (output.reshape(inputs.shape), grad_inputs.reshape(inputs.shape), *grads)


def solution(mesh):
    reps, shards = mesh.shape["rep"], mesh.shape["shard"]
    token = P(("rep", "shard"), None, None)
    matrix, vector = P("shard", None), P("shard")
    return jax.shard_map(
        functools.partial(on_device, reps, shards),
        mesh=mesh,
        in_specs=(token, P(("rep", "shard"), None)) + (matrix,) * 6 + (vector,) * 6 + (token,),
        out_specs=(token, token) + (matrix,) * 6 + (vector,) * 6,
        check_vma=False,
    )
```

```python
import functools
import types

import jax
import jax.numpy as jnp
from jax import lax
from jax.experimental import pallas as pl
from jax.experimental.pallas import tpu as pltpu
from jax.sharding import PartitionSpec as P

WIDTH = 512
CHUNK = 256
HEAD_DIM = 64
GROUP = 256
PER_GROUP = GROUP // HEAD_DIM
GROUPS = WIDTH // GROUP

epsilon = 1e-05
MESH = pl.DeviceIdType.MESH
F32 = jnp.float32
BF16 = jnp.bfloat16


class Place:
    def __init__(self, reps, shards):
        self.reps, self.shards = reps, shards
        self.A = 4
        self.B = shards // 8
        self.r = lax.axis_index("rep")
        s = lax.axis_index("shard")
        self.s = s
        self.c = lax.rem(s, 2)
        self.b = lax.rem(s // 2, self.B)
        self.a = s // (2 * self.B)
        self.h = lax.rem(self.r, 2)

    def at(self, a=None, b=None, c=None, r=None):
        a = self.a if a is None else a
        b = self.b if b is None else b
        c = self.c if c is None else c
        r = self.r if r is None else r
        return (r, (a * self.B + b) * 2 + c)

    def near(self, k):
        high = self.a // 2
        return (1 - self.a + 4 * high, 2 - high, 3 * (1 - high))[k]

    def next_a(self, j):
        return lax.rem(self.a + j, self.A)

    def next_b(self, j):
        return lax.rem(self.b + j, self.B)

    def sibling(self):
        return self.at(c=1 - self.c)

    def twin(self, bit=1):
        return self.at(r=self.r + bit - 2 * bit * lax.rem(self.r // bit, 2))

    def bits(self):
        bit, out = 2, []
        while bit < self.reps:
            out.append(bit)
            bit *= 2
        return out

    def partners(self):
        out = [self.sibling(), self.twin()]
        out += [self.at(a=self.next_a(j)) for j in range(1, self.A)]
        out += [self.at(b=self.next_b(j)) for j in range(1, self.B)]
        return out + [self.twin(bit) for bit in self.bits()]


def greet(partners):
    barrier = pltpu.get_barrier_semaphore()
    for device in partners:
        pl.semaphore_signal(barrier, inc=1, device_id=device, device_id_type=MESH)
    pl.semaphore_wait(barrier, len(partners))


def remote(src, dst, send, recv, device):
    return pltpu.make_async_remote_copy(
        src_ref=src, dst_ref=dst, send_sem=send, recv_sem=recv, device_id=device, device_id_type=MESH
    )


def both(one, two):
    if one is None:
        return two
    return one if two is None else jnp.logical_and(one, two)


class Sends:
    def __init__(self):
        self.made = []

    @staticmethod
    def act(copy, do):
        cond, make = copy()
        if cond is None:
            do(make())
        else:
            pl.when(cond)(lambda: do(make()))

    def go(self, copy):
        self.act(copy, lambda made: made.start())
        self.made.append(copy)

    def arrived(self, copy):
        self.act(copy, lambda made: made.wait_recv())

    def finish(self):
        for copy in self.made:
            self.act(copy, lambda made: made.wait_send())
        self.made = []


class Gather:
    def __init__(self, place, full, window, send, recv, base, sends):
        self.p, self.full = place, full
        self.lo, self.rows, self.left, self.lanes = window
        self.send, self.recv, self.base, self.sends = send, recv, base, sends

    def whole(self, a, b, c):
        return self.full.at[a, b, c, pl.ds(self.lo, self.rows), pl.ds(self.left, self.lanes)]

    def half(self, a, b, c, h):
        size = self.lanes // 2
        lanes = pl.ds(pl.multiple_of(self.left + h * size, 128), size)
        return self.full.at[a, b, c, pl.ds(self.lo, self.rows), lanes]

    def copy(self, ref, k, device, other=None):
        return remote(ref, ref, self.send.at[k], self.recv.at[k if other is None else other], device)

    def go(self, make):
        self.sends.go(lambda: (None, make))

    def slot(self, kind, k=0, j=0):
        more = self.p.B - 1
        j = max(j - 1, 0)
        base = (0, 4, 4 + more, 4 + 4 * more, 7 + 4 * more, 7 + 7 * more)
        base += (8 + 7 * more, 8 + 8 * more, 11 + 8 * more)
        return self.base + base[kind] + (k * more if kind in (2, 4) else k) + j

    def own(self):
        p = self.p
        for k in (2, 1, 0):
            self.go(
                lambda k=k: self.copy(
                    self.half(p.a, p.b, p.c, p.h) if k else self.whole(p.a, p.b, p.c),
                    self.slot(0, k),
                    p.at(a=p.near(k)),
                    self.slot(0, p.a),
                )
            )
        for j in range(1, p.B):
            self.go(
                lambda j=j: self.copy(
                    self.whole(p.a, p.b, p.c), self.slot(1, 0, j), p.at(b=p.next_b(j))
                )
            )
        self.go(lambda: self.copy(self.whole(p.a, p.b, p.c), self.slot(5), p.sibling()))

    def line_a(self, k):
        p = self.p
        place = (p.near(k), p.b, p.c)
        ref = self.half(*place, p.h) if k else self.whole(*place)
        self.copy(ref, self.slot(0, p.near(k)), p.sibling()).wait_recv()

        def mine():
            return self.half(p.near(k), p.b, p.c, p.h)

        for j in range(1, p.B):
            self.go(lambda j=j: self.copy(mine(), self.slot(2, k, j), p.at(b=p.next_b(j))))
        if k:
            self.go(lambda: self.copy(mine(), self.slot(3, k), p.twin()))

    def line_b_own(self):
        p = self.p
        for j in range(1, p.B):
            b = p.next_b(p.B - j)
            self.copy(self.whole(p.a, b, p.c), self.slot(1, 0, j), p.sibling()).wait_recv()
            self.go(
                lambda j=j: self.copy(
                    self.whole(p.a, p.next_b(p.B - j), p.c), self.slot(6, 0, j), p.sibling()
                )
            )

    def line_b(self, k):
        p = self.p
        for j in range(1, p.B):
            b = p.next_b(p.B - j)
            ref = self.half(p.near(k), b, p.c, p.h)
            self.copy(ref, self.slot(2, k, j), p.sibling()).wait_recv()
            self.go(
                lambda j=j: self.copy(
                    self.half(p.near(k), p.next_b(p.B - j), p.c, p.h), self.slot(4, k, j), p.twin()
                )
            )
        self.go(
            lambda: self.copy(
                self.half(p.near(k), slice(None), p.c, p.h), self.slot(7, k), p.sibling()
            )
        )

    def twin(self, k):
        p = self.p
        for j in range(0 if k else 1, p.B):
            ref = self.half(p.near(k), p.next_b(p.B - j), p.c, 1 - p.h)
            kind = 4 if j else 3
            self.copy(ref, self.slot(kind, k, j), p.sibling()).wait_recv()
        self.go(
            lambda: self.copy(
                self.half(p.near(k), slice(None), p.c, 1 - p.h), self.slot(8, k), p.sibling()
            )
        )

    def rest(self):
        p = self.p
        other = 1 - p.c
        self.copy(self.whole(p.a, p.b, other), self.slot(5), p.sibling()).wait_recv()
        for j in range(1, p.B):
            ref = self.whole(p.a, p.next_b(p.B - j), other)
            self.copy(ref, self.slot(6, 0, j), p.sibling()).wait_recv()
        for k in range(3):
            for kind, h in ((7, p.h), (8, 1 - p.h)):
                ref = self.half(p.near(k), slice(None), other, h)
                self.copy(ref, self.slot(kind, k), p.sibling()).wait_recv()

    @staticmethod
    def n_sems(shards):
        return 14 + 8 * (shards // 8 - 1)


class SmallGather:
    def __init__(self, place, full, send, recv, sends):
        self.p, self.full, self.send, self.recv, self.sends = place, full, send, recv, sends

    def copy(self, ref, k, device):
        return remote(ref, ref, self.send.at[k], self.recv.at[k], device)

    def own(self):
        p = self.p
        for j in range(1, p.A):
            self.sends.go(
                lambda j=j: (
                    None,
                    lambda: self.copy(self.full.at[p.a, p.b, p.c], j, p.at(a=p.next_a(j))),
                )
            )

    def second(self):
        p = self.p
        for j in range(1, p.A):
            self.copy(self.full.at[p.next_a(p.A - j), p.b, p.c], j, p.sibling()).wait_recv()
        for j in range(1, p.B):
            self.sends.go(
                lambda j=j: (
                    None,
                    lambda: self.copy(self.full.at[:, p.b, p.c], p.A + j, p.at(b=p.next_b(j))),
                )
            )

    def third(self):
        p = self.p
        for j in range(1, p.B):
            self.copy(self.full.at[:, p.next_b(p.B - j), p.c], p.A + j, p.sibling()).wait_recv()
        self.sends.go(lambda: (None, lambda: self.copy(self.full.at[:, :, p.c], 0, p.sibling())))

    def last(self):
        p = self.p
        self.copy(self.full.at[:, :, 1 - p.c], 0, p.sibling()).wait_recv()


class Reduce:
    def __init__(self, place, part, bufs, window, sems, base, sends, pair_first=False, span=None, end=None):
        self.p, self.part = place, part
        self.lo, self.rows, self.at, self.lanes = window
        self.core, self.line_b, self.pair, self.line_a, self.wide, self.done = bufs
        self.send, self.recv = sems
        self.sends = sends
        self.pair_first = pair_first
        self.first, self.last = span or (0, place.A)
        self.end = end or self
        self.base = base

    def slot(self, kind, j=0):
        B = self.p.B
        twins = B if self.pair_first else 1
        base = (0, B - 1, 2 * B - 1, 2 * B - 2 + twins, 2 * B + 2 + twins, 2 * B + 3 + twins)
        return self.base + base[kind] + j

    def n_sems(self):
        last = self.slot(3, 1) if self.end is not self else self.slot(5, len(self.p.bits()))
        return last - self.base

    def span(self):
        return slice(self.first, self.last)

    def win(self):
        return (pl.ds(self.lo, self.rows), pl.ds(self.at, self.lanes))

    def half(self, h):
        size = self.lanes // 2
        return (
            pl.ds(self.lo, self.rows),
            pl.ds(pl.multiple_of(self.at + h * size, 128), size),
        )

    def go(self, copy, when=lambda: None):
        self.sends.go(lambda: (when(), lambda: self.copy(*copy())))

    def copy(self, src, dst, k, device):
        return remote(src, dst, self.send.at[k], self.recv.at[k], device)

    def arrived(self, ref, k):
        self.copy(ref, ref, k, self.p.sibling()).wait_recv()

    def order(self):
        return list(range(1, self.p.B)) + [0]

    def start(self):
        p = self.p
        for j in self.order():
            self.go(
                lambda j=j: (
                    self.part.at[(self.span(), p.next_b(j), 1 - p.c) + self.win()],
                    self.core.at[(self.span(), j) + self.win()],
                    self.slot(0, j),
                    p.sibling(),
                )
            )

    def after_core(self):
        p = self.p
        for j in self.order():
            mine = (self.span(), p.next_b(j), p.c) + self.win()
            got = (self.span(), j) + self.win()
            self.arrived(self.core.at[got], self.slot(0, j))
            self.part[mine] = self.part[mine] + self.core[got]
            if self.pair_first:
                self.to_pair(j)
            elif j > 0:
                self.to_b(j, self.win)

    def to_b(self, j, win):
        p = self.p
        self.go(
            lambda: (
                self.part.at[(self.span(), p.next_b(j), p.c) + win()],
                self.line_b.at[(j - 1, self.span()) + win()],
                self.slot(1, j),
                p.at(b=p.next_b(j)),
            )
        )

    def to_pair(self, j):
        p = self.p
        self.go(
            lambda: (
                self.part.at[(self.span(), p.next_b(j), p.c) + self.half(1 - p.h)],
                self.pair.at[(self.span(), j) + self.half(1 - p.h)],
                self.slot(2, j),
                p.twin(),
            )
        )

    def to_a(self):
        p, end = self.p, self.end
        partial = self.last - self.first < p.A
        for j in range(1, p.A):

            def when(j=j):
                a = p.next_a(j)
                return both(a >= self.first, a < self.last) if partial else None

            end.go(
                lambda j=j: (
                    self.part.at[(p.next_a(j), p.b, p.c) + self.half(p.h)],
                    self.line_a.at[(j - 1,) + self.half(p.h)],
                    end.slot(3, j),
                    p.at(a=p.next_a(j)),
                ),
                when,
            )

    def add_b(self, win):
        p = self.p
        mine = (self.span(), p.b, p.c) + win
        total = self.part[mine].astype(F32)
        for j in range(1, p.B):
            got = (j - 1, self.span()) + win
            self.arrived(self.line_b.at[got], self.slot(1, j))
            total = total + self.line_b[got].astype(F32)
        self.part[mine] = total.astype(BF16)

    def add_pair(self, j):
        p = self.p
        got = (self.span(), j) + self.half(p.h)
        mine = (self.span(), p.next_b(j), p.c) + self.half(p.h)
        self.arrived(self.pair.at[got], self.slot(2, j))
        self.part[mine] = self.part[mine] + self.pair[got]

    def second(self):
        p = self.p
        if self.pair_first:
            for j in self.order():
                self.add_pair(j)
                if j > 0:
                    self.to_b(j, lambda: self.half(p.h))
        else:
            self.add_b(self.win())
            self.to_pair(0)

    def third(self):
        p = self.p
        if self.pair_first:
            self.add_b(self.half(p.h))
        else:
            self.add_pair(0)
        self.to_a()

    def after_a(self):
        p = self.p
        mine = self.half(p.h)
        total = self.part[(p.a, p.b, p.c) + mine].astype(F32)
        for j in range(1, p.A):
            got = (j - 1,) + mine
            self.arrived(self.line_a.at[got], self.slot(3, j))
            total = total + self.line_a[got].astype(F32)
        for i, bit in enumerate(p.bits()):
            k = self.slot(5, i)
            self.wide[(2 * i,) + mine] = total.astype(BF16)

            def copy(i=i, k=k, bit=bit):
                here = self.half(p.h)
                return (
                    self.wide.at[(2 * i,) + here],
                    self.wide.at[(2 * i + 1,) + here],
                    k,
                    p.twin(bit),
                )

            self.go(copy)
            self.arrived(self.wide.at[(2 * i + 1,) + mine], k)
            total = self.wide[(2 * i,) + mine].astype(F32)
            total = total + self.wide[(2 * i + 1,) + mine].astype(F32)
        self.done[mine] = total.astype(BF16)
        self.go(
            lambda: (
                self.done.at[self.half(p.h)],
                self.done.at[self.half(p.h)],
                self.slot(4),
                p.twin(),
            )
        )

    def finish(self):
        p = self.p
        self.arrived(self.done.at[self.half(1 - p.h)], self.slot(4))

    def steps(self):
        return [self.start, self.after_core, self.second, self.third, self.after_a, self.finish]


class SmallReduce:
    def __init__(self, place, slots, send, recv, sends):
        self.p, self.slots, self.send, self.recv, self.sends = place, slots, send, recv, sends
        self.now, self.free, self.k = 0, 1, 0

    def copy(self, src, dst, k, device):
        return remote(self.slots.at[src], self.slots.at[dst], self.send.at[k], self.recv.at[k], device)

    def exchange(self, devices):
        self.fresh = []
        for device in devices:
            src, dst, k = self.now, self.free, self.k
            self.fresh.append((dst, k))
            self.sends.go(
                lambda src=src, dst=dst, k=k, device=device: (
                    None,
                    lambda: self.copy(src, dst, k, device()),
                )
            )
            self.free, self.k = self.free + 1, self.k + 1

    def add(self):
        total = self.slots[self.now]
        for slot, k in self.fresh:
            self.copy(slot, slot, k, self.p.sibling()).wait_recv()
            total = total + self.slots[slot]
        self.slots[self.free] = total
        self.now, self.free = self.free, self.free + 1

    def steps(self):
        p = self.p
        stages = [
            [p.sibling],
            [lambda j=j: p.at(b=p.next_b(j)) for j in range(1, p.B)],
            [p.twin],
            [lambda j=j: p.at(a=p.next_a(j)) for j in range(1, p.A)],
        ] + [[functools.partial(p.twin, bit)] for bit in p.bits()]
        out = [lambda: self.exchange(stages[0])]
        for stage in stages[1:]:
            out.append(lambda stage=stage: (self.add(), self.exchange(stage)))
        out.append(self.add)
        return out

    @staticmethod
    def counts(reps, shards):
        wide = max(reps.bit_length() - 2, 0)
        copies = 1 + (shards // 8 - 1) + 1 + 3 + wide
        return copies, 1 + copies + 4 + wide


def dot(lhs, rhs):
    return lax.dot_general(lhs, rhs, (((1,), (0,)), ((), ())), preferred_element_type=F32)


def dot_nt(lhs, rhs):
    return lax.dot_general(lhs, rhs, (((1,), (1,)), ((), ())), preferred_element_type=F32)


def dot_tn(lhs, rhs):
    return lax.dot_general(lhs, rhs, (((0,), (0,)), ((), ())), preferred_element_type=F32)


def iota(shape, axis):
    return lax.broadcasted_iota(jnp.int32, shape, axis)


def mean_last(value):
    return jnp.sum(value, axis=-1, keepdims=True) * (1.0 / value.shape[-1])


def column_sum(value):
    return jnp.sum(value, axis=0, keepdims=True)


def twice(value):
    return jnp.concatenate([value, value], axis=1)


def feature(value):
    return jnp.where(value > 0, value + 1.0, jnp.exp(jnp.minimum(value, 0.0)))


def layer_kernel(reps, shards, length, n):
    p = Place(reps, shards)
    A, B = p.A, p.B
    rows_w = n.w_query.shape[0]
    R = rows_w
    chunks = length // CHUNK
    full, part, smalls, slots, vecs = n.full, n.part, n.smalls, n.slots, n.vecs

    mine = full.at[p.a, p.b, p.c]
    pieces = [
        (ref, mine.at[pl.ds(i * R, R)])
        for i, ref in enumerate((n.w_query, n.w_key, n.w_value, n.w_out))
    ]
    pieces += [
        (n.w_up.at[:, pl.ds(i * WIDTH, WIDTH)], mine.at[pl.ds((4 + i) * R, R)]) for i in range(4)
    ]
    pieces += [(n.w_down, mine.at[pl.ds(8 * R, 4 * R)])]
    pieces += [(n.inputs_far, n.inputs), (n.cotangent_far, n.cotangent)]
    local = [
        pltpu.make_async_copy(src, dst, n.sem_local.at[i]) for i, (src, dst) in enumerate(pieces)
    ]
    for copy in local:
        copy.start()
    smalls[p.a, p.b, p.c] = jnp.zeros((8, 128), F32)
    vectors = (n.b_up, n.b_down, n.gain_attn, n.shift_attn, n.gain_ffn, n.shift_ffn)
    for i, ref in enumerate(vectors):
        size = ref.shape[0]
        smalls[p.a, p.b, p.c, i : i + 1, 0:size] = ref[...].astype(F32).reshape(1, size)
    greet(p.partners())
    for copy in local[:9]:
        copy.wait()

    sends = Sends()
    tiny = SmallGather(p, smalls, n.send0, n.recv0, sends)
    windows = ((0 * R, 3 * R, 0, 512), (3 * R, 5 * R, 0, 512), (8 * R, 4 * R, 0, 512))
    gather_0, gather_1, gather_2 = (
        Gather(p, full, window, n.send1, n.recv1, i * Gather.n_sems(shards), sends)
        for i, window in enumerate(windows)
    )
    bufs = (n.core, n.line_b, n.pair, n.line_a, n.wide, n.done)

    made = []

    def job(lo, rows, at=0, lanes=WIDTH, **more):
        base = sum(one.n_sems() for one in made)
        window = (lo * R, rows * R, at, lanes)
        made.append(Reduce(p, part, bufs, window, (n.send2, n.recv2), base, sends, **more))
        return made[-1]

    up_one = job(4, 2)
    up_two = job(6, 2)
    down_one = job(8, 4, pair_first=True, span=(0, 2))
    down_two = job(8, 4, pair_first=True, span=(2, 4), end=down_one)
    out_all = job(3, 1)
    attn_one = job(0, 3, 0, 256)
    attn_two = job(0, 1, 256, 256)
    attn_three = job(1, 2, 256, 256, pair_first=True)
    assert sum(one.n_sems() for one in made) <= n.recv2.shape[0]
    small_sum = SmallReduce(p, slots, n.send3, n.recv3, sends)
    T = small_sum.steps()

    def rows_of(t):
        return pl.ds(pl.multiple_of(t * CHUNK, CHUNK), CHUNK)

    def per_chunk(events, body, down=False):
        def step(i, carry):
            body(chunks - 1 - i if down else i)
            for at, calls in enumerate(events):
                if calls:

                    @pl.when(i == at)
                    def _():
                        for call in calls:
                            call()

            return carry

        lax.fori_loop(0, chunks, step, 0)

    tiny.own()
    gather_0.own()
    tiny.second()
    gather_1.own()
    gather_0.line_a(1)
    gather_0.line_a(2)
    gather_0.line_a(0)
    gather_0.line_b(1)
    tiny.third()
    gather_1.line_b_own()
    gather_0.line_b(2)
    gather_2.own()
    gather_0.line_b_own()
    gather_0.line_b(0)

    seg_row = n.segment_ids[...].astype(F32)
    seg_rows = n.seg_rows
    seg_rows[0:8, :] = jnp.full((8, 128), -1.0, F32)
    seg_rows[pl.ds(8, length), :] = jnp.broadcast_to(seg_row, (128, length)).T
    seg_rows[pl.ds(8 + length, 8), :] = jnp.full((8, 128), -2.0, F32)
    heads, mask, mask_t = n.heads, n.mask, n.mask_t
    for i in range(PER_GROUP):
        heads[i] = jnp.where(iota((CHUNK, GROUP), 1) // HEAD_DIM == i, 1.0, 0.0).astype(BF16)
    same_head = (iota((GROUP, GROUP), 0) // HEAD_DIM) == (iota((GROUP, GROUP), 1) // HEAD_DIM)
    n.ones[...] = jnp.where(same_head, 1.0, 0.0).astype(BF16)
    later_row = iota((CHUNK, CHUNK), 0) >= iota((CHUNK, CHUNK), 1)
    later_col = iota((CHUNK, CHUNK), 0) <= iota((CHUNK, CHUNK), 1)
    for t in range(chunks):
        same = twice(seg_rows[pl.ds(8 + t * CHUNK, CHUNK), :]) == seg_row[
            :, t * CHUNK : (t + 1) * CHUNK
        ]
        mask[t] = jnp.where(same & later_row, 1.0, 0.0).astype(BF16)
        mask_t[t] = jnp.where(same & later_col, 1.0, 0.0).astype(BF16)

    def seg_chunk(t):
        return seg_rows[pl.ds(pl.multiple_of(8 + t * CHUNK, 8), CHUNK), :]

    def seg_at(t, row):
        return seg_rows[pl.ds(8 + t * CHUNK + row, 1), :]

    def flags(one, two):
        return twice(jnp.where(one == two, 1.0, 0.0))

    tiny.last()
    gather_0.twin(2)
    gather_1.line_a(1)
    gather_0.twin(1)

    local[9].wait()
    def norm_one(t):
        at = rows_of(t)
        h = n.inputs[at].astype(F32)
        centre = h - mean_last(h)
        scale = lax.rsqrt(mean_last(centre * centre) + epsilon)
        n.normal_one[at] = (centre * scale).astype(BF16)
        n.scale_one[at] = jnp.broadcast_to(scale, (CHUNK, 128))

    per_chunk([], norm_one)
    gather_0.twin(0)
    gather_1.line_a(2)

    blocks = smalls[...].reshape(shards * 8, 128).astype(BF16)
    lane = iota((128, WIDTH), 1)
    row = iota((128, WIDTH), 0)
    block = iota((shards, 8, WIDTH), 0)
    at_lane = iota((shards, 8, WIDTH), 2)
    spread = jnp.where(lane % R == row, 1.0, 0.0).astype(BF16)
    laid = dot(blocks, spread).reshape(shards, 8, WIDTH)
    vecs[0:8] = jnp.sum(jnp.where(at_lane // R == block, laid, 0.0), axis=0)
    spread = jnp.where(lane % (4 * R) == row, 1.0, 0.0).astype(BF16)
    laid = dot(blocks, spread).reshape(shards, 8, WIDTH)
    for i in range(4):
        picked = jnp.where((at_lane + i * WIDTH) // (4 * R) == block, laid, 0.0)
        vecs[8 + i : 9 + i] = jnp.sum(picked, axis=0)[0:1]
    b_down, gain_one, shift_one, gain_two, shift_two = (vecs[i : i + 1] for i in range(1, 6))

    gather_0.rest()

    def weight(i):
        return full[:, :, :, i * R : (i + 1) * R, :].reshape(WIDTH, WIDTH)

    def weight_down(i):
        return full[i, :, :, 8 * R : 12 * R, :].reshape(WIDTH, WIDTH)

    lanes = [slice(g * GROUP, (g + 1) * GROUP) for g in range(GROUPS)]
    state, state_now, keys_now = n.state, n.state_now, n.keys_now
    state_now[...] = jnp.zeros(state_now.shape, F32)
    keys_now[...] = jnp.zeros(keys_now.shape, F32)
    slots[0] = jnp.zeros(slots.shape[1:], F32)

    def forward(g):
        cut = lanes[g]

        def weight_part(i):
            return full[:, :, :, i * R : (i + 1) * R, cut].reshape(WIDTH, GROUP)

        def body(t):
            at = rows_of(t)
            if g == 0:
                normed = (n.normal_one[at].astype(F32) * gain_one + shift_one).astype(BF16)
                n.normed_attn[at] = normed
            else:
                normed = n.normed_attn[at]
            q = feature(dot(normed, weight_part(0))).astype(BF16)
            k = feature(dot(normed, weight_part(1))).astype(BF16)
            v = dot(normed, weight_part(2)).astype(BF16)
            n.query[at, cut], n.key[at, cut], n.value[at, cut] = q, k, v
            seg = seg_chunk(t)
            before = flags(seg, seg_at(t, -1))
            ending = flags(seg, seg_at(t, CHUNK - 1)).astype(BF16)
            carry = flags(seg_at(t, CHUNK - 1), seg_at(t, -1))
            old = state_now[g].astype(BF16)
            state[g, t] = old
            mixed = dot(q * before.astype(BF16), old)
            for i in range(PER_GROUP):
                scores = dot_nt(q * heads[i], k).astype(BF16) * mask[t]
                mixed = mixed + dot(scores, v * heads[i])
            sums = dot(mask[t], k) + before * keys_now[g, 0:1]
            n.key_sums[at, cut] = sums
            totals = dot((q.astype(F32) * sums).astype(BF16), n.ones[...])
            inverse = 1.0 / totals
            n.inverse[at, cut] = inverse
            n.context[at, cut] = (mixed * inverse).astype(BF16)
            ended = k * ending
            state_now[g] = state_now[g] * carry + dot_tn(ended, v) * n.ones[...].astype(F32)
            keys_now[g, 0:1] = keys_now[g, 0:1] * carry + column_sum(ended.astype(F32))

        return body

    per_chunk([[(lambda: gather_1.line_b(1)), gather_2.line_b_own, (lambda: gather_1.line_a(0))], [(lambda: gather_1.line_b(2))], [(lambda: gather_2.line_a(0))], []], forward(0))
    gather_1.line_b(0)
    per_chunk([[], [(lambda: gather_1.twin(2))], [(lambda: gather_1.twin(1)), (lambda: gather_2.line_a(2)), (lambda: gather_1.twin(0)), (lambda: gather_2.line_a(1))], []], forward(1))
    gather_2.line_b(0)
    gather_1.rest()

    c0 = 0.7978845608028654
    c1 = c0 * 0.044715

    def hidden_units(which):
        def body(t):
            at = rows_of(t)
            if which == 0:
                after = n.inputs[at].astype(F32) + dot(n.context[at], weight(3))
                centre = after - mean_last(after)
                scale = lax.rsqrt(mean_last(centre * centre) + epsilon)
                normal = centre * scale
                n.normal_two[at] = normal.astype(BF16)
                n.scale_two[at] = jnp.broadcast_to(scale, (CHUNK, 128))
                normed = (normal * gain_two + shift_two).astype(BF16)
                n.normed_ffn[at] = normed
                n.result[at] = after + b_down
            else:
                normed = n.normed_ffn[at]
            for i in (2 * which, 2 * which + 1):
                pre = dot(normed, weight(4 + i)) + vecs[8 + i : 9 + i]
                square = pre * pre
                half = 0.5 + 0.5 * jnp.tanh(pre * (c0 + c1 * square))
                hidden = pre * half
                slope = half + (2.0 * hidden) * (1.0 - half) * (c0 + (3.0 * c1) * square)
                cut = slice(i * WIDTH, (i + 1) * WIDTH)
                n.hidden[at, cut] = hidden.astype(BF16)
                n.grad_pre[at, cut] = slope.astype(BF16)

        return body

    per_chunk([[], [], [(lambda: gather_2.line_b(1))], []], hidden_units(0))
    per_chunk([[(lambda: gather_2.line_b(2))], [], [], []], hidden_units(1))
    local[10].wait()

    def down_grads(i):
        for m in range(2):
            some = slice(i * WIDTH + m * 256, i * WIDTH + (m + 1) * 256)
            grad = dot_tn(n.hidden[:, some], n.cotangent[...]).astype(BF16)
            part[i, m * B // 2 : (m + 1) * B // 2, :, 8 * R : 12 * R, :] = grad.reshape(
                B // 2, 2, 4 * R, WIDTH
            )

    down_grads(0)
    gather_2.twin(2)
    down_grads(1)
    gather_2.twin(0)
    gather_2.twin(1)
    down_grads(2)
    down_grads(3)
    gather_2.rest()

    def ffn(i, events):
        cut = slice(i * WIDTH, (i + 1) * WIDTH)

        def body(t):
            at = rows_of(t)
            grad = dot_nt(n.cotangent[at], weight_down(i)) * n.grad_pre[at, cut].astype(F32)
            grad = grad.astype(BF16)
            n.grad_pre[at, cut] = grad
            slots[0, i : i + 1] += column_sum(grad.astype(F32))

        per_chunk(events, body)
        for m in range(2):
            some = slice(m * 256, (m + 1) * 256)
            grad = dot_tn(n.normed_ffn[:, some], n.grad_pre[:, cut]).astype(BF16)
            part[2 * m : 2 * m + 2, :, :, (4 + i) * R : (5 + i) * R, :] = grad.reshape(
                2, B, 2, R, WIDTH
            )

    ffn(0, [[down_two.start], [], [], []])
    down_one.start()
    ffn(1, [[], [], [], []])
    up_one.start()
    ffn(2, [[], [], [], [down_one.after_core]])
    ffn(3, [[], [up_one.after_core], [], []])
    up_two.start()
    down_two.after_core()

    def norm_two_back(t):
        at = rows_of(t)
        grad = dot_nt(n.grad_pre[at, 0:WIDTH], weight(4))
        for i in range(1, 4):
            grad = grad + dot_nt(n.grad_pre[at, i * WIDTH : (i + 1) * WIDTH], weight(4 + i))
        normal = n.normal_two[at].astype(F32)
        up = n.cotangent[at].astype(F32)
        slots[0, 4:5] += column_sum(up)
        slots[0, 7:8] += column_sum(grad * normal)
        slots[0, 8:9] += column_sum(grad)
        e = grad * gain_two
        back = e - mean_last(e) - normal * mean_last(e * normal)
        after = up + n.scale_two[at][:, 0:1] * back
        n.grad_normed[at] = after
        low = after.astype(BF16)
        n.grad_attn[at] = low
        grad_context = dot_nt(low, weight(3)).astype(BF16).astype(F32)
        inverse = n.inverse[at]
        n.grad_mixed[at] = (grad_context * inverse).astype(BF16)
        turned = (grad_context * n.context[at].astype(F32)).astype(BF16)
        for g in range(GROUPS):
            n.grad_totals[at, lanes[g]] = -dot(turned[:, lanes[g]], n.ones[...]) * inverse[
                :, lanes[g]
            ]

    per_chunk([[up_two.after_core], [], [], []], norm_two_back)
    for m in range(2):
        grad = dot_tn(n.context[:, m * 256 : (m + 1) * 256], n.grad_attn[...]).astype(BF16)
        part[2 * m : 2 * m + 2, :, :, 3 * R : 4 * R, :] = grad.reshape(2, B, 2, R, WIDTH)

    def backward(g):
        state_now[g] = jnp.zeros((GROUP, GROUP), F32)
        keys_now[g] = jnp.zeros((8, GROUP), F32)

        def body(t):
            at = rows_of(t)
            seg = seg_chunk(t)
            before = flags(seg, seg_at(t, -1)).astype(BF16)
            after = flags(seg, seg_at(t, CHUNK))
            opening = flags(seg, seg_at(t, 0)).astype(BF16)
            carry = flags(seg_at(t, 0), seg_at(t, CHUNK))
            q, k, v, gm = (
                ref[at, lanes[g]] for ref in (n.query, n.key, n.value, n.grad_mixed)
            )
            totals = n.grad_totals[at, lanes[g]]
            old = state_now[g].astype(BF16)
            weighted = totals * q.astype(F32)
            gq = dot_nt(gm * before, state[g, t]) + totals * n.key_sums[at, lanes[g]]
            gk = after * (dot_nt(v, old) + keys_now[g, 0:1]) + dot(mask_t[t], weighted.astype(BF16))
            gv = after * dot(k, old)
            for i in range(PER_GROUP):
                head = heads[i]
                gm_head = gm * head
                back = dot_nt(gm_head, v).astype(BF16) * mask[t]
                gq = gq + dot(back, k * head)
                back = dot_nt(v * head, gm).astype(BF16) * mask_t[t]
                gk = gk + dot(back, q * head)
                back = dot_nt(k * head, q).astype(BF16) * mask_t[t]
                gv = gv + dot(back, gm_head)
            n.grad_query[at, lanes[g]] = (gq * jnp.minimum(q.astype(F32), 1.0)).astype(BF16)
            n.grad_key[at, lanes[g]] = (gk * jnp.minimum(k.astype(F32), 1.0)).astype(BF16)
            n.grad_value[at, lanes[g]] = gv.astype(BF16)
            opened = q * opening
            state_now[g] = state_now[g] * carry + dot_tn(opened, gm) * n.ones[...].astype(F32)
            keys_now[g, 0:1] = keys_now[g, 0:1] * carry + column_sum(
                weighted * opening.astype(F32)
            )

        return body

    def weight_grads(g):
        for i, ref in enumerate((n.grad_query, n.grad_key, n.grad_value)):
            grad = dot_tn(n.normed_attn[...], ref[:, lanes[g]]).astype(BF16)
            part[:, :, :, i * R : (i + 1) * R, lanes[g]] = grad.reshape(A, B, 2, R, GROUP)

    per_chunk([[], [down_one.second, out_all.start, up_one.second, down_two.second], [], []], backward(0), down=True)
    weight_grads(0)
    attn_one.start()
    per_chunk([[up_one.third, attn_one.after_core, up_two.second], [down_two.third, down_one.third], [], []], backward(1), down=True)
    weight_grads(1)
    attn_one.second()
    out_all.after_core()
    attn_three.start()
    up_two.third()
    attn_two.start()

    def norm_one_back(t):
        at = rows_of(t)
        grad = dot_nt(n.grad_query[at], weight(0))
        grad = grad + dot_nt(n.grad_key[at], weight(1))
        grad = grad + dot_nt(n.grad_value[at], weight(2))
        normal = n.normal_one[at].astype(F32)
        slots[0, 5:6] += column_sum(grad * normal)
        slots[0, 6:7] += column_sum(grad)
        e = grad * gain_one
        back = e - mean_last(e) - normal * mean_last(e * normal)
        n.grad_normed[at] = n.grad_normed[at] + n.scale_one[at][:, 0:1] * back

    per_chunk([[], [attn_three.after_core], [], []], norm_one_back)
    store = pltpu.make_async_copy(n.grad_normed, n.grad_inputs_far, n.sem_local.at[11])
    store.start()
    T[0]()
    attn_two.after_core()
    out_all.second()
    attn_one.third()
    T[1]()
    attn_three.second()
    attn_two.second()

    def outputs(t):
        at = rows_of(t)
        total = n.result[at]
        for i in range(4):
            total = total + dot(n.hidden[at, i * WIDTH : (i + 1) * WIDTH], weight_down(i))
        n.output[at] = total.astype(BF16)

    per_chunk([[out_all.third, T[2], up_two.after_a, down_one.after_a, up_one.after_a, attn_two.third], [attn_three.third, T[3], out_all.after_a, attn_one.after_a], [], []], outputs)
    store_more = pltpu.make_async_copy(n.output, n.output_far, n.sem_local.at[12])
    store_more.start()
    attn_three.after_a()
    down_one.finish()
    up_one.finish()
    attn_one.finish()
    out_all.finish()
    attn_two.after_a()
    up_two.finish()
    T[4]()

    total = slots[small_sum.now]
    high = total.astype(BF16)
    low = (total - high.astype(F32)).astype(BF16)
    row, lane = iota((WIDTH, 128), 0), iota((WIDTH, 128), 1)
    pick = jnp.where((row == lane + p.s * R) & (lane < R), 1.0, 0.0).astype(BF16)
    n.tiny_out[0:16] = dot(high, pick) + dot(low, pick)
    picked = jnp.zeros((16, 128), F32)
    for i in range(4):
        wanted = (row + i * WIDTH == lane + p.s * (4 * R)) & (lane < 4 * R)
        pick = jnp.where(wanted, 1.0, 0.0).astype(BF16)
        keep = iota((16, 128), 0) == i
        picked = picked + jnp.where(keep, dot(high, pick) + dot(low, pick), 0.0)
    n.tiny_out[16:17] = column_sum(picked)

    attn_three.finish()
    attn_two.finish()
    store.wait()
    store_more.wait()
    sends.finish()


PIECES = 4


def final_kernel(output, grad_inputs, done, tiny, *refs):
    outs = refs[:14]
    held_out, held_grad, held_done, held_tiny = refs[14:18]
    held = refs[18:-2]
    sem, more = refs[-2:]
    rows = output.shape[0] // PIECES
    first = [
        pltpu.make_async_copy(done, held_done, more.at[0]),
        pltpu.make_async_copy(tiny, held_tiny, more.at[1]),
    ]
    into, back = [], []
    for i in range(PIECES):
        cut = pl.ds(i * rows, rows)
        for k, (src, mid, dst) in enumerate(
            ((grad_inputs, held_grad, outs[1]), (output, held_out, outs[0]))
        ):
            into.append(pltpu.make_async_copy(src.at[cut], mid.at[cut], sem.at[0, k, i]))
            back.append(pltpu.make_async_copy(mid.at[cut], dst.at[cut], sem.at[1, k, i]))
    for copy in first + into:
        copy.start()
    for copy in first:
        copy.wait()
    R = held[0].shape[0]
    for i in range(4):
        held[i][...] = held_done[i * R : (i + 1) * R].astype(F32)
        held[4][:, i * WIDTH : (i + 1) * WIDTH] = held_done[(4 + i) * R : (5 + i) * R].astype(F32)
    held[5][...] = held_done[8 * R : 12 * R].astype(F32)
    for i in range(6):
        back.append(pltpu.make_async_copy(held[i], outs[2 + i], more.at[2 + i]))
        back[-1].start()
    for ref, row in zip(outs[8:14], (16, 4, 5, 6, 7, 8), strict=True):
        ref[...] = held_tiny[row, : ref.shape[0]]
    for one, two in zip(into, back, strict=False):
        one.wait()
        two.start()
    for copy in back:
        copy.wait()


def final(output, grad_inputs, done, tiny):
    R = done.shape[0] // 12
    vmem, far = pl.BlockSpec(memory_space=pltpu.VMEM), pl.BlockSpec(memory_space=pl.ANY)
    grads = [((R, WIDTH), F32)] * 4 + [((R, 4 * WIDTH), F32), ((4 * R, WIDTH), F32)]
    shapes = [(output.shape, BF16), (grad_inputs.shape, F32)] + grads
    shapes += [((4 * R,), F32)] + [((R,), F32)] * 5
    return pl.pallas_call(
        final_kernel,
        out_shape=tuple(jax.ShapeDtypeStruct(*shape) for shape in shapes),
        in_specs=[far] * 4,
        out_specs=(far,) * 8 + (vmem,) * 6,
        scratch_shapes=[
            pltpu.VMEM(output.shape, BF16),
            pltpu.VMEM(grad_inputs.shape, F32),
            pltpu.VMEM(done.shape, BF16),
            pltpu.VMEM(tiny.shape, F32),
        ]
        + [pltpu.VMEM(*shape) for shape in grads]
        + [pltpu.SemaphoreType.DMA((2, 2, PIECES)), pltpu.SemaphoreType.DMA((8,))],
        name="final",
    )(output, grad_inputs, done, tiny)


def layer(reps, shards, inputs, segment_ids, weights, vectors, cotangent):
    length = inputs.shape[0]
    A, B = 4, shards // 8
    R = weights[0].shape[0]
    rows = 12 * R
    bits = max(reps.bit_length() - 2, 0)
    copies, n_slots = SmallReduce.counts(reps, shards)
    sums = 5 * (2 * B + A + bits) + 2 * (3 * B - 1 + A + bits) + 1 * (3 * B - 1)
    groups = 3
    w_query, w_key, w_value, w_out, w_up, w_down = weights
    b_up, b_down, gain_attn, shift_attn, gain_ffn, shift_ffn = vectors
    far_ins = dict(
        inputs_far=inputs,
        cotangent_far=cotangent,
        w_query=w_query,
        w_key=w_key,
        w_value=w_value,
        w_out=w_out,
        w_up=w_up,
        w_down=w_down,
    )
    ins = dict(
        segment_ids=segment_ids,
        b_up=b_up,
        b_down=b_down,
        gain_attn=gain_attn,
        shift_attn=shift_attn,
        gain_ffn=gain_ffn,
        shift_ffn=shift_ffn,
    )
    far_outs = dict(
        output_far=((length, WIDTH), BF16),
        grad_inputs_far=((length, WIDTH), F32),
    )
    outs = dict(
        done=((rows, WIDTH), BF16),
        tiny_out=((24, 128), F32),
    )
    tall = (length, WIDTH)
    buffers = dict(
        inputs=(tall, BF16),
        cotangent=(tall, BF16),
        output=(tall, BF16),
        result=(tall, F32),
        full=((A, B, 2, rows, WIDTH), BF16),
        part=((A, B, 2, rows, WIDTH), BF16),
        core=((A, B, rows, WIDTH), BF16),
        line_b=((B - 1, A, rows, WIDTH), BF16),
        pair=((A, B, rows, WIDTH), BF16),
        line_a=((A - 1, rows, WIDTH), BF16),
        wide=((max(2 * bits, 1), rows if bits else 16, WIDTH), BF16),
        smalls=((A, B, 2, 8, 128), F32),
        slots=((n_slots, 16, WIDTH), F32),
        vecs=((16, WIDTH), F32),
        seg_rows=((length + 16, 128), F32),
        heads=((PER_GROUP, CHUNK, GROUP), BF16),
        ones=((GROUP, GROUP), BF16),
        mask=((length // CHUNK, CHUNK, CHUNK), BF16),
        mask_t=((length // CHUNK, CHUNK, CHUNK), BF16),
        normal_one=(tall, BF16),
        scale_one=((length, 128), F32),
        normed_attn=(tall, BF16),
        query=(tall, BF16),
        key=(tall, BF16),
        value=(tall, BF16),
        key_sums=(tall, F32),
        inverse=(tall, F32),
        context=(tall, BF16),
        state=((GROUPS, length // CHUNK, GROUP, GROUP), BF16),
        state_now=((GROUPS, GROUP, GROUP), F32),
        keys_now=((GROUPS, 8, GROUP), F32),
        normal_two=(tall, BF16),
        scale_two=((length, 128), F32),
        normed_ffn=(tall, BF16),
        hidden=((length, 4 * WIDTH), BF16),
        grad_pre=((length, 4 * WIDTH), BF16),
        grad_normed=(tall, F32),
        grad_attn=(tall, BF16),
        grad_mixed=(tall, BF16),
        grad_totals=(tall, F32),
    )
    sems = dict(
        sem_local=(13,),
        send0=(A + B,),
        recv0=(A + B,),
        send1=(groups * Gather.n_sems(shards),),
        recv1=(groups * Gather.n_sems(shards),),
        send2=(sums,),
        recv2=(sums,),
        send3=(copies,),
        recv3=(copies,),
    )
    names = [*far_ins, *ins, *far_outs, *outs, *buffers, *sems]

    def kernel(*refs):
        n = types.SimpleNamespace(**dict(zip(names, refs, strict=True)))
        n.grad_query, n.grad_key, n.grad_value = (
            n.grad_pre.at[:, pl.ds(i * WIDTH, WIDTH)] for i in range(3)
        )
        layer_kernel(reps, shards, length, n)

    vmem, far = pl.BlockSpec(memory_space=pltpu.VMEM), pl.BlockSpec(memory_space=pl.ANY)
    flops = 2 * 3 * length * WIDTH * WIDTH * 12 + 20 * length * length * WIDTH
    return pl.pallas_call(
        kernel,
        out_shape=tuple(
            jax.ShapeDtypeStruct(*spec) for spec in [*far_outs.values(), *outs.values()]
        ),
        in_specs=[far] * len(far_ins) + [vmem] * len(ins),
        out_specs=(far,) * len(far_outs) + (vmem,) * len(outs),
        scratch_shapes=[pltpu.VMEM(*spec) for spec in buffers.values()]
        + [pltpu.SemaphoreType.DMA(shape) for shape in sems.values()],
        compiler_params=pltpu.CompilerParams(
            collective_id=1, has_side_effects=True, vmem_limit_bytes=63 << 20
        ),
        cost_estimate=pl.CostEstimate(flops=flops, bytes_accessed=8 << 20, transcendentals=0),
        name="layer",
    )(*far_ins.values(), *ins.values())


def on_device(
    reps,
    shards,
    inputs,
    segment_ids,
    w_query,
    w_key,
    w_value,
    w_out,
    w_up,
    w_down,
    b_up,
    b_down,
    gain_attn,
    shift_attn,
    gain_ffn,
    shift_ffn,
    cotangent,
):
    sequences, length, width = inputs.shape
    output, grad_inputs, done, tiny = layer(
        reps,
        shards,
        inputs.reshape(sequences * length, width),
        segment_ids,
        (w_query, w_key, w_value, w_out, w_up, w_down),
        (b_up, b_down, gain_attn, shift_attn, gain_ffn, shift_ffn),
        cotangent.reshape(sequences * length, width),
    )
    output, grad_inputs, *grads = final(output, grad_inputs, done, tiny)
    return (output.reshape(inputs.shape), grad_inputs.reshape(inputs.shape), *grads)


def solution(mesh):
    reps, shards = mesh.shape["rep"], mesh.shape["shard"]
    token = P(("rep", "shard"), None, None)
    matrix, vector = P("shard", None), P("shard")
    return jax.shard_map(
        functools.partial(on_device, reps, shards),
        mesh=mesh,
        in_specs=(token, P(("rep", "shard"), None)) + (matrix,) * 6 + (vector,) * 6 + (token,),
        out_specs=(token, token) + (matrix,) * 6 + (vector,) * 6,
        check_vma=False,
    )
```

```python
import functools
import types

import jax
import jax.numpy as jnp
from jax import lax
from jax.experimental import pallas as pl
from jax.experimental.pallas import tpu as pltpu
from jax.sharding import PartitionSpec as P

WIDTH = 512
CHUNK = 256
HEAD_DIM = 64
GROUP = 256
PER_GROUP = GROUP // HEAD_DIM
GROUPS = WIDTH // GROUP

epsilon = 1e-05
MESH = pl.DeviceIdType.MESH
F32 = jnp.float32
BF16 = jnp.bfloat16


class Place:
    def __init__(self, reps, shards):
        self.reps, self.shards = reps, shards
        self.A = 4
        self.B = shards // 8
        self.r = lax.axis_index("rep")
        s = lax.axis_index("shard")
        self.s = s
        self.c = lax.rem(s, 2)
        self.b = lax.rem(s // 2, self.B)
        self.a = s // (2 * self.B)
        self.h = lax.rem(self.r, 2)

    def at(self, a=None, b=None, c=None, r=None):
        a = self.a if a is None else a
        b = self.b if b is None else b
        c = self.c if c is None else c
        r = self.r if r is None else r
        return (r, (a * self.B + b) * 2 + c)

    def near(self, k):
        high = self.a // 2
        return (1 - self.a + 4 * high, 2 - high, 3 * (1 - high))[k]

    def next_a(self, j):
        return lax.rem(self.a + j, self.A)

    def next_b(self, j):
        return lax.rem(self.b + j, self.B)

    def sibling(self):
        return self.at(c=1 - self.c)

    def twin(self, bit=1):
        return self.at(r=self.r + bit - 2 * bit * lax.rem(self.r // bit, 2))

    def bits(self):
        bit, out = 2, []
        while bit < self.reps:
            out.append(bit)
            bit *= 2
        return out

    def partners(self):
        out = [self.sibling(), self.twin()]
        out += [self.at(a=self.next_a(j)) for j in range(1, self.A)]
        out += [self.at(b=self.next_b(j)) for j in range(1, self.B)]
        return out + [self.twin(bit) for bit in self.bits()]


def greet(partners):
    barrier = pltpu.get_barrier_semaphore()
    for device in partners:
        pl.semaphore_signal(barrier, inc=1, device_id=device, device_id_type=MESH)
    pl.semaphore_wait(barrier, len(partners))


def remote(src, dst, send, recv, device):
    return pltpu.make_async_remote_copy(
        src_ref=src, dst_ref=dst, send_sem=send, recv_sem=recv, device_id=device, device_id_type=MESH
    )


def both(one, two):
    if one is None:
        return two
    return one if two is None else jnp.logical_and(one, two)


class Sends:
    def __init__(self):
        self.made = []

    @staticmethod
    def act(copy, do):
        cond, make = copy()
        if cond is None:
            do(make())
        else:
            pl.when(cond)(lambda: do(make()))

    def go(self, copy):
        self.act(copy, lambda made: made.start())
        self.made.append(copy)

    def arrived(self, copy):
        self.act(copy, lambda made: made.wait_recv())

    def finish(self):
        for copy in self.made:
            self.act(copy, lambda made: made.wait_send())
        self.made = []


class Gather:
    def __init__(self, place, full, window, send, recv, base, sends):
        self.p, self.full = place, full
        self.lo, self.rows, self.left, self.lanes = window
        self.send, self.recv, self.base, self.sends = send, recv, base, sends

    def whole(self, a, b, c):
        return self.full.at[a, b, c, pl.ds(self.lo, self.rows), pl.ds(self.left, self.lanes)]

    def half(self, a, b, c, h):
        size = self.lanes // 2
        lanes = pl.ds(pl.multiple_of(self.left + h * size, 128), size)
        return self.full.at[a, b, c, pl.ds(self.lo, self.rows), lanes]

    def copy(self, ref, k, device, other=None):
        return remote(ref, ref, self.send.at[k], self.recv.at[k if other is None else other], device)

    def go(self, make):
        self.sends.go(lambda: (None, make))

    def slot(self, kind, k=0, j=0):
        more = self.p.B - 1
        j = max(j - 1, 0)
        base = (0, 4, 4 + more, 4 + 4 * more, 7 + 4 * more, 7 + 7 * more)
        base += (8 + 7 * more, 8 + 8 * more, 11 + 8 * more)
        return self.base + base[kind] + (k * more if kind in (2, 4) else k) + j

    def own(self):
        p = self.p
        for k in (2, 1, 0):
            self.go(
                lambda k=k: self.copy(
                    self.half(p.a, p.b, p.c, p.h) if k else self.whole(p.a, p.b, p.c),
                    self.slot(0, k),
                    p.at(a=p.near(k)),
                    self.slot(0, p.a),
                )
            )
        for j in range(1, p.B):
            self.go(
                lambda j=j: self.copy(
                    self.whole(p.a, p.b, p.c), self.slot(1, 0, j), p.at(b=p.next_b(j))
                )
            )
        self.go(lambda: self.copy(self.whole(p.a, p.b, p.c), self.slot(5), p.sibling()))

    def line_a(self, k):
        p = self.p
        place = (p.near(k), p.b, p.c)
        ref = self.half(*place, p.h) if k else self.whole(*place)
        self.copy(ref, self.slot(0, p.near(k)), p.sibling()).wait_recv()

        def mine():
            return self.half(p.near(k), p.b, p.c, p.h)

        for j in range(1, p.B):
            self.go(lambda j=j: self.copy(mine(), self.slot(2, k, j), p.at(b=p.next_b(j))))
        if k:
            self.go(lambda: self.copy(mine(), self.slot(3, k), p.twin()))

    def line_b_own(self):
        p = self.p
        for j in range(1, p.B):
            b = p.next_b(p.B - j)
            self.copy(self.whole(p.a, b, p.c), self.slot(1, 0, j), p.sibling()).wait_recv()
            self.go(
                lambda j=j: self.copy(
                    self.whole(p.a, p.next_b(p.B - j), p.c), self.slot(6, 0, j), p.sibling()
                )
            )

    def line_b(self, k):
        p = self.p
        for j in range(1, p.B):
            b = p.next_b(p.B - j)
            ref = self.half(p.near(k), b, p.c, p.h)
            self.copy(ref, self.slot(2, k, j), p.sibling()).wait_recv()
            self.go(
                lambda j=j: self.copy(
                    self.half(p.near(k), p.next_b(p.B - j), p.c, p.h), self.slot(4, k, j), p.twin()
                )
            )
        self.go(
            lambda: self.copy(
                self.half(p.near(k), slice(None), p.c, p.h), self.slot(7, k), p.sibling()
            )
        )

    def twin(self, k):
        p = self.p
        for j in range(0 if k else 1, p.B):
            ref = self.half(p.near(k), p.next_b(p.B - j), p.c, 1 - p.h)
            kind = 4 if j else 3
            self.copy(ref, self.slot(kind, k, j), p.sibling()).wait_recv()
        self.go(
            lambda: self.copy(
                self.half(p.near(k), slice(None), p.c, 1 - p.h), self.slot(8, k), p.sibling()
            )
        )

    def rest(self):
        p = self.p
        other = 1 - p.c
        self.copy(self.whole(p.a, p.b, other), self.slot(5), p.sibling()).wait_recv()
        for j in range(1, p.B):
            ref = self.whole(p.a, p.next_b(p.B - j), other)
            self.copy(ref, self.slot(6, 0, j), p.sibling()).wait_recv()
        for k in range(3):
            for kind, h in ((7, p.h), (8, 1 - p.h)):
                ref = self.half(p.near(k), slice(None), other, h)
                self.copy(ref, self.slot(kind, k), p.sibling()).wait_recv()

    @staticmethod
    def n_sems(shards):
        return 14 + 8 * (shards // 8 - 1)


class SmallGather:
    def __init__(self, place, full, send, recv, sends):
        self.p, self.full, self.send, self.recv, self.sends = place, full, send, recv, sends

    def copy(self, ref, k, device):
        return remote(ref, ref, self.send.at[k], self.recv.at[k], device)

    def own(self):
        p = self.p
        for j in range(1, p.A):
            self.sends.go(
                lambda j=j: (
                    None,
                    lambda: self.copy(self.full.at[p.a, p.b, p.c], j, p.at(a=p.next_a(j))),
                )
            )

    def second(self):
        p = self.p
        for j in range(1, p.A):
            self.copy(self.full.at[p.next_a(p.A - j), p.b, p.c], j, p.sibling()).wait_recv()
        for j in range(1, p.B):
            self.sends.go(
                lambda j=j: (
                    None,
                    lambda: self.copy(self.full.at[:, p.b, p.c], p.A + j, p.at(b=p.next_b(j))),
                )
            )

    def third(self):
        p = self.p
        for j in range(1, p.B):
            self.copy(self.full.at[:, p.next_b(p.B - j), p.c], p.A + j, p.sibling()).wait_recv()
        self.sends.go(lambda: (None, lambda: self.copy(self.full.at[:, :, p.c], 0, p.sibling())))

    def last(self):
        p = self.p
        self.copy(self.full.at[:, :, 1 - p.c], 0, p.sibling()).wait_recv()


class Reduce:
    def __init__(self, place, part, bufs, window, sems, base, sends, pair_first=False, span=None, end=None):
        self.p, self.part = place, part
        self.lo, self.rows, self.at, self.lanes = window
        self.core, self.line_b, self.pair, self.line_a, self.wide, self.done = bufs
        self.send, self.recv = sems
        self.sends = sends
        self.pair_first = pair_first
        self.first, self.last = span or (0, place.A)
        self.end = end or self
        self.base = base

    def slot(self, kind, j=0):
        B = self.p.B
        twins = B if self.pair_first else 1
        base = (0, B - 1, 2 * B - 1, 2 * B - 2 + twins, 2 * B + 2 + twins, 2 * B + 3 + twins)
        return self.base + base[kind] + j

    def n_sems(self):
        last = self.slot(3, 1) if self.end is not self else self.slot(5, len(self.p.bits()))
        return last - self.base

    def span(self):
        return slice(self.first, self.last)

    def win(self):
        return (pl.ds(self.lo, self.rows), pl.ds(self.at, self.lanes))

    def half(self, h):
        size = self.lanes // 2
        return (
            pl.ds(self.lo, self.rows),
            pl.ds(pl.multiple_of(self.at + h * size, 128), size),
        )

    def go(self, copy, when=lambda: None):
        self.sends.go(lambda: (when(), lambda: self.copy(*copy())))

    def copy(self, src, dst, k, device):
        return remote(src, dst, self.send.at[k], self.recv.at[k], device)

    def arrived(self, ref, k):
        self.copy(ref, ref, k, self.p.sibling()).wait_recv()

    def order(self):
        return list(range(1, self.p.B)) + [0]

    def start(self):
        p = self.p
        for j in self.order():
            self.go(
                lambda j=j: (
                    self.part.at[(self.span(), p.next_b(j), 1 - p.c) + self.win()],
                    self.core.at[(self.span(), j) + self.win()],
                    self.slot(0, j),
                    p.sibling(),
                )
            )

    def after_core(self):
        p = self.p
        for j in self.order():
            mine = (self.span(), p.next_b(j), p.c) + self.win()
            got = (self.span(), j) + self.win()
            self.arrived(self.core.at[got], self.slot(0, j))
            self.part[mine] = self.part[mine] + self.core[got]
            if self.pair_first:
                self.to_pair(j)
            elif j > 0:
                self.to_b(j, self.win)

    def to_b(self, j, win):
        p = self.p
        self.go(
            lambda: (
                self.part.at[(self.span(), p.next_b(j), p.c) + win()],
                self.line_b.at[(j - 1, self.span()) + win()],
                self.slot(1, j),
                p.at(b=p.next_b(j)),
            )
        )

    def to_pair(self, j):
        p = self.p
        self.go(
            lambda: (
                self.part.at[(self.span(), p.next_b(j), p.c) + self.half(1 - p.h)],
                self.pair.at[(self.span(), j) + self.half(1 - p.h)],
                self.slot(2, j),
                p.twin(),
            )
        )

    def to_a(self):
        p, end = self.p, self.end
        partial = self.last - self.first < p.A
        for j in range(1, p.A):

            def when(j=j):
                a = p.next_a(j)
                return both(a >= self.first, a < self.last) if partial else None

            end.go(
                lambda j=j: (
                    self.part.at[(p.next_a(j), p.b, p.c) + self.half(p.h)],
                    self.line_a.at[(j - 1,) + self.half(p.h)],
                    end.slot(3, j),
                    p.at(a=p.next_a(j)),
                ),
                when,
            )

    def add_b(self, win):
        p = self.p
        mine = (self.span(), p.b, p.c) + win
        total = self.part[mine].astype(F32)
        for j in range(1, p.B):
            got = (j - 1, self.span()) + win
            self.arrived(self.line_b.at[got], self.slot(1, j))
            total = total + self.line_b[got].astype(F32)
        self.part[mine] = total.astype(BF16)

    def add_pair(self, j):
        p = self.p
        got = (self.span(), j) + self.half(p.h)
        mine = (self.span(), p.next_b(j), p.c) + self.half(p.h)
        self.arrived(self.pair.at[got], self.slot(2, j))
        self.part[mine] = self.part[mine] + self.pair[got]

    def second(self):
        p = self.p
        if self.pair_first:
            for j in self.order():
                self.add_pair(j)
                if j > 0:
                    self.to_b(j, lambda: self.half(p.h))
        else:
            self.add_b(self.win())
            self.to_pair(0)

    def third(self):
        p = self.p
        if self.pair_first:
            self.add_b(self.half(p.h))
        else:
            self.add_pair(0)
        self.to_a()

    def after_a(self):
        p = self.p
        mine = self.half(p.h)
        total = self.part[(p.a, p.b, p.c) + mine].astype(F32)
        for j in range(1, p.A):
            got = (j - 1,) + mine
            self.arrived(self.line_a.at[got], self.slot(3, j))
            total = total + self.line_a[got].astype(F32)
        for i, bit in enumerate(p.bits()):
            k = self.slot(5, i)
            self.wide[(2 * i,) + mine] = total.astype(BF16)

            def copy(i=i, k=k, bit=bit):
                here = self.half(p.h)
                return (
                    self.wide.at[(2 * i,) + here],
                    self.wide.at[(2 * i + 1,) + here],
                    k,
                    p.twin(bit),
                )

            self.go(copy)
            self.arrived(self.wide.at[(2 * i + 1,) + mine], k)
            total = self.wide[(2 * i,) + mine].astype(F32)
            total = total + self.wide[(2 * i + 1,) + mine].astype(F32)
        self.done[mine] = total.astype(BF16)
        self.go(
            lambda: (
                self.done.at[self.half(p.h)],
                self.done.at[self.half(p.h)],
                self.slot(4),
                p.twin(),
            )
        )

    def finish(self):
        p = self.p
        self.arrived(self.done.at[self.half(1 - p.h)], self.slot(4))

    def steps(self):
        return [self.start, self.after_core, self.second, self.third, self.after_a, self.finish]


class SmallReduce:
    def __init__(self, place, slots, send, recv, sends):
        self.p, self.slots, self.send, self.recv, self.sends = place, slots, send, recv, sends
        self.now, self.free, self.k = 0, 1, 0

    def copy(self, src, dst, k, device):
        return remote(self.slots.at[src], self.slots.at[dst], self.send.at[k], self.recv.at[k], device)

    def exchange(self, devices):
        self.fresh = []
        for device in devices:
            src, dst, k = self.now, self.free, self.k
            self.fresh.append((dst, k))
            self.sends.go(
                lambda src=src, dst=dst, k=k, device=device: (
                    None,
                    lambda: self.copy(src, dst, k, device()),
                )
            )
            self.free, self.k = self.free + 1, self.k + 1

    def add(self):
        total = self.slots[self.now]
        for slot, k in self.fresh:
            self.copy(slot, slot, k, self.p.sibling()).wait_recv()
            total = total + self.slots[slot]
        self.slots[self.free] = total
        self.now, self.free = self.free, self.free + 1

    def steps(self):
        p = self.p
        stages = [
            [p.sibling],
            [lambda j=j: p.at(b=p.next_b(j)) for j in range(1, p.B)],
            [p.twin],
            [lambda j=j: p.at(a=p.next_a(j)) for j in range(1, p.A)],
        ] + [[functools.partial(p.twin, bit)] for bit in p.bits()]
        out = [lambda: self.exchange(stages[0])]
        for stage in stages[1:]:
            out.append(lambda stage=stage: (self.add(), self.exchange(stage)))
        out.append(self.add)
        return out

    @staticmethod
    def counts(reps, shards):
        wide = max(reps.bit_length() - 2, 0)
        copies = 1 + (shards // 8 - 1) + 1 + 3 + wide
        return copies, 1 + copies + 4 + wide


def dot(lhs, rhs):
    return lax.dot_general(lhs, rhs, (((1,), (0,)), ((), ())), preferred_element_type=F32)


def dot_nt(lhs, rhs):
    return lax.dot_general(lhs, rhs, (((1,), (1,)), ((), ())), preferred_element_type=F32)


def dot_tn(lhs, rhs):
    return lax.dot_general(lhs, rhs, (((0,), (0,)), ((), ())), preferred_element_type=F32)


def iota(shape, axis):
    return lax.broadcasted_iota(jnp.int32, shape, axis)


def mean_last(value):
    return jnp.sum(value, axis=-1, keepdims=True) * (1.0 / value.shape[-1])


def column_sum(value):
    return jnp.sum(value, axis=0, keepdims=True)


def twice(value):
    return jnp.concatenate([value, value], axis=1)


def feature(value):
    return jnp.where(value > 0, value + 1.0, jnp.exp(jnp.minimum(value, 0.0)))


def layer_kernel(reps, shards, length, n):
    p = Place(reps, shards)
    A, B = p.A, p.B
    rows_w = n.w_query.shape[0]
    R = rows_w
    chunks = length // CHUNK
    full, part, smalls, slots, vecs = n.full, n.part, n.smalls, n.slots, n.vecs

    mine = full.at[p.a, p.b, p.c]
    pieces = [
        (ref, mine.at[pl.ds(i * R, R)])
        for i, ref in enumerate((n.w_query, n.w_key, n.w_value, n.w_out))
    ]
    pieces += [
        (n.w_up.at[:, pl.ds(i * WIDTH, WIDTH)], mine.at[pl.ds((4 + i) * R, R)]) for i in range(4)
    ]
    pieces += [(n.w_down, mine.at[pl.ds(8 * R, 4 * R)])]
    pieces += [(n.inputs_far, n.inputs), (n.cotangent_far, n.cotangent)]
    local = [
        pltpu.make_async_copy(src, dst, n.sem_local.at[i]) for i, (src, dst) in enumerate(pieces)
    ]
    for copy in local:
        copy.start()
    smalls[p.a, p.b, p.c] = jnp.zeros((8, 128), F32)
    vectors = (n.b_up, n.b_down, n.gain_attn, n.shift_attn, n.gain_ffn, n.shift_ffn)
    for i, ref in enumerate(vectors):
        size = ref.shape[0]
        smalls[p.a, p.b, p.c, i : i + 1, 0:size] = ref[...].astype(F32).reshape(1, size)
    greet(p.partners())
    for copy in local[:9]:
        copy.wait()

    sends = Sends()
    tiny = SmallGather(p, smalls, n.send0, n.recv0, sends)
    windows = ((0 * R, 3 * R, 0, 512), (3 * R, 5 * R, 0, 512), (8 * R, 4 * R, 0, 512))
    gather_0, gather_1, gather_2 = (
        Gather(p, full, window, n.send1, n.recv1, i * Gather.n_sems(shards), sends)
        for i, window in enumerate(windows)
    )
    bufs = (n.core, n.line_b, n.pair, n.line_a, n.wide, n.done)

    made = []

    def job(lo, rows, at=0, lanes=WIDTH, **more):
        base = sum(one.n_sems() for one in made)
        window = (lo * R, rows * R, at, lanes)
        made.append(Reduce(p, part, bufs, window, (n.send2, n.recv2), base, sends, **more))
        return made[-1]

    up_one = job(4, 2)
    up_two = job(6, 2, pair_first=True)
    down_one = job(8, 4, pair_first=True, span=(0, 2))
    down_two = job(8, 4, span=(2, 4), end=down_one)
    out_all = job(3, 1)
    attn_one = job(0, 3, 0, 256)
    attn_two = job(0, 1, 256, 256)
    attn_three = job(1, 2, 256, 256, pair_first=True)
    assert sum(one.n_sems() for one in made) <= n.recv2.shape[0]
    small_sum = SmallReduce(p, slots, n.send3, n.recv3, sends)
    T = small_sum.steps()

    def rows_of(t, size=CHUNK):
        return pl.ds(pl.multiple_of(t * size, size), size)

    def per_chunk(events, body, down=False, size=CHUNK):
        chunks = length // size

        def step(i, carry):
            body(chunks - 1 - i if down else i)
            for at, calls in enumerate(events):
                if calls:

                    @pl.when(i == at)
                    def _():
                        for call in calls:
                            call()

            return carry

        lax.fori_loop(0, chunks, step, 0)

    tiny.own()
    gather_0.own()
    tiny.second()
    gather_1.own()
    gather_0.line_a(1)

    seg_row = n.segment_ids[...].astype(F32)
    seg_rows = n.seg_rows
    seg_rows[0:8, :] = jnp.full((8, 128), -1.0, F32)
    seg_rows[pl.ds(8, length), :] = jnp.broadcast_to(seg_row, (128, length)).T
    seg_rows[pl.ds(8 + length, 8), :] = jnp.full((8, 128), -2.0, F32)
    heads, mask, mask_t = n.heads, n.mask, n.mask_t
    for i in range(PER_GROUP):
        heads[i] = jnp.where(iota((CHUNK, GROUP), 1) // HEAD_DIM == i, 1.0, 0.0).astype(BF16)
    same_head = (iota((GROUP, GROUP), 0) // HEAD_DIM) == (iota((GROUP, GROUP), 1) // HEAD_DIM)
    n.ones[...] = jnp.where(same_head, 1.0, 0.0).astype(BF16)
    later_row = iota((CHUNK, CHUNK), 0) >= iota((CHUNK, CHUNK), 1)
    later_col = iota((CHUNK, CHUNK), 0) <= iota((CHUNK, CHUNK), 1)
    for t in range(chunks):
        same = twice(seg_rows[pl.ds(8 + t * CHUNK, CHUNK), :]) == seg_row[
            :, t * CHUNK : (t + 1) * CHUNK
        ]
        mask[t] = jnp.where(same & later_row, 1.0, 0.0).astype(BF16)
        mask_t[t] = jnp.where(same & later_col, 1.0, 0.0).astype(BF16)

    def seg_chunk(t):
        return seg_rows[pl.ds(pl.multiple_of(8 + t * CHUNK, 8), CHUNK), :]

    def seg_at(t, row):
        return seg_rows[pl.ds(8 + t * CHUNK + row, 1), :]

    def flags(one, two):
        return twice(jnp.where(one == two, 1.0, 0.0))

    tiny.third()
    gather_0.line_a(2)
    tiny.last()
    gather_0.line_a(0)
    gather_0.line_b(1)

    local[9].wait()
    def norm_one(t):
        at = rows_of(t)
        h = n.inputs[at].astype(F32)
        centre = h - mean_last(h)
        scale = lax.rsqrt(mean_last(centre * centre) + epsilon)
        n.normal_one[at] = (centre * scale).astype(BF16)
        n.scale_one[at] = jnp.broadcast_to(scale, (CHUNK, 128))

    per_chunk([], norm_one)
    gather_0.line_b(2)
    gather_1.line_a(1)
    gather_0.twin(2)
    gather_1.line_a(0)
    gather_0.twin(1)
    gather_0.line_b(0)
    gather_1.line_b(1)
    gather_0.line_b_own()
    gather_1.line_a(2)

    blocks = smalls[...].reshape(shards * 8, 128).astype(BF16)
    lane = iota((128, WIDTH), 1)
    row = iota((128, WIDTH), 0)
    block = iota((shards, 8, WIDTH), 0)
    at_lane = iota((shards, 8, WIDTH), 2)
    spread = jnp.where(lane % R == row, 1.0, 0.0).astype(BF16)
    laid = dot(blocks, spread).reshape(shards, 8, WIDTH)
    vecs[0:8] = jnp.sum(jnp.where(at_lane // R == block, laid, 0.0), axis=0)
    spread = jnp.where(lane % (4 * R) == row, 1.0, 0.0).astype(BF16)
    laid = dot(blocks, spread).reshape(shards, 8, WIDTH)
    for i in range(4):
        picked = jnp.where((at_lane + i * WIDTH) // (4 * R) == block, laid, 0.0)
        vecs[8 + i : 9 + i] = jnp.sum(picked, axis=0)[0:1]
    b_down, gain_one, shift_one, gain_two, shift_two = (vecs[i : i + 1] for i in range(1, 6))

    gather_2.own()
    gather_0.twin(0)
    gather_0.rest()

    def weight(i):
        return full[:, :, :, i * R : (i + 1) * R, :].reshape(WIDTH, WIDTH)

    def weight_down(i):
        return full[i, :, :, 8 * R : 12 * R, :].reshape(WIDTH, WIDTH)

    lanes = [slice(g * GROUP, (g + 1) * GROUP) for g in range(GROUPS)]
    state, state_now, keys_now = n.state, n.state_now, n.keys_now
    state_now[...] = jnp.zeros(state_now.shape, F32)
    keys_now[...] = jnp.zeros(keys_now.shape, F32)
    slots[0] = jnp.zeros(slots.shape[1:], F32)

    def project(t):
        at = rows_of(t, 512)
        normed = (n.normal_one[at].astype(F32) * gain_one + shift_one).astype(BF16)
        n.normed_attn[at] = normed
        n.query[at] = feature(dot(normed, weight(0))).astype(BF16)
        n.key[at] = feature(dot(normed, weight(1))).astype(BF16)
        n.value[at] = dot(normed, weight(2)).astype(BF16)

    def forward(g):
        cut = lanes[g]

        def body(t):
            at = rows_of(t)
            q, k, v = n.query[at, cut], n.key[at, cut], n.value[at, cut]
            seg = seg_chunk(t)
            before = flags(seg, seg_at(t, -1))
            ending = flags(seg, seg_at(t, CHUNK - 1)).astype(BF16)
            carry = flags(seg_at(t, CHUNK - 1), seg_at(t, -1))
            old = state_now[g].astype(BF16)
            state[g, t] = old
            mixed = dot(q * before.astype(BF16), old)
            for i in range(PER_GROUP):
                scores = dot_nt(q * heads[i], k).astype(BF16) * mask[t]
                mixed = mixed + dot(scores, v * heads[i])
            sums = dot(mask[t], k) + before * keys_now[g, 0:1]
            n.key_sums[at, cut] = sums
            totals = dot((q.astype(F32) * sums).astype(BF16), n.ones[...])
            inverse = 1.0 / totals
            n.inverse[at, cut] = inverse
            n.context[at, cut] = (mixed * inverse).astype(BF16)
            ended = k * ending
            state_now[g] = state_now[g] * carry + dot_tn(ended, v) * n.ones[...].astype(F32)
            keys_now[g, 0:1] = keys_now[g, 0:1] * carry + column_sum(ended.astype(F32))

        return body

    per_chunk([[(lambda: gather_1.line_b(0))], []], project, size=512)
    gather_1.line_b(2)
    per_chunk([[], [], [], []], forward(0))
    per_chunk([[gather_1.line_b_own, (lambda: gather_2.line_a(1)), (lambda: gather_1.twin(0)), (lambda: gather_1.twin(1)), gather_2.line_b_own], [(lambda: gather_1.twin(2))], [], []], forward(1))
    gather_2.line_a(2)
    gather_1.rest()

    c0 = 0.7978845608028654
    c1 = c0 * 0.044715

    def norm_two(t):
        at = rows_of(t, 512)
        after = n.inputs[at].astype(F32) + dot(n.context[at], weight(3))
        centre = after - mean_last(after)
        scale = lax.rsqrt(mean_last(centre * centre) + epsilon)
        normal = centre * scale
        n.normal_two[at] = normal.astype(BF16)
        n.scale_two[at] = jnp.broadcast_to(scale, (512, 128))
        n.normed_ffn[at] = (normal * gain_two + shift_two).astype(BF16)
        n.result[at] = after + b_down

    def hidden_units(i):
        cut = slice(i * WIDTH, (i + 1) * WIDTH)
        pre = dot(n.normed_ffn[...], weight(4 + i)) + vecs[8 + i : 9 + i]
        square = pre * pre
        half = 0.5 + 0.5 * jnp.tanh(pre * (c0 + c1 * square))
        hidden = pre * half
        slope = half + (2.0 * hidden) * (1.0 - half) * (c0 + (3.0 * c1) * square)
        n.hidden[:, cut] = hidden.astype(BF16)
        n.grad_pre[:, cut] = slope.astype(BF16)

    per_chunk([[(lambda: gather_2.line_a(0))], []], norm_two, size=512)
    hidden_units(0)
    gather_2.line_b(1)
    hidden_units(1)
    gather_2.line_b(2)
    hidden_units(2)
    gather_2.line_b(0)
    hidden_units(3)
    local[10].wait()

    def down_grads(i):
        for m in range(2):
            some = slice(i * WIDTH + m * 256, i * WIDTH + (m + 1) * 256)
            grad = dot_tn(n.hidden[:, some], n.cotangent[...]).astype(BF16)
            part[i, m * B // 2 : (m + 1) * B // 2, :, 8 * R : 12 * R, :] = grad.reshape(
                B // 2, 2, 4 * R, WIDTH
            )

    down_grads(0)
    down_grads(1)
    gather_2.twin(1)
    gather_2.twin(2)
    gather_2.twin(0)
    down_grads(2)
    down_grads(3)
    down_one.start()
    gather_2.rest()

    def ffn(i):
        cut = slice(i * WIDTH, (i + 1) * WIDTH)
        grad = dot_nt(n.cotangent[...], weight_down(i)) * n.grad_pre[:, cut].astype(F32)
        grad = grad.astype(BF16)
        n.grad_pre[:, cut] = grad
        slots[0, i : i + 1] += column_sum(grad.astype(F32))

    def up_grads(i):
        cut = slice(i * WIDTH, (i + 1) * WIDTH)
        for m in range(2):
            some = slice(m * 256, (m + 1) * 256)
            grad = dot_tn(n.normed_ffn[:, some], n.grad_pre[:, cut]).astype(BF16)
            part[2 * m : 2 * m + 2, :, :, (4 + i) * R : (5 + i) * R, :] = grad.reshape(
                2, B, 2, R, WIDTH
            )

    ffn(0)
    up_grads(0)
    down_two.start()
    ffn(1)
    up_grads(1)
    down_one.after_core()
    up_one.start()
    down_two.after_core()
    ffn(2)
    up_grads(2)
    ffn(3)
    up_grads(3)
    up_two.start()

    def norm_two_back(t):
        at = rows_of(t, 512)
        grad = dot_nt(n.grad_pre[at, 0:WIDTH], weight(4))
        for i in range(1, 4):
            grad = grad + dot_nt(n.grad_pre[at, i * WIDTH : (i + 1) * WIDTH], weight(4 + i))
        normal = n.normal_two[at].astype(F32)
        up = n.cotangent[at].astype(F32)
        slots[0, 4:5] += column_sum(up)
        slots[0, 7:8] += column_sum(grad * normal)
        slots[0, 8:9] += column_sum(grad)
        e = grad * gain_two
        back = e - mean_last(e) - normal * mean_last(e * normal)
        after = up + n.scale_two[at][:, 0:1] * back
        n.grad_normed[at] = after
        low = after.astype(BF16)
        n.grad_attn[at] = low
        grad_context = dot_nt(low, weight(3)).astype(BF16).astype(F32)
        inverse = n.inverse[at]
        n.grad_mixed[at] = (grad_context * inverse).astype(BF16)
        turned = (grad_context * n.context[at].astype(F32)).astype(BF16)
        for g in range(GROUPS):
            n.grad_totals[at, lanes[g]] = -dot(turned[:, lanes[g]], n.ones[...]) * inverse[
                :, lanes[g]
            ]

    per_chunk([[up_one.after_core, up_two.after_core], []], norm_two_back, size=512)
    for m in range(2):
        grad = dot_tn(n.context[:, m * 256 : (m + 1) * 256], n.grad_attn[...]).astype(BF16)
        part[2 * m : 2 * m + 2, :, :, 3 * R : 4 * R, :] = grad.reshape(2, B, 2, R, WIDTH)
    down_one.second()

    def backward(g):
        state_now[g] = jnp.zeros((GROUP, GROUP), F32)
        keys_now[g] = jnp.zeros((8, GROUP), F32)

        def body(t):
            at = rows_of(t)
            seg = seg_chunk(t)
            before = flags(seg, seg_at(t, -1)).astype(BF16)
            after = flags(seg, seg_at(t, CHUNK))
            opening = flags(seg, seg_at(t, 0)).astype(BF16)
            carry = flags(seg_at(t, 0), seg_at(t, CHUNK))
            q, k, v, gm = (
                ref[at, lanes[g]] for ref in (n.query, n.key, n.value, n.grad_mixed)
            )
            totals = n.grad_totals[at, lanes[g]]
            old = state_now[g].astype(BF16)
            weighted = totals * q.astype(F32)
            gq = dot_nt(gm * before, state[g, t]) + totals * n.key_sums[at, lanes[g]]
            gk = after * (dot_nt(v, old) + keys_now[g, 0:1]) + dot(mask_t[t], weighted.astype(BF16))
            gv = after * dot(k, old)
            for i in range(PER_GROUP):
                head = heads[i]
                gm_head = gm * head
                back = dot_nt(gm_head, v).astype(BF16) * mask[t]
                gq = gq + dot(back, k * head)
                back = dot_nt(v * head, gm).astype(BF16) * mask_t[t]
                gk = gk + dot(back, q * head)
                back = dot_nt(k * head, q).astype(BF16) * mask_t[t]
                gv = gv + dot(back, gm_head)
            n.grad_query[at, lanes[g]] = (gq * jnp.minimum(q.astype(F32), 1.0)).astype(BF16)
            n.grad_key[at, lanes[g]] = (gk * jnp.minimum(k.astype(F32), 1.0)).astype(BF16)
            n.grad_value[at, lanes[g]] = gv.astype(BF16)
            opened = q * opening
            state_now[g] = state_now[g] * carry + dot_tn(opened, gm) * n.ones[...].astype(F32)
            keys_now[g, 0:1] = keys_now[g, 0:1] * carry + column_sum(
                weighted * opening.astype(F32)
            )

        return body

    def weight_grads(g):
        for i, ref in enumerate((n.grad_query, n.grad_key, n.grad_value)):
            grad = dot_tn(n.normed_attn[...], ref[:, lanes[g]]).astype(BF16)
            part[:, :, :, i * R : (i + 1) * R, lanes[g]] = grad.reshape(A, B, 2, R, GROUP)

    per_chunk([[down_two.second, out_all.start], [], [], []], backward(0), down=True)
    out_all.after_core()
    weight_grads(0)
    attn_one.start()
    per_chunk([[down_one.third, attn_one.after_core, up_one.second, down_two.third], [], [out_all.second], []], backward(1), down=True)
    up_two.second()
    weight_grads(1)
    up_one.third()
    attn_three.start()
    attn_one.second()
    attn_two.start()

    def norm_one_back(t):
        at = rows_of(t, 512)
        grad = dot_nt(n.grad_query[at], weight(0))
        grad = grad + dot_nt(n.grad_key[at], weight(1))
        grad = grad + dot_nt(n.grad_value[at], weight(2))
        normal = n.normal_one[at].astype(F32)
        slots[0, 5:6] += column_sum(grad * normal)
        slots[0, 6:7] += column_sum(grad)
        e = grad * gain_one
        back = e - mean_last(e) - normal * mean_last(e * normal)
        n.grad_normed[at] = n.grad_normed[at] + n.scale_one[at][:, 0:1] * back

    per_chunk([[attn_two.after_core, attn_three.after_core, up_two.third], []], norm_one_back, size=512)
    store = pltpu.make_async_copy(n.grad_normed, n.grad_inputs_far, n.sem_local.at[11])
    store.start()
    T[0]()
    attn_one.third()
    T[1]()
    attn_two.second()
    down_one.after_a()
    attn_three.second()
    out_all.third()

    def outputs(t):
        at = rows_of(t, 512)
        total = n.result[at]
        for i in range(4):
            total = total + dot(n.hidden[at, i * WIDTH : (i + 1) * WIDTH], weight_down(i))
        n.output[at] = total.astype(BF16)

    per_chunk([[T[2], attn_two.third, attn_three.third, T[3], up_two.after_a, up_one.after_a, attn_one.after_a, down_one.finish, attn_two.after_a, up_one.finish, out_all.after_a, attn_three.after_a], []], outputs, size=512)
    store_more = pltpu.make_async_copy(n.output, n.output_far, n.sem_local.at[12])
    store_more.start()
    attn_one.finish()
    attn_two.finish()
    out_all.finish()
    T[4]()

    total = slots[small_sum.now]
    high = total.astype(BF16)
    low = (total - high.astype(F32)).astype(BF16)
    row, lane = iota((WIDTH, 128), 0), iota((WIDTH, 128), 1)
    pick = jnp.where((row == lane + p.s * R) & (lane < R), 1.0, 0.0).astype(BF16)
    n.tiny_out[0:16] = dot(high, pick) + dot(low, pick)
    picked = jnp.zeros((16, 128), F32)
    for i in range(4):
        wanted = (row + i * WIDTH == lane + p.s * (4 * R)) & (lane < 4 * R)
        pick = jnp.where(wanted, 1.0, 0.0).astype(BF16)
        keep = iota((16, 128), 0) == i
        picked = picked + jnp.where(keep, dot(high, pick) + dot(low, pick), 0.0)
    n.tiny_out[16:17] = column_sum(picked)

    up_two.finish()
    attn_three.finish()
    store.wait()
    store_more.wait()
    sends.finish()


PIECES = 4


def final_kernel(output, grad_inputs, done, tiny, *refs):
    outs = refs[:14]
    held_out, held_grad, held_done, held_tiny = refs[14:18]
    held = refs[18:-2]
    sem, more = refs[-2:]
    rows = output.shape[0] // PIECES
    first = [
        pltpu.make_async_copy(done, held_done, more.at[0]),
        pltpu.make_async_copy(tiny, held_tiny, more.at[1]),
    ]
    into, back = [], []
    for i in range(PIECES):
        cut = pl.ds(i * rows, rows)
        for k, (src, mid, dst) in enumerate(
            ((grad_inputs, held_grad, outs[1]), (output, held_out, outs[0]))
        ):
            into.append(pltpu.make_async_copy(src.at[cut], mid.at[cut], sem.at[0, k, i]))
            back.append(pltpu.make_async_copy(mid.at[cut], dst.at[cut], sem.at[1, k, i]))
    for copy in first + into:
        copy.start()
    for copy in first:
        copy.wait()
    R = held[0].shape[0]
    for i in range(4):
        held[i][...] = held_done[i * R : (i + 1) * R].astype(F32)
        held[4][:, i * WIDTH : (i + 1) * WIDTH] = held_done[(4 + i) * R : (5 + i) * R].astype(F32)
    held[5][...] = held_done[8 * R : 12 * R].astype(F32)
    for i in range(6):
        back.append(pltpu.make_async_copy(held[i], outs[2 + i], more.at[2 + i]))
        back[-1].start()
    for ref, row in zip(outs[8:14], (16, 4, 5, 6, 7, 8), strict=True):
        ref[...] = held_tiny[row, : ref.shape[0]]
    for one, two in zip(into, back, strict=False):
        one.wait()
        two.start()
    for copy in back:
        copy.wait()


def final(output, grad_inputs, done, tiny):
    R = done.shape[0] // 12
    vmem, far = pl.BlockSpec(memory_space=pltpu.VMEM), pl.BlockSpec(memory_space=pl.ANY)
    grads = [((R, WIDTH), F32)] * 4 + [((R, 4 * WIDTH), F32), ((4 * R, WIDTH), F32)]
    shapes = [(output.shape, BF16), (grad_inputs.shape, F32)] + grads
    shapes += [((4 * R,), F32)] + [((R,), F32)] * 5
    return pl.pallas_call(
        final_kernel,
        out_shape=tuple(jax.ShapeDtypeStruct(*shape) for shape in shapes),
        in_specs=[far] * 4,
        out_specs=(far,) * 8 + (vmem,) * 6,
        scratch_shapes=[
            pltpu.VMEM(output.shape, BF16),
            pltpu.VMEM(grad_inputs.shape, F32),
            pltpu.VMEM(done.shape, BF16),
            pltpu.VMEM(tiny.shape, F32),
        ]
        + [pltpu.VMEM(*shape) for shape in grads]
        + [pltpu.SemaphoreType.DMA((2, 2, PIECES)), pltpu.SemaphoreType.DMA((8,))],
        name="final",
    )(output, grad_inputs, done, tiny)


def layer(reps, shards, inputs, segment_ids, weights, vectors, cotangent):
    length = inputs.shape[0]
    A, B = 4, shards // 8
    R = weights[0].shape[0]
    rows = 12 * R
    bits = max(reps.bit_length() - 2, 0)
    copies, n_slots = SmallReduce.counts(reps, shards)
    sums = 5 * (2 * B + A + bits) + 3 * (3 * B - 1 + A + bits) + 1 * (3 * B - 1)
    groups = 3
    w_query, w_key, w_value, w_out, w_up, w_down = weights
    b_up, b_down, gain_attn, shift_attn, gain_ffn, shift_ffn = vectors
    far_ins = dict(
        inputs_far=inputs,
        cotangent_far=cotangent,
        w_query=w_query,
        w_key=w_key,
        w_value=w_value,
        w_out=w_out,
        w_up=w_up,
        w_down=w_down,
    )
    ins = dict(
        segment_ids=segment_ids,
        b_up=b_up,
        b_down=b_down,
        gain_attn=gain_attn,
        shift_attn=shift_attn,
        gain_ffn=gain_ffn,
        shift_ffn=shift_ffn,
    )
    far_outs = dict(
        output_far=((length, WIDTH), BF16),
        grad_inputs_far=((length, WIDTH), F32),
    )
    outs = dict(
        done=((rows, WIDTH), BF16),
        tiny_out=((24, 128), F32),
    )
    tall = (length, WIDTH)
    buffers = dict(
        inputs=(tall, BF16),
        cotangent=(tall, BF16),
        result=(tall, F32),
        full=((A, B, 2, rows, WIDTH), BF16),
        part=((A, B, 2, rows, WIDTH), BF16),
        core=((A, B, rows, WIDTH), BF16),
        line_b=((B - 1, A, rows, WIDTH), BF16),
        pair=((A, B, rows, WIDTH), BF16),
        line_a=((A - 1, rows, WIDTH), BF16),
        wide=((max(2 * bits, 1), rows if bits else 16, WIDTH), BF16),
        smalls=((A, B, 2, 8, 128), F32),
        slots=((n_slots, 16, WIDTH), F32),
        vecs=((16, WIDTH), F32),
        seg_rows=((length + 16, 128), F32),
        heads=((PER_GROUP, CHUNK, GROUP), BF16),
        ones=((GROUP, GROUP), BF16),
        mask=((length // CHUNK, CHUNK, CHUNK), BF16),
        mask_t=((length // CHUNK, CHUNK, CHUNK), BF16),
        normal_one=(tall, BF16),
        scale_one=((length, 128), F32),
        normed_attn=(tall, BF16),
        query=(tall, BF16),
        key=(tall, BF16),
        value=(tall, BF16),
        key_sums=(tall, F32),
        inverse=(tall, F32),
        context=(tall, BF16),
        state=((GROUPS, length // CHUNK, GROUP, GROUP), BF16),
        state_now=((GROUPS, GROUP, GROUP), F32),
        keys_now=((GROUPS, 8, GROUP), F32),
        normal_two=(tall, BF16),
        scale_two=((length, 128), F32),
        normed_ffn=(tall, BF16),
        hidden=((length, 4 * WIDTH), BF16),
        grad_pre=((length, 4 * WIDTH), BF16),
        grad_normed=(tall, F32),
        grad_mixed=(tall, BF16),
        grad_totals=(tall, F32),
    )
    sems = dict(
        sem_local=(13,),
        send0=(A + B,),
        recv0=(A + B,),
        send1=(groups * Gather.n_sems(shards),),
        recv1=(groups * Gather.n_sems(shards),),
        send2=(sums,),
        recv2=(sums,),
        send3=(copies,),
        recv3=(copies,),
    )
    names = [*far_ins, *ins, *far_outs, *outs, *buffers, *sems]

    def kernel(*refs):
        n = types.SimpleNamespace(**dict(zip(names, refs, strict=True)))
        n.output, n.grad_attn = n.inputs, n.normed_ffn
        n.grad_query, n.grad_key, n.grad_value = (
            n.grad_pre.at[:, pl.ds(i * WIDTH, WIDTH)] for i in range(3)
        )
        layer_kernel(reps, shards, length, n)

    vmem, far = pl.BlockSpec(memory_space=pltpu.VMEM), pl.BlockSpec(memory_space=pl.ANY)
    flops = 2 * 3 * length * WIDTH * WIDTH * 12 + 20 * length * length * WIDTH
    return pl.pallas_call(
        kernel,
        out_shape=tuple(
            jax.ShapeDtypeStruct(*spec) for spec in [*far_outs.values(), *outs.values()]
        ),
        in_specs=[far] * len(far_ins) + [vmem] * len(ins),
        out_specs=(far,) * len(far_outs) + (vmem,) * len(outs),
        scratch_shapes=[pltpu.VMEM(*spec) for spec in buffers.values()]
        + [pltpu.SemaphoreType.DMA(shape) for shape in sems.values()],
        compiler_params=pltpu.CompilerParams(
            collective_id=1, has_side_effects=True, vmem_limit_bytes=63 << 20
        ),
        cost_estimate=pl.CostEstimate(flops=flops, bytes_accessed=8 << 20, transcendentals=0),
        name="layer",
    )(*far_ins.values(), *ins.values())


def on_device(
    reps,
    shards,
    inputs,
    segment_ids,
    w_query,
    w_key,
    w_value,
    w_out,
    w_up,
    w_down,
    b_up,
    b_down,
    gain_attn,
    shift_attn,
    gain_ffn,
    shift_ffn,
    cotangent,
):
    sequences, length, width = inputs.shape
    output, grad_inputs, done, tiny = layer(
        reps,
        shards,
        inputs.reshape(sequences * length, width),
        segment_ids,
        (w_query, w_key, w_value, w_out, w_up, w_down),
        (b_up, b_down, gain_attn, shift_attn, gain_ffn, shift_ffn),
        cotangent.reshape(sequences * length, width),
    )
    output, grad_inputs, *grads = final(output, grad_inputs, done, tiny)
    return (output.reshape(inputs.shape), grad_inputs.reshape(inputs.shape), *grads)


def solution(mesh):
    reps, shards = mesh.shape["rep"], mesh.shape["shard"]
    token = P(("rep", "shard"), None, None)
    matrix, vector = P("shard", None), P("shard")
    return jax.shard_map(
        functools.partial(on_device, reps, shards),
        mesh=mesh,
        in_specs=(token, P(("rep", "shard"), None)) + (matrix,) * 6 + (vector,) * 6 + (token,),
        out_specs=(token, token) + (matrix,) * 6 + (vector,) * 6,
        check_vma=False,
    )
```

```python
import functools
import types

import jax
import jax.numpy as jnp
from jax import lax
from jax.experimental import pallas as pl
from jax.experimental.pallas import tpu as pltpu
from jax.sharding import PartitionSpec as P

WIDTH = 512
CHUNK = 256
HEAD_DIM = 64
GROUP = 256
PER_GROUP = GROUP // HEAD_DIM
GROUPS = WIDTH // GROUP

epsilon = 1e-05
MESH = pl.DeviceIdType.MESH
F32 = jnp.float32
BF16 = jnp.bfloat16


class Place:
    def __init__(self, reps, shards):
        self.reps, self.shards = reps, shards
        self.A = 4
        self.B = shards // 8
        self.r = lax.axis_index("rep")
        s = lax.axis_index("shard")
        self.s = s
        self.c = lax.rem(s, 2)
        self.b = lax.rem(s // 2, self.B)
        self.a = s // (2 * self.B)
        self.h = lax.rem(self.r, 2)

    def at(self, a=None, b=None, c=None, r=None):
        a = self.a if a is None else a
        b = self.b if b is None else b
        c = self.c if c is None else c
        r = self.r if r is None else r
        return (r, (a * self.B + b) * 2 + c)

    def near(self, k):
        high = self.a // 2
        return (1 - self.a + 4 * high, 2 - high, 3 * (1 - high))[k]

    def next_a(self, j):
        return lax.rem(self.a + j, self.A)

    def next_b(self, j):
        return lax.rem(self.b + j, self.B)

    def sibling(self):
        return self.at(c=1 - self.c)

    def twin(self, bit=1):
        return self.at(r=self.r + bit - 2 * bit * lax.rem(self.r // bit, 2))

    def bits(self):
        bit, out = 2, []
        while bit < self.reps:
            out.append(bit)
            bit *= 2
        return out

    def partners(self):
        out = [self.sibling(), self.twin()]
        out += [self.at(a=self.next_a(j)) for j in range(1, self.A)]
        out += [self.at(b=self.next_b(j)) for j in range(1, self.B)]
        return out + [self.twin(bit) for bit in self.bits()]


def greet(partners):
    barrier = pltpu.get_barrier_semaphore()
    for device in partners:
        pl.semaphore_signal(barrier, inc=1, device_id=device, device_id_type=MESH)
    pl.semaphore_wait(barrier, len(partners))


def remote(src, dst, send, recv, device):
    return pltpu.make_async_remote_copy(
        src_ref=src, dst_ref=dst, send_sem=send, recv_sem=recv, device_id=device, device_id_type=MESH
    )


def both(one, two):
    if one is None:
        return two
    return one if two is None else jnp.logical_and(one, two)


class Sends:
    def __init__(self):
        self.made = []

    @staticmethod
    def act(copy, do):
        cond, make = copy()
        if cond is None:
            do(make())
        else:
            pl.when(cond)(lambda: do(make()))

    def go(self, copy):
        self.act(copy, lambda made: made.start())
        self.made.append(copy)

    def arrived(self, copy):
        self.act(copy, lambda made: made.wait_recv())

    def finish(self):
        for copy in self.made:
            self.act(copy, lambda made: made.wait_send())
        self.made = []


class Gather:
    def __init__(self, place, full, window, send, recv, base, sends):
        self.p, self.full = place, full
        self.lo, self.rows, self.left, self.lanes = window
        self.send, self.recv, self.base, self.sends = send, recv, base, sends

    def whole(self, a, b, c):
        return self.full.at[a, b, c, pl.ds(self.lo, self.rows), pl.ds(self.left, self.lanes)]

    def half(self, a, b, c, h):
        size = self.lanes // 2
        lanes = pl.ds(pl.multiple_of(self.left + h * size, 128), size)
        return self.full.at[a, b, c, pl.ds(self.lo, self.rows), lanes]

    def copy(self, ref, k, device, other=None):
        return remote(ref, ref, self.send.at[k], self.recv.at[k if other is None else other], device)

    def go(self, make):
        self.sends.go(lambda: (None, make))

    def slot(self, kind, k=0, j=0):
        more = self.p.B - 1
        j = max(j - 1, 0)
        base = (0, 4, 4 + more, 4 + 4 * more, 7 + 4 * more, 7 + 7 * more)
        base += (8 + 7 * more, 8 + 8 * more, 11 + 8 * more)
        return self.base + base[kind] + (k * more if kind in (2, 4) else k) + j

    def own(self):
        p = self.p
        for k in (2, 1, 0):
            self.go(
                lambda k=k: self.copy(
                    self.half(p.a, p.b, p.c, p.h) if k else self.whole(p.a, p.b, p.c),
                    self.slot(0, k),
                    p.at(a=p.near(k)),
                    self.slot(0, p.a),
                )
            )
        for j in range(1, p.B):
            self.go(
                lambda j=j: self.copy(
                    self.whole(p.a, p.b, p.c), self.slot(1, 0, j), p.at(b=p.next_b(j))
                )
            )
        self.go(lambda: self.copy(self.whole(p.a, p.b, p.c), self.slot(5), p.sibling()))

    def line_a(self, k):
        p = self.p
        place = (p.near(k), p.b, p.c)
        ref = self.half(*place, p.h) if k else self.whole(*place)
        self.copy(ref, self.slot(0, p.near(k)), p.sibling()).wait_recv()

        def mine():
            return self.half(p.near(k), p.b, p.c, p.h)

        for j in range(1, p.B):
            self.go(lambda j=j: self.copy(mine(), self.slot(2, k, j), p.at(b=p.next_b(j))))
        if k:
            self.go(lambda: self.copy(mine(), self.slot(3, k), p.twin()))

    def line_b_own(self):
        p = self.p
        for j in range(1, p.B):
            b = p.next_b(p.B - j)
            self.copy(self.whole(p.a, b, p.c), self.slot(1, 0, j), p.sibling()).wait_recv()
            self.go(
                lambda j=j: self.copy(
                    self.whole(p.a, p.next_b(p.B - j), p.c), self.slot(6, 0, j), p.sibling()
                )
            )

    def line_b(self, k):
        p = self.p
        for j in range(1, p.B):
            b = p.next_b(p.B - j)
            ref = self.half(p.near(k), b, p.c, p.h)
            self.copy(ref, self.slot(2, k, j), p.sibling()).wait_recv()
            self.go(
                lambda j=j: self.copy(
                    self.half(p.near(k), p.next_b(p.B - j), p.c, p.h), self.slot(4, k, j), p.twin()
                )
            )
        self.go(
            lambda: self.copy(
                self.half(p.near(k), slice(None), p.c, p.h), self.slot(7, k), p.sibling()
            )
        )

    def twin(self, k):
        p = self.p
        for j in range(0 if k else 1, p.B):
            ref = self.half(p.near(k), p.next_b(p.B - j), p.c, 1 - p.h)
            kind = 4 if j else 3
            self.copy(ref, self.slot(kind, k, j), p.sibling()).wait_recv()
        self.go(
            lambda: self.copy(
                self.half(p.near(k), slice(None), p.c, 1 - p.h), self.slot(8, k), p.sibling()
            )
        )

    def rest(self):
        p = self.p
        other = 1 - p.c
        self.copy(self.whole(p.a, p.b, other), self.slot(5), p.sibling()).wait_recv()
        for j in range(1, p.B):
            ref = self.whole(p.a, p.next_b(p.B - j), other)
            self.copy(ref, self.slot(6, 0, j), p.sibling()).wait_recv()
        for k in range(3):
            for kind, h in ((7, p.h), (8, 1 - p.h)):
                ref = self.half(p.near(k), slice(None), other, h)
                self.copy(ref, self.slot(kind, k), p.sibling()).wait_recv()

    @staticmethod
    def n_sems(shards):
        return 14 + 8 * (shards // 8 - 1)


class SmallGather:
    def __init__(self, place, full, send, recv, sends):
        self.p, self.full, self.send, self.recv, self.sends = place, full, send, recv, sends

    def copy(self, ref, k, device):
        return remote(ref, ref, self.send.at[k], self.recv.at[k], device)

    def own(self):
        p = self.p
        for j in range(1, p.A):
            self.sends.go(
                lambda j=j: (
                    None,
                    lambda: self.copy(self.full.at[p.a, p.b, p.c], j, p.at(a=p.next_a(j))),
                )
            )

    def second(self):
        p = self.p
        for j in range(1, p.A):
            self.copy(self.full.at[p.next_a(p.A - j), p.b, p.c], j, p.sibling()).wait_recv()
        for j in range(1, p.B):
            self.sends.go(
                lambda j=j: (
                    None,
                    lambda: self.copy(self.full.at[:, p.b, p.c], p.A + j, p.at(b=p.next_b(j))),
                )
            )

    def third(self):
        p = self.p
        for j in range(1, p.B):
            self.copy(self.full.at[:, p.next_b(p.B - j), p.c], p.A + j, p.sibling()).wait_recv()
        self.sends.go(lambda: (None, lambda: self.copy(self.full.at[:, :, p.c], 0, p.sibling())))

    def last(self):
        p = self.p
        self.copy(self.full.at[:, :, 1 - p.c], 0, p.sibling()).wait_recv()


class Reduce:
    def __init__(self, place, part, bufs, window, sems, base, sends, pair_first=False, span=None, end=None):
        self.p, self.part = place, part
        self.lo, self.rows, self.at, self.lanes = window
        self.core, self.line_b, self.pair, self.line_a, self.wide, self.done = bufs
        self.send, self.recv = sems
        self.sends = sends
        self.pair_first = pair_first
        self.first, self.last = span or (0, place.A)
        self.end = end or self
        self.base = base

    def slot(self, kind, j=0):
        B = self.p.B
        twins = B if self.pair_first else 1
        base = (0, B - 1, 2 * B - 1, 2 * B - 2 + twins, 2 * B + 2 + twins, 2 * B + 3 + twins)
        return self.base + base[kind] + j

    def n_sems(self):
        last = self.slot(3, 1) if self.end is not self else self.slot(5, len(self.p.bits()))
        return last - self.base

    def span(self):
        return slice(self.first, self.last)

    def win(self):
        return (pl.ds(self.lo, self.rows), pl.ds(self.at, self.lanes))

    def half(self, h):
        size = self.lanes // 2
        return (
            pl.ds(self.lo, self.rows),
            pl.ds(pl.multiple_of(self.at + h * size, 128), size),
        )

    def go(self, copy, when=lambda: None):
        self.sends.go(lambda: (when(), lambda: self.copy(*copy())))

    def copy(self, src, dst, k, device):
        return remote(src, dst, self.send.at[k], self.recv.at[k], device)

    def arrived(self, ref, k):
        self.copy(ref, ref, k, self.p.sibling()).wait_recv()

    def order(self):
        return list(range(1, self.p.B)) + [0]

    def start(self):
        p = self.p
        for j in self.order():
            self.go(
                lambda j=j: (
                    self.part.at[(self.span(), p.next_b(j), 1 - p.c) + self.win()],
                    self.core.at[(self.span(), j) + self.win()],
                    self.slot(0, j),
                    p.sibling(),
                )
            )

    def after_core(self):
        p = self.p
        for j in self.order():
            mine = (self.span(), p.next_b(j), p.c) + self.win()
            got = (self.span(), j) + self.win()
            self.arrived(self.core.at[got], self.slot(0, j))
            self.part[mine] = self.part[mine] + self.core[got]
            if self.pair_first:
                self.to_pair(j)
            elif j > 0:
                self.to_b(j, self.win)

    def to_b(self, j, win):
        p = self.p
        self.go(
            lambda: (
                self.part.at[(self.span(), p.next_b(j), p.c) + win()],
                self.line_b.at[(j - 1, self.span()) + win()],
                self.slot(1, j),
                p.at(b=p.next_b(j)),
            )
        )

    def to_pair(self, j):
        p = self.p
        self.go(
            lambda: (
                self.part.at[(self.span(), p.next_b(j), p.c) + self.half(1 - p.h)],
                self.pair.at[(self.span(), j) + self.half(1 - p.h)],
                self.slot(2, j),
                p.twin(),
            )
        )

    def to_a(self):
        p, end = self.p, self.end
        partial = self.last - self.first < p.A
        for j in range(1, p.A):

            def when(j=j):
                a = p.next_a(j)
                return both(a >= self.first, a < self.last) if partial else None

            end.go(
                lambda j=j: (
                    self.part.at[(p.next_a(j), p.b, p.c) + self.half(p.h)],
                    self.line_a.at[(j - 1,) + self.half(p.h)],
                    end.slot(3, j),
                    p.at(a=p.next_a(j)),
                ),
                when,
            )

    def add_b(self, win):
        p = self.p
        mine = (self.span(), p.b, p.c) + win
        total = self.part[mine].astype(F32)
        for j in range(1, p.B):
            got = (j - 1, self.span()) + win
            self.arrived(self.line_b.at[got], self.slot(1, j))
            total = total + self.line_b[got].astype(F32)
        self.part[mine] = total.astype(BF16)

    def add_pair(self, j):
        p = self.p
        got = (self.span(), j) + self.half(p.h)
        mine = (self.span(), p.next_b(j), p.c) + self.half(p.h)
        self.arrived(self.pair.at[got], self.slot(2, j))
        self.part[mine] = self.part[mine] + self.pair[got]

    def second(self):
        p = self.p
        if self.pair_first:
            for j in self.order():
                self.add_pair(j)
                if j > 0:
                    self.to_b(j, lambda: self.half(p.h))
        else:
            self.add_b(self.win())
            self.to_pair(0)

    def third(self):
        p = self.p
        if self.pair_first:
            self.add_b(self.half(p.h))
        else:
            self.add_pair(0)
        self.to_a()

    def after_a(self):
        p = self.p
        mine = self.half(p.h)
        total = self.part[(p.a, p.b, p.c) + mine].astype(F32)
        for j in range(1, p.A):
            got = (j - 1,) + mine
            self.arrived(self.line_a.at[got], self.slot(3, j))
            total = total + self.line_a[got].astype(F32)
        for i, bit in enumerate(p.bits()):
            k = self.slot(5, i)
            self.wide[(2 * i,) + mine] = total.astype(BF16)

            def copy(i=i, k=k, bit=bit):
                here = self.half(p.h)
                return (
                    self.wide.at[(2 * i,) + here],
                    self.wide.at[(2 * i + 1,) + here],
                    k,
                    p.twin(bit),
                )

            self.go(copy)
            self.arrived(self.wide.at[(2 * i + 1,) + mine], k)
            total = self.wide[(2 * i,) + mine].astype(F32)
            total = total + self.wide[(2 * i + 1,) + mine].astype(F32)
        self.done[mine] = total.astype(BF16)
        self.go(
            lambda: (
                self.done.at[self.half(p.h)],
                self.done.at[self.half(p.h)],
                self.slot(4),
                p.twin(),
            )
        )

    def finish(self):
        p = self.p
        self.arrived(self.done.at[self.half(1 - p.h)], self.slot(4))

    def steps(self):
        return [self.start, self.after_core, self.second, self.third, self.after_a, self.finish]


class SmallReduce:
    def __init__(self, place, slots, send, recv, sends):
        self.p, self.slots, self.send, self.recv, self.sends = place, slots, send, recv, sends
        self.now, self.free, self.k = 0, 1, 0

    def copy(self, src, dst, k, device):
        return remote(self.slots.at[src], self.slots.at[dst], self.send.at[k], self.recv.at[k], device)

    def exchange(self, devices):
        self.fresh = []
        for device in devices:
            src, dst, k = self.now, self.free, self.k
            self.fresh.append((dst, k))
            self.sends.go(
                lambda src=src, dst=dst, k=k, device=device: (
                    None,
                    lambda: self.copy(src, dst, k, device()),
                )
            )
            self.free, self.k = self.free + 1, self.k + 1

    def add(self):
        total = self.slots[self.now]
        for slot, k in self.fresh:
            self.copy(slot, slot, k, self.p.sibling()).wait_recv()
            total = total + self.slots[slot]
        self.slots[self.free] = total
        self.now, self.free = self.free, self.free + 1

    def steps(self):
        p = self.p
        stages = [
            [p.sibling],
            [lambda j=j: p.at(b=p.next_b(j)) for j in range(1, p.B)],
            [p.twin],
            [lambda j=j: p.at(a=p.next_a(j)) for j in range(1, p.A)],
        ] + [[functools.partial(p.twin, bit)] for bit in p.bits()]
        out = [lambda: self.exchange(stages[0])]
        for stage in stages[1:]:
            out.append(lambda stage=stage: (self.add(), self.exchange(stage)))
        out.append(self.add)
        return out

    @staticmethod
    def counts(reps, shards):
        wide = max(reps.bit_length() - 2, 0)
        copies = 1 + (shards // 8 - 1) + 1 + 3 + wide
        return copies, 1 + copies + 4 + wide


def dot(lhs, rhs):
    return lax.dot_general(lhs, rhs, (((1,), (0,)), ((), ())), preferred_element_type=F32)


def dot_nt(lhs, rhs):
    return lax.dot_general(lhs, rhs, (((1,), (1,)), ((), ())), preferred_element_type=F32)


def dot_tn(lhs, rhs):
    return lax.dot_general(lhs, rhs, (((0,), (0,)), ((), ())), preferred_element_type=F32)


def iota(shape, axis):
    return lax.broadcasted_iota(jnp.int32, shape, axis)


def mean_last(value):
    return jnp.sum(value, axis=-1, keepdims=True) * (1.0 / value.shape[-1])


def column_sum(value):
    return jnp.sum(value, axis=0, keepdims=True)


def twice(value):
    return jnp.concatenate([value, value], axis=1)


def feature(value):
    return jnp.where(value > 0, value + 1.0, jnp.exp(jnp.minimum(value, 0.0)))


def layer_kernel(reps, shards, length, n):
    p = Place(reps, shards)
    A, B = p.A, p.B
    rows_w = n.w_query.shape[0]
    R = rows_w
    chunks = length // CHUNK
    full, part, smalls, slots, vecs = n.full, n.part, n.smalls, n.slots, n.vecs

    mine = full.at[p.a, p.b, p.c]
    pieces = [
        (ref, mine.at[pl.ds(i * R, R)])
        for i, ref in enumerate((n.w_query, n.w_key, n.w_value, n.w_out))
    ]
    pieces += [
        (n.w_up.at[:, pl.ds(i * WIDTH, WIDTH)], mine.at[pl.ds((4 + i) * R, R)]) for i in range(4)
    ]
    pieces += [(n.w_down, mine.at[pl.ds(8 * R, 4 * R)])]
    pieces += [(n.inputs_far, n.inputs), (n.cotangent_far, n.cotangent)]
    local = [
        pltpu.make_async_copy(src, dst, n.sem_local.at[i]) for i, (src, dst) in enumerate(pieces)
    ]
    for copy in local:
        copy.start()
    smalls[p.a, p.b, p.c] = jnp.zeros((8, 128), F32)
    vectors = (n.b_up, n.b_down, n.gain_attn, n.shift_attn, n.gain_ffn, n.shift_ffn)
    for i, ref in enumerate(vectors):
        size = ref.shape[0]
        smalls[p.a, p.b, p.c, i : i + 1, 0:size] = ref[...].astype(F32).reshape(1, size)
    greet(p.partners())
    for copy in local[:9]:
        copy.wait()

    sends = Sends()
    tiny = SmallGather(p, smalls, n.send0, n.recv0, sends)
    windows = ((0 * R, 3 * R, 0, 512), (3 * R, 5 * R, 0, 512), (8 * R, 4 * R, 0, 512))
    gather_0, gather_1, gather_2 = (
        Gather(p, full, window, n.send1, n.recv1, i * Gather.n_sems(shards), sends)
        for i, window in enumerate(windows)
    )
    bufs = (n.core, n.line_b, n.pair, n.line_a, n.wide, n.done)

    made = []

    def job(lo, rows, at=0, lanes=WIDTH, **more):
        base = sum(one.n_sems() for one in made)
        window = (lo * R, rows * R, at, lanes)
        made.append(Reduce(p, part, bufs, window, (n.send2, n.recv2), base, sends, **more))
        return made[-1]

    up_one = job(4, 2)
    up_two = job(6, 2, pair_first=True)
    down_one = job(8, 4, pair_first=True, span=(0, 2))
    down_two = job(8, 4, span=(2, 4), end=down_one)
    out_all = job(3, 1)
    attn_one = job(0, 3, 0, 256)
    attn_two = job(0, 1, 256, 256)
    attn_three = job(1, 2, 256, 256, pair_first=True)
    assert sum(one.n_sems() for one in made) <= n.recv2.shape[0]
    small_sum = SmallReduce(p, slots, n.send3, n.recv3, sends)
    T = small_sum.steps()

    def rows_of(t, size=CHUNK):
        return pl.ds(pl.multiple_of(t * size, size), size)

    def per_chunk(events, body, down=False, size=CHUNK):
        chunks = length // size

        def step(i, carry):
            body(chunks - 1 - i if down else i)
            for at, calls in enumerate(events):
                if calls:

                    @pl.when(i == at)
                    def _():
                        for call in calls:
                            call()

            return carry

        lax.fori_loop(0, chunks, step, 0)

    gather_0.own()
    tiny.own()
    tiny.second()
    gather_1.own()
    tiny.third()

    seg_row = n.segment_ids[...].astype(F32)
    seg_rows = n.seg_rows
    seg_rows[0:8, :] = jnp.full((8, 128), -1.0, F32)
    seg_rows[pl.ds(8, length), :] = jnp.broadcast_to(seg_row, (128, length)).T
    seg_rows[pl.ds(8 + length, 8), :] = jnp.full((8, 128), -2.0, F32)
    heads, mask, mask_t = n.heads, n.mask, n.mask_t
    for i in range(PER_GROUP):
        heads[i] = jnp.where(iota((CHUNK, GROUP), 1) // HEAD_DIM == i, 1.0, 0.0).astype(BF16)
    same_head = (iota((GROUP, GROUP), 0) // HEAD_DIM) == (iota((GROUP, GROUP), 1) // HEAD_DIM)
    n.ones[...] = jnp.where(same_head, 1.0, 0.0).astype(BF16)
    later_row = iota((CHUNK, CHUNK), 0) >= iota((CHUNK, CHUNK), 1)
    later_col = iota((CHUNK, CHUNK), 0) <= iota((CHUNK, CHUNK), 1)
    for t in range(chunks):
        same = twice(seg_rows[pl.ds(8 + t * CHUNK, CHUNK), :]) == seg_row[
            :, t * CHUNK : (t + 1) * CHUNK
        ]
        mask[t] = jnp.where(same & later_row, 1.0, 0.0).astype(BF16)
        mask_t[t] = jnp.where(same & later_col, 1.0, 0.0).astype(BF16)

    def seg_chunk(t):
        return seg_rows[pl.ds(pl.multiple_of(8 + t * CHUNK, 8), CHUNK), :]

    def seg_at(t, row):
        return seg_rows[pl.ds(8 + t * CHUNK + row, 1), :]

    def flags(one, two):
        return twice(jnp.where(one == two, 1.0, 0.0))

    gather_0.line_a(1)
    tiny.last()
    gather_0.line_a(2)
    gather_0.line_a(0)
    gather_0.line_b(1)
    gather_0.line_b(2)
    gather_0.line_b(0)
    gather_1.line_a(1)
    gather_0.line_b_own()
    gather_1.line_a(2)

    local[9].wait()
    def norm_one(t):
        at = rows_of(t)
        h = n.inputs[at].astype(F32)
        centre = h - mean_last(h)
        scale = lax.rsqrt(mean_last(centre * centre) + epsilon)
        n.normal_one[at] = (centre * scale).astype(BF16)
        n.scale_one[at] = jnp.broadcast_to(scale, (CHUNK, 128))

    per_chunk([], norm_one)
    gather_0.twin(2)
    gather_1.line_a(0)
    gather_0.twin(0)
    gather_0.twin(1)
    gather_2.own()

    blocks = smalls[...].reshape(shards * 8, 128).astype(BF16)
    lane = iota((128, WIDTH), 1)
    row = iota((128, WIDTH), 0)
    block = iota((shards, 8, WIDTH), 0)
    at_lane = iota((shards, 8, WIDTH), 2)
    spread = jnp.where(lane % R == row, 1.0, 0.0).astype(BF16)
    laid = dot(blocks, spread).reshape(shards, 8, WIDTH)
    vecs[0:8] = jnp.sum(jnp.where(at_lane // R == block, laid, 0.0), axis=0)
    spread = jnp.where(lane % (4 * R) == row, 1.0, 0.0).astype(BF16)
    laid = dot(blocks, spread).reshape(shards, 8, WIDTH)
    for i in range(4):
        picked = jnp.where((at_lane + i * WIDTH) // (4 * R) == block, laid, 0.0)
        vecs[8 + i : 9 + i] = jnp.sum(picked, axis=0)[0:1]
    b_down, gain_one, shift_one, gain_two, shift_two = (vecs[i : i + 1] for i in range(1, 6))

    gather_0.rest()
    gather_1.line_b(1)

    def weight(i):
        return full[:, :, :, i * R : (i + 1) * R, :].reshape(WIDTH, WIDTH)

    def weight_down(i):
        return full[i, :, :, 8 * R : 12 * R, :].reshape(WIDTH, WIDTH)

    lanes = [slice(g * GROUP, (g + 1) * GROUP) for g in range(GROUPS)]
    state, state_now, keys_now = n.state, n.state_now, n.keys_now
    state_now[...] = jnp.zeros(state_now.shape, F32)
    keys_now[...] = jnp.zeros(keys_now.shape, F32)
    slots[0] = jnp.zeros(slots.shape[1:], F32)

    def project(t):
        at = rows_of(t, 512)
        normed = (n.normal_one[at].astype(F32) * gain_one + shift_one).astype(BF16)
        n.normed_attn[at] = normed
        n.query[at] = feature(dot(normed, weight(0))).astype(BF16)
        n.key[at] = feature(dot(normed, weight(1))).astype(BF16)
        n.value[at] = dot(normed, weight(2)).astype(BF16)

    def forward(g):
        cut = lanes[g]

        def body(t):
            at = rows_of(t)
            q, k, v = n.query[at, cut], n.key[at, cut], n.value[at, cut]
            seg = seg_chunk(t)
            before = flags(seg, seg_at(t, -1))
            ending = flags(seg, seg_at(t, CHUNK - 1)).astype(BF16)
            carry = flags(seg_at(t, CHUNK - 1), seg_at(t, -1))
            old = state_now[g].astype(BF16)
            state[g, t] = old
            mixed = dot(q * before.astype(BF16), old)
            for i in range(PER_GROUP):
                scores = dot_nt(q * heads[i], k).astype(BF16) * mask[t]
                mixed = mixed + dot(scores, v * heads[i])
            sums = dot(mask[t], k) + before * keys_now[g, 0:1]
            n.key_sums[at, cut] = sums
            totals = dot((q.astype(F32) * sums).astype(BF16), n.ones[...])
            inverse = 1.0 / totals
            n.inverse[at, cut] = inverse
            n.context[at, cut] = (mixed * inverse).astype(BF16)
            ended = k * ending
            state_now[g] = state_now[g] * carry + dot_tn(ended, v) * n.ones[...].astype(F32)
            keys_now[g, 0:1] = keys_now[g, 0:1] * carry + column_sum(ended.astype(F32))

        return body

    per_chunk([[], []], project, size=512)
    gather_1.line_b(2)
    per_chunk([[], [], [(lambda: gather_1.line_b(0))], []], forward(0))
    per_chunk([[gather_2.line_b_own, (lambda: gather_2.line_a(0))], [(lambda: gather_1.twin(1))], [gather_1.line_b_own, (lambda: gather_1.twin(2)), (lambda: gather_1.twin(0)), (lambda: gather_2.line_a(1))], []], forward(1))
    gather_1.rest()

    c0 = 0.7978845608028654
    c1 = c0 * 0.044715

    def norm_two(t):
        at = rows_of(t, 512)
        after = n.inputs[at].astype(F32) + dot(n.context[at], weight(3))
        centre = after - mean_last(after)
        scale = lax.rsqrt(mean_last(centre * centre) + epsilon)
        normal = centre * scale
        n.normal_two[at] = normal.astype(BF16)
        n.scale_two[at] = jnp.broadcast_to(scale, (512, 128))
        n.normed_ffn[at] = (normal * gain_two + shift_two).astype(BF16)
        n.result[at] = after + b_down

    def hidden_units(i):
        cut = slice(i * WIDTH, (i + 1) * WIDTH)
        pre = dot(n.normed_ffn[...], weight(4 + i)) + vecs[8 + i : 9 + i]
        square = pre * pre
        half = 0.5 + 0.5 * jnp.tanh(pre * (c0 + c1 * square))
        hidden = pre * half
        slope = half + (2.0 * hidden) * (1.0 - half) * (c0 + (3.0 * c1) * square)
        n.hidden[:, cut] = hidden.astype(BF16)
        n.grad_pre[:, cut] = slope.astype(BF16)

    per_chunk([[(lambda: gather_2.line_a(2))], [(lambda: gather_2.line_b(0))]], norm_two, size=512)
    hidden_units(0)
    gather_2.line_b(1)
    hidden_units(1)
    gather_2.line_b(2)
    hidden_units(2)
    hidden_units(3)
    local[10].wait()

    def down_grads(i):
        for m in range(2):
            some = slice(i * WIDTH + m * 256, i * WIDTH + (m + 1) * 256)
            grad = dot_tn(n.hidden[:, some], n.cotangent[...]).astype(BF16)
            part[i, m * B // 2 : (m + 1) * B // 2, :, 8 * R : 12 * R, :] = grad.reshape(
                B // 2, 2, 4 * R, WIDTH
            )

    down_grads(0)
    gather_2.twin(1)
    gather_2.twin(0)
    gather_2.twin(2)
    down_grads(1)
    down_grads(2)
    down_grads(3)
    down_two.start()
    down_one.start()
    gather_2.rest()

    def ffn(i):
        cut = slice(i * WIDTH, (i + 1) * WIDTH)
        grad = dot_nt(n.cotangent[...], weight_down(i)) * n.grad_pre[:, cut].astype(F32)
        grad = grad.astype(BF16)
        n.grad_pre[:, cut] = grad
        slots[0, i : i + 1] += column_sum(grad.astype(F32))

    def up_grads(i):
        cut = slice(i * WIDTH, (i + 1) * WIDTH)
        for m in range(2):
            some = slice(m * 256, (m + 1) * 256)
            grad = dot_tn(n.normed_ffn[:, some], n.grad_pre[:, cut]).astype(BF16)
            part[2 * m : 2 * m + 2, :, :, (4 + i) * R : (5 + i) * R, :] = grad.reshape(
                2, B, 2, R, WIDTH
            )

    ffn(0)
    up_grads(0)
    ffn(1)
    up_grads(1)
    up_one.start()
    down_two.after_core()
    ffn(2)
    up_grads(2)
    ffn(3)
    down_one.after_core()
    up_grads(3)
    up_two.start()

    def norm_two_back(t):
        at = rows_of(t, 512)
        grad = dot_nt(n.grad_pre[at, 0:WIDTH], weight(4))
        for i in range(1, 4):
            grad = grad + dot_nt(n.grad_pre[at, i * WIDTH : (i + 1) * WIDTH], weight(4 + i))
        normal = n.normal_two[at].astype(F32)
        up = n.cotangent[at].astype(F32)
        slots[0, 4:5] += column_sum(up)
        slots[0, 7:8] += column_sum(grad * normal)
        slots[0, 8:9] += column_sum(grad)
        e = grad * gain_two
        back = e - mean_last(e) - normal * mean_last(e * normal)
        after = up + n.scale_two[at][:, 0:1] * back
        n.grad_normed[at] = after
        low = after.astype(BF16)
        n.grad_attn[at] = low
        grad_context = dot_nt(low, weight(3)).astype(BF16).astype(F32)
        inverse = n.inverse[at]
        n.grad_mixed[at] = (grad_context * inverse).astype(BF16)
        turned = (grad_context * n.context[at].astype(F32)).astype(BF16)
        for g in range(GROUPS):
            n.grad_totals[at, lanes[g]] = -dot(turned[:, lanes[g]], n.ones[...]) * inverse[
                :, lanes[g]
            ]

    per_chunk([[up_one.after_core], []], norm_two_back, size=512)
    for m in range(2):
        grad = dot_tn(n.context[:, m * 256 : (m + 1) * 256], n.grad_attn[...]).astype(BF16)
        part[2 * m : 2 * m + 2, :, :, 3 * R : 4 * R, :] = grad.reshape(2, B, 2, R, WIDTH)

    def backward(g):
        state_now[g] = jnp.zeros((GROUP, GROUP), F32)
        keys_now[g] = jnp.zeros((8, GROUP), F32)

        def body(t):
            at = rows_of(t)
            seg = seg_chunk(t)
            before = flags(seg, seg_at(t, -1)).astype(BF16)
            after = flags(seg, seg_at(t, CHUNK))
            opening = flags(seg, seg_at(t, 0)).astype(BF16)
            carry = flags(seg_at(t, 0), seg_at(t, CHUNK))
            q, k, v, gm = (
                ref[at, lanes[g]] for ref in (n.query, n.key, n.value, n.grad_mixed)
            )
            totals = n.grad_totals[at, lanes[g]]
            old = state_now[g].astype(BF16)
            weighted = totals * q.astype(F32)
            gq = dot_nt(gm * before, state[g, t]) + totals * n.key_sums[at, lanes[g]]
            gk = after * (dot_nt(v, old) + keys_now[g, 0:1]) + dot(mask_t[t], weighted.astype(BF16))
            gv = after * dot(k, old)
            for i in range(PER_GROUP):
                head = heads[i]
                gm_head = gm * head
                back = dot_nt(gm_head, v).astype(BF16) * mask[t]
                gq = gq + dot(back, k * head)
                back = dot_nt(v * head, gm).astype(BF16) * mask_t[t]
                gk = gk + dot(back, q * head)
                back = dot_nt(k * head, q).astype(BF16) * mask_t[t]
                gv = gv + dot(back, gm_head)
            n.grad_query[at, lanes[g]] = (gq * jnp.minimum(q.astype(F32), 1.0)).astype(BF16)
            n.grad_key[at, lanes[g]] = (gk * jnp.minimum(k.astype(F32), 1.0)).astype(BF16)
            n.grad_value[at, lanes[g]] = gv.astype(BF16)
            opened = q * opening
            state_now[g] = state_now[g] * carry + dot_tn(opened, gm) * n.ones[...].astype(F32)
            keys_now[g, 0:1] = keys_now[g, 0:1] * carry + column_sum(
                weighted * opening.astype(F32)
            )

        return body

    def weight_grads(g):
        for i, ref in enumerate((n.grad_query, n.grad_key, n.grad_value)):
            grad = dot_tn(n.normed_attn[...], ref[:, lanes[g]]).astype(BF16)
            part[:, :, :, i * R : (i + 1) * R, lanes[g]] = grad.reshape(A, B, 2, R, GROUP)

    per_chunk([[down_two.second, down_one.second], [], [out_all.start, up_two.after_core], []], backward(0), down=True)
    out_all.after_core()
    down_two.third()
    weight_grads(0)
    attn_one.start()
    per_chunk([[down_one.third, attn_one.after_core, up_one.second], [], [out_all.second], []], backward(1), down=True)
    up_two.second()
    weight_grads(1)
    attn_one.second()
    up_one.third()
    attn_three.start()
    attn_two.start()

    def norm_one_back(t):
        at = rows_of(t, 512)
        grad = dot_nt(n.grad_query[at], weight(0))
        grad = grad + dot_nt(n.grad_key[at], weight(1))
        grad = grad + dot_nt(n.grad_value[at], weight(2))
        normal = n.normal_one[at].astype(F32)
        slots[0, 5:6] += column_sum(grad * normal)
        slots[0, 6:7] += column_sum(grad)
        e = grad * gain_one
        back = e - mean_last(e) - normal * mean_last(e * normal)
        n.grad_normed[at] = n.grad_normed[at] + n.scale_one[at][:, 0:1] * back

    per_chunk([[attn_two.after_core, attn_three.after_core, out_all.third], []], norm_one_back, size=512)
    store = pltpu.make_async_copy(n.grad_normed, n.grad_inputs_far, n.sem_local.at[11])
    store.start()
    up_two.third()
    attn_one.third()
    T[0]()
    T[1]()
    down_one.after_a()
    attn_three.second()
    attn_two.second()
    up_one.after_a()

    def outputs(t):
        at = rows_of(t, 512)
        total = n.result[at]
        for i in range(4):
            total = total + dot(n.hidden[at, i * WIDTH : (i + 1) * WIDTH], weight_down(i))
        n.output[at] = total.astype(BF16)

    per_chunk([[attn_two.third, T[2], attn_three.third, up_one.finish, out_all.after_a, T[3], up_two.after_a], []], outputs, size=512)
    store_more = pltpu.make_async_copy(n.output, n.output_far, n.sem_local.at[12])
    store_more.start()
    down_one.finish()
    attn_two.after_a()
    attn_one.after_a()
    out_all.finish()
    attn_three.after_a()
    attn_two.finish()
    attn_three.finish()
    up_two.finish()
    attn_one.finish()
    T[4]()

    total = slots[small_sum.now]
    high = total.astype(BF16)
    low = (total - high.astype(F32)).astype(BF16)
    row, lane = iota((WIDTH, 128), 0), iota((WIDTH, 128), 1)
    pick = jnp.where((row == lane + p.s * R) & (lane < R), 1.0, 0.0).astype(BF16)
    n.tiny_out[0:16] = dot(high, pick) + dot(low, pick)
    picked = jnp.zeros((16, 128), F32)
    for i in range(4):
        wanted = (row + i * WIDTH == lane + p.s * (4 * R)) & (lane < 4 * R)
        pick = jnp.where(wanted, 1.0, 0.0).astype(BF16)
        keep = iota((16, 128), 0) == i
        picked = picked + jnp.where(keep, dot(high, pick) + dot(low, pick), 0.0)
    n.tiny_out[16:17] = column_sum(picked)

    store.wait()
    store_more.wait()
    sends.finish()


PIECES = 2


def final_kernel(output, grad_inputs, done, tiny, *refs):
    outs = refs[:14]
    held_out, held_grad, held_done, held_tiny = refs[14:18]
    held = refs[18:-2]
    sem, more = refs[-2:]
    rows = output.shape[0] // PIECES
    first = [
        pltpu.make_async_copy(done, held_done, more.at[0]),
        pltpu.make_async_copy(tiny, held_tiny, more.at[1]),
    ]
    into, back = [], []
    for i in range(PIECES):
        cut = pl.ds(i * rows, rows)
        for k, (src, mid, dst) in enumerate(
            ((grad_inputs, held_grad, outs[1]), (output, held_out, outs[0]))
        ):
            into.append(pltpu.make_async_copy(src.at[cut], mid.at[cut], sem.at[0, k, i]))
            back.append(pltpu.make_async_copy(mid.at[cut], dst.at[cut], sem.at[1, k, i]))
    for copy in first + into:
        copy.start()
    for copy in first:
        copy.wait()
    R = held[0].shape[0]
    for i in range(4):
        held[i][...] = held_done[i * R : (i + 1) * R].astype(F32)
        held[4][:, i * WIDTH : (i + 1) * WIDTH] = held_done[(4 + i) * R : (5 + i) * R].astype(F32)
    held[5][...] = held_done[8 * R : 12 * R].astype(F32)
    for i in range(6):
        back.append(pltpu.make_async_copy(held[i], outs[2 + i], more.at[2 + i]))
        back[-1].start()
    for ref, row in zip(outs[8:14], (16, 4, 5, 6, 7, 8), strict=True):
        ref[...] = held_tiny[row, : ref.shape[0]]
    for one, two in zip(into, back, strict=False):
        one.wait()
        two.start()
    for copy in back:
        copy.wait()


def final(output, grad_inputs, done, tiny):
    R = done.shape[0] // 12
    vmem, far = pl.BlockSpec(memory_space=pltpu.VMEM), pl.BlockSpec(memory_space=pl.ANY)
    grads = [((R, WIDTH), F32)] * 4 + [((R, 4 * WIDTH), F32), ((4 * R, WIDTH), F32)]
    shapes = [(output.shape, BF16), (grad_inputs.shape, F32)] + grads
    shapes += [((4 * R,), F32)] + [((R,), F32)] * 5
    return pl.pallas_call(
        final_kernel,
        out_shape=tuple(jax.ShapeDtypeStruct(*shape) for shape in shapes),
        in_specs=[far] * 4,
        out_specs=(far,) * 8 + (vmem,) * 6,
        scratch_shapes=[
            pltpu.VMEM(output.shape, BF16),
            pltpu.VMEM(grad_inputs.shape, F32),
            pltpu.VMEM(done.shape, BF16),
            pltpu.VMEM(tiny.shape, F32),
        ]
        + [pltpu.VMEM(*shape) for shape in grads]
        + [pltpu.SemaphoreType.DMA((2, 2, PIECES)), pltpu.SemaphoreType.DMA((8,))],
        name="final",
    )(output, grad_inputs, done, tiny)


def layer(reps, shards, inputs, segment_ids, weights, vectors, cotangent):
    length = inputs.shape[0]
    A, B = 4, shards // 8
    R = weights[0].shape[0]
    rows = 12 * R
    bits = max(reps.bit_length() - 2, 0)
    copies, n_slots = SmallReduce.counts(reps, shards)
    sums = 5 * (2 * B + A + bits) + 3 * (3 * B - 1 + A + bits) + 1 * (3 * B - 1)
    groups = 3
    w_query, w_key, w_value, w_out, w_up, w_down = weights
    b_up, b_down, gain_attn, shift_attn, gain_ffn, shift_ffn = vectors
    far_ins = dict(
        inputs_far=inputs,
        cotangent_far=cotangent,
        w_query=w_query,
        w_key=w_key,
        w_value=w_value,
        w_out=w_out,
        w_up=w_up,
        w_down=w_down,
    )
    ins = dict(
        segment_ids=segment_ids,
        b_up=b_up,
        b_down=b_down,
        gain_attn=gain_attn,
        shift_attn=shift_attn,
        gain_ffn=gain_ffn,
        shift_ffn=shift_ffn,
    )
    far_outs = dict(
        output_far=((length, WIDTH), BF16),
        grad_inputs_far=((length, WIDTH), F32),
    )
    outs = dict(
        done=((rows, WIDTH), BF16),
        tiny_out=((24, 128), F32),
    )
    tall = (length, WIDTH)
    buffers = dict(
        inputs=(tall, BF16),
        cotangent=(tall, BF16),
        result=(tall, F32),
        full=((A, B, 2, rows, WIDTH), BF16),
        part=((A, B, 2, rows, WIDTH), BF16),
        core=((A, B, rows, WIDTH), BF16),
        line_b=((B - 1, A, rows, WIDTH), BF16),
        pair=((A, B, rows, WIDTH), BF16),
        line_a=((A - 1, rows, WIDTH), BF16),
        wide=((max(2 * bits, 1), rows if bits else 16, WIDTH), BF16),
        smalls=((A, B, 2, 8, 128), F32),
        slots=((n_slots, 16, WIDTH), F32),
        vecs=((16, WIDTH), F32),
        seg_rows=((length + 16, 128), F32),
        heads=((PER_GROUP, CHUNK, GROUP), BF16),
        ones=((GROUP, GROUP), BF16),
        mask=((length // CHUNK, CHUNK, CHUNK), BF16),
        mask_t=((length // CHUNK, CHUNK, CHUNK), BF16),
        normal_one=(tall, BF16),
        scale_one=((length, 128), F32),
        normed_attn=(tall, BF16),
        query=(tall, BF16),
        key=(tall, BF16),
        value=(tall, BF16),
        key_sums=(tall, F32),
        inverse=(tall, F32),
        context=(tall, BF16),
        state=((GROUPS, length // CHUNK, GROUP, GROUP), BF16),
        state_now=((GROUPS, GROUP, GROUP), F32),
        keys_now=((GROUPS, 8, GROUP), F32),
        normal_two=(tall, BF16),
        scale_two=((length, 128), F32),
        normed_ffn=(tall, BF16),
        hidden=((length, 4 * WIDTH), BF16),
        grad_pre=((length, 4 * WIDTH), BF16),
        grad_normed=(tall, F32),
        grad_mixed=(tall, BF16),
        grad_totals=(tall, F32),
    )
    sems = dict(
        sem_local=(13,),
        send0=(A + B,),
        recv0=(A + B,),
        send1=(groups * Gather.n_sems(shards),),
        recv1=(groups * Gather.n_sems(shards),),
        send2=(sums,),
        recv2=(sums,),
        send3=(copies,),
        recv3=(copies,),
    )
    names = [*far_ins, *ins, *far_outs, *outs, *buffers, *sems]

    def kernel(*refs):
        n = types.SimpleNamespace(**dict(zip(names, refs, strict=True)))
        n.output, n.grad_attn = n.inputs, n.normed_ffn
        n.grad_query, n.grad_key, n.grad_value = (
            n.grad_pre.at[:, pl.ds(i * WIDTH, WIDTH)] for i in range(3)
        )
        layer_kernel(reps, shards, length, n)

    vmem, far = pl.BlockSpec(memory_space=pltpu.VMEM), pl.BlockSpec(memory_space=pl.ANY)
    flops = 2 * 3 * length * WIDTH * WIDTH * 12 + 20 * length * length * WIDTH
    return pl.pallas_call(
        kernel,
        out_shape=tuple(
            jax.ShapeDtypeStruct(*spec) for spec in [*far_outs.values(), *outs.values()]
        ),
        in_specs=[far] * len(far_ins) + [vmem] * len(ins),
        out_specs=(far,) * len(far_outs) + (vmem,) * len(outs),
        scratch_shapes=[pltpu.VMEM(*spec) for spec in buffers.values()]
        + [pltpu.SemaphoreType.DMA(shape) for shape in sems.values()],
        compiler_params=pltpu.CompilerParams(
            collective_id=1, has_side_effects=True, vmem_limit_bytes=63 << 20
        ),
        cost_estimate=pl.CostEstimate(flops=flops, bytes_accessed=8 << 20, transcendentals=0),
        name="layer",
    )(*far_ins.values(), *ins.values())


def on_device(
    reps,
    shards,
    inputs,
    segment_ids,
    w_query,
    w_key,
    w_value,
    w_out,
    w_up,
    w_down,
    b_up,
    b_down,
    gain_attn,
    shift_attn,
    gain_ffn,
    shift_ffn,
    cotangent,
):
    sequences, length, width = inputs.shape
    output, grad_inputs, done, tiny = layer(
        reps,
        shards,
        inputs.reshape(sequences * length, width),
        segment_ids,
        (w_query, w_key, w_value, w_out, w_up, w_down),
        (b_up, b_down, gain_attn, shift_attn, gain_ffn, shift_ffn),
        cotangent.reshape(sequences * length, width),
    )
    output, grad_inputs, *grads = final(output, grad_inputs, done, tiny)
    return (output.reshape(inputs.shape), grad_inputs.reshape(inputs.shape), *grads)


def solution(mesh):
    reps, shards = mesh.shape["rep"], mesh.shape["shard"]
    token = P(("rep", "shard"), None, None)
    matrix, vector = P("shard", None), P("shard")
    return jax.shard_map(
        functools.partial(on_device, reps, shards),
        mesh=mesh,
        in_specs=(token, P(("rep", "shard"), None)) + (matrix,) * 6 + (vector,) * 6 + (token,),
        out_specs=(token, token) + (matrix,) * 6 + (vector,) * 6,
        check_vma=False,
    )
```

```python
import functools
import types

import jax
import jax.numpy as jnp
from jax import lax
from jax.experimental import pallas as pl
from jax.experimental.pallas import tpu as pltpu
from jax.sharding import PartitionSpec as P

WIDTH = 512
CHUNK = 256
HEAD_DIM = 64
GROUP = 256
PER_GROUP = GROUP // HEAD_DIM
GROUPS = WIDTH // GROUP

epsilon = 1e-05
MESH = pl.DeviceIdType.MESH
F32 = jnp.float32
BF16 = jnp.bfloat16


class Place:
    def __init__(self, reps, shards):
        self.reps, self.shards = reps, shards
        self.A = 4
        self.B = shards // 8
        self.r = lax.axis_index("rep")
        s = lax.axis_index("shard")
        self.s = s
        self.c = lax.rem(s, 2)
        self.b = lax.rem(s // 2, self.B)
        self.a = s // (2 * self.B)
        self.h = lax.rem(self.r, 2)

    def at(self, a=None, b=None, c=None, r=None):
        a = self.a if a is None else a
        b = self.b if b is None else b
        c = self.c if c is None else c
        r = self.r if r is None else r
        return (r, (a * self.B + b) * 2 + c)

    def near(self, k):
        high = self.a // 2
        return (1 - self.a + 4 * high, 2 - high, 3 * (1 - high))[k]

    def next_a(self, j):
        return lax.rem(self.a + j, self.A)

    def next_b(self, j):
        return lax.rem(self.b + j, self.B)

    def sibling(self):
        return self.at(c=1 - self.c)

    def twin(self, bit=1):
        return self.at(r=self.r + bit - 2 * bit * lax.rem(self.r // bit, 2))

    def bits(self):
        bit, out = 2, []
        while bit < self.reps:
            out.append(bit)
            bit *= 2
        return out

    def partners(self):
        out = [self.sibling(), self.twin()]
        out += [self.at(a=self.next_a(j)) for j in range(1, self.A)]
        out += [self.at(b=self.next_b(j)) for j in range(1, self.B)]
        return out + [self.twin(bit) for bit in self.bits()]


def greet(partners):
    barrier = pltpu.get_barrier_semaphore()
    for device in partners:
        pl.semaphore_signal(barrier, inc=1, device_id=device, device_id_type=MESH)
    pl.semaphore_wait(barrier, len(partners))


def remote(src, dst, send, recv, device):
    return pltpu.make_async_remote_copy(
        src_ref=src, dst_ref=dst, send_sem=send, recv_sem=recv, device_id=device, device_id_type=MESH
    )


def both(one, two):
    if one is None:
        return two
    return one if two is None else jnp.logical_and(one, two)


class Sends:
    def __init__(self):
        self.made = []

    @staticmethod
    def act(copy, do):
        cond, make = copy()
        if cond is None:
            do(make())
        else:
            pl.when(cond)(lambda: do(make()))

    def go(self, copy):
        self.act(copy, lambda made: made.start())
        self.made.append(copy)

    def arrived(self, copy):
        self.act(copy, lambda made: made.wait_recv())

    def finish(self):
        for copy in self.made:
            self.act(copy, lambda made: made.wait_send())
        self.made = []


class Gather:
    def __init__(self, place, full, window, send, recv, base, sends):
        self.p, self.full = place, full
        self.lo, self.rows, self.left, self.lanes = window
        self.send, self.recv, self.base, self.sends = send, recv, base, sends

    def whole(self, a, b, c):
        return self.full.at[a, b, c, pl.ds(self.lo, self.rows), pl.ds(self.left, self.lanes)]

    def half(self, a, b, c, h):
        size = self.lanes // 2
        lanes = pl.ds(pl.multiple_of(self.left + h * size, 128), size)
        return self.full.at[a, b, c, pl.ds(self.lo, self.rows), lanes]

    def copy(self, ref, k, device, other=None):
        return remote(ref, ref, self.send.at[k], self.recv.at[k if other is None else other], device)

    def go(self, make):
        self.sends.go(lambda: (None, make))

    def slot(self, kind, k=0, j=0):
        more = self.p.B - 1
        j = max(j - 1, 0)
        base = (0, 4, 4 + more, 4 + 4 * more, 7 + 4 * more, 7 + 7 * more)
        base += (8 + 7 * more, 8 + 8 * more, 11 + 8 * more)
        return self.base + base[kind] + (k * more if kind in (2, 4) else k) + j

    def own(self):
        p = self.p
        for k in (2, 1, 0):
            self.go(
                lambda k=k: self.copy(
                    self.half(p.a, p.b, p.c, p.h) if k else self.whole(p.a, p.b, p.c),
                    self.slot(0, k),
                    p.at(a=p.near(k)),
                    self.slot(0, p.a),
                )
            )
        for j in range(1, p.B):
            self.go(
                lambda j=j: self.copy(
                    self.whole(p.a, p.b, p.c), self.slot(1, 0, j), p.at(b=p.next_b(j))
                )
            )
        self.go(lambda: self.copy(self.whole(p.a, p.b, p.c), self.slot(5), p.sibling()))

    def line_a(self, k):
        p = self.p
        place = (p.near(k), p.b, p.c)
        ref = self.half(*place, p.h) if k else self.whole(*place)
        self.copy(ref, self.slot(0, p.near(k)), p.sibling()).wait_recv()

        def mine():
            return self.half(p.near(k), p.b, p.c, p.h)

        for j in range(1, p.B):
            self.go(lambda j=j: self.copy(mine(), self.slot(2, k, j), p.at(b=p.next_b(j))))
        if k:
            self.go(lambda: self.copy(mine(), self.slot(3, k), p.twin()))

    def line_b_own(self):
        p = self.p
        for j in range(1, p.B):
            b = p.next_b(p.B - j)
            self.copy(self.whole(p.a, b, p.c), self.slot(1, 0, j), p.sibling()).wait_recv()
            self.go(
                lambda j=j: self.copy(
                    self.whole(p.a, p.next_b(p.B - j), p.c), self.slot(6, 0, j), p.sibling()
                )
            )

    def line_b(self, k):
        p = self.p
        for j in range(1, p.B):
            b = p.next_b(p.B - j)
            ref = self.half(p.near(k), b, p.c, p.h)
            self.copy(ref, self.slot(2, k, j), p.sibling()).wait_recv()
            self.go(
                lambda j=j: self.copy(
                    self.half(p.near(k), p.next_b(p.B - j), p.c, p.h), self.slot(4, k, j), p.twin()
                )
            )
        self.go(
            lambda: self.copy(
                self.half(p.near(k), slice(None), p.c, p.h), self.slot(7, k), p.sibling()
            )
        )

    def twin(self, k):
        p = self.p
        for j in range(0 if k else 1, p.B):
            ref = self.half(p.near(k), p.next_b(p.B - j), p.c, 1 - p.h)
            kind = 4 if j else 3
            self.copy(ref, self.slot(kind, k, j), p.sibling()).wait_recv()
        self.go(
            lambda: self.copy(
                self.half(p.near(k), slice(None), p.c, 1 - p.h), self.slot(8, k), p.sibling()
            )
        )

    def rest(self):
        p = self.p
        other = 1 - p.c
        self.copy(self.whole(p.a, p.b, other), self.slot(5), p.sibling()).wait_recv()
        for j in range(1, p.B):
            ref = self.whole(p.a, p.next_b(p.B - j), other)
            self.copy(ref, self.slot(6, 0, j), p.sibling()).wait_recv()
        for k in range(3):
            for kind, h in ((7, p.h), (8, 1 - p.h)):
                ref = self.half(p.near(k), slice(None), other, h)
                self.copy(ref, self.slot(kind, k), p.sibling()).wait_recv()

    @staticmethod
    def n_sems(shards):
        return 14 + 8 * (shards // 8 - 1)


class SmallGather:
    def __init__(self, place, full, send, recv, sends):
        self.p, self.full, self.send, self.recv, self.sends = place, full, send, recv, sends

    def copy(self, ref, k, device):
        return remote(ref, ref, self.send.at[k], self.recv.at[k], device)

    def own(self):
        p = self.p
        for j in range(1, p.A):
            self.sends.go(
                lambda j=j: (
                    None,
                    lambda: self.copy(self.full.at[p.a, p.b, p.c], j, p.at(a=p.next_a(j))),
                )
            )

    def second(self):
        p = self.p
        for j in range(1, p.A):
            self.copy(self.full.at[p.next_a(p.A - j), p.b, p.c], j, p.sibling()).wait_recv()
        for j in range(1, p.B):
            self.sends.go(
                lambda j=j: (
                    None,
                    lambda: self.copy(self.full.at[:, p.b, p.c], p.A + j, p.at(b=p.next_b(j))),
                )
            )

    def third(self):
        p = self.p
        for j in range(1, p.B):
            self.copy(self.full.at[:, p.next_b(p.B - j), p.c], p.A + j, p.sibling()).wait_recv()
        self.sends.go(lambda: (None, lambda: self.copy(self.full.at[:, :, p.c], 0, p.sibling())))

    def last(self):
        p = self.p
        self.copy(self.full.at[:, :, 1 - p.c], 0, p.sibling()).wait_recv()


class Reduce:
    def __init__(self, place, part, bufs, window, sems, base, sends, pair_first=False, span=None, end=None):
        self.p, self.part = place, part
        self.lo, self.rows, self.at, self.lanes = window
        self.core, self.line_b, self.pair, self.line_a, self.wide, self.done = bufs
        self.send, self.recv = sems
        self.sends = sends
        self.pair_first = pair_first
        self.first, self.last = span or (0, place.A)
        self.end = end or self
        self.base = base

    def slot(self, kind, j=0):
        B = self.p.B
        twins = B if self.pair_first else 1
        base = (0, B - 1, 2 * B - 1, 2 * B - 2 + twins, 2 * B + 2 + twins, 2 * B + 3 + twins)
        return self.base + base[kind] + j

    def n_sems(self):
        last = self.slot(3, 1) if self.end is not self else self.slot(5, len(self.p.bits()))
        return last - self.base

    def span(self):
        return slice(self.first, self.last)

    def win(self):
        return (pl.ds(self.lo, self.rows), pl.ds(self.at, self.lanes))

    def half(self, h):
        size = self.lanes // 2
        return (
            pl.ds(self.lo, self.rows),
            pl.ds(pl.multiple_of(self.at + h * size, 128), size),
        )

    def go(self, copy, when=lambda: None):
        self.sends.go(lambda: (when(), lambda: self.copy(*copy())))

    def copy(self, src, dst, k, device):
        return remote(src, dst, self.send.at[k], self.recv.at[k], device)

    def arrived(self, ref, k):
        self.copy(ref, ref, k, self.p.sibling()).wait_recv()

    def order(self):
        return list(range(1, self.p.B)) + [0]

    def start(self):
        p = self.p
        for j in self.order():
            self.go(
                lambda j=j: (
                    self.part.at[(self.span(), p.next_b(j), 1 - p.c) + self.win()],
                    self.core.at[(self.span(), j) + self.win()],
                    self.slot(0, j),
                    p.sibling(),
                )
            )

    def after_core(self):
        p = self.p
        for j in self.order():
            mine = (self.span(), p.next_b(j), p.c) + self.win()
            got = (self.span(), j) + self.win()
            self.arrived(self.core.at[got], self.slot(0, j))
            self.part[mine] = self.part[mine] + self.core[got]
            if self.pair_first:
                self.to_pair(j)
            elif j > 0:
                self.to_b(j, self.win)

    def to_b(self, j, win):
        p = self.p
        self.go(
            lambda: (
                self.part.at[(self.span(), p.next_b(j), p.c) + win()],
                self.line_b.at[(j - 1, self.span()) + win()],
                self.slot(1, j),
                p.at(b=p.next_b(j)),
            )
        )

    def to_pair(self, j):
        p = self.p
        self.go(
            lambda: (
                self.part.at[(self.span(), p.next_b(j), p.c) + self.half(1 - p.h)],
                self.pair.at[(self.span(), j) + self.half(1 - p.h)],
                self.slot(2, j),
                p.twin(),
            )
        )

    def to_a(self):
        p, end = self.p, self.end
        partial = self.last - self.first < p.A
        for j in range(1, p.A):

            def when(j=j):
                a = p.next_a(j)
                return both(a >= self.first, a < self.last) if partial else None

            end.go(
                lambda j=j: (
                    self.part.at[(p.next_a(j), p.b, p.c) + self.half(p.h)],
                    self.line_a.at[(j - 1,) + self.half(p.h)],
                    end.slot(3, j),
                    p.at(a=p.next_a(j)),
                ),
                when,
            )

    def add_b(self, win):
        p = self.p
        mine = (self.span(), p.b, p.c) + win
        total = self.part[mine].astype(F32)
        for j in range(1, p.B):
            got = (j - 1, self.span()) + win
            self.arrived(self.line_b.at[got], self.slot(1, j))
            total = total + self.line_b[got].astype(F32)
        self.part[mine] = total.astype(BF16)

    def add_pair(self, j):
        p = self.p
        got = (self.span(), j) + self.half(p.h)
        mine = (self.span(), p.next_b(j), p.c) + self.half(p.h)
        self.arrived(self.pair.at[got], self.slot(2, j))
        self.part[mine] = self.part[mine] + self.pair[got]

    def second(self):
        p = self.p
        if self.pair_first:
            for j in self.order():
                self.add_pair(j)
                if j > 0:
                    self.to_b(j, lambda: self.half(p.h))
        else:
            self.add_b(self.win())
            self.to_pair(0)

    def third(self):
        p = self.p
        if self.pair_first:
            self.add_b(self.half(p.h))
        else:
            self.add_pair(0)
        self.to_a()

    def after_a(self):
        p = self.p
        mine = self.half(p.h)
        total = self.part[(p.a, p.b, p.c) + mine].astype(F32)
        for j in range(1, p.A):
            got = (j - 1,) + mine
            self.arrived(self.line_a.at[got], self.slot(3, j))
            total = total + self.line_a[got].astype(F32)
        for i, bit in enumerate(p.bits()):
            k = self.slot(5, i)
            self.wide[(2 * i,) + mine] = total.astype(BF16)

            def copy(i=i, k=k, bit=bit):
                here = self.half(p.h)
                return (
                    self.wide.at[(2 * i,) + here],
                    self.wide.at[(2 * i + 1,) + here],
                    k,
                    p.twin(bit),
                )

            self.go(copy)
            self.arrived(self.wide.at[(2 * i + 1,) + mine], k)
            total = self.wide[(2 * i,) + mine].astype(F32)
            total = total + self.wide[(2 * i + 1,) + mine].astype(F32)
        self.done[mine] = total.astype(BF16)
        self.go(
            lambda: (
                self.done.at[self.half(p.h)],
                self.done.at[self.half(p.h)],
                self.slot(4),
                p.twin(),
            )
        )

    def finish(self):
        p = self.p
        self.arrived(self.done.at[self.half(1 - p.h)], self.slot(4))

    def steps(self):
        return [self.start, self.after_core, self.second, self.third, self.after_a, self.finish]


class SmallReduce:
    def __init__(self, place, slots, send, recv, sends):
        self.p, self.slots, self.send, self.recv, self.sends = place, slots, send, recv, sends
        self.now, self.free, self.k = 0, 1, 0

    def copy(self, src, dst, k, device):
        return remote(self.slots.at[src], self.slots.at[dst], self.send.at[k], self.recv.at[k], device)

    def exchange(self, devices):
        self.fresh = []
        for device in devices:
            src, dst, k = self.now, self.free, self.k
            self.fresh.append((dst, k))
            self.sends.go(
                lambda src=src, dst=dst, k=k, device=device: (
                    None,
                    lambda: self.copy(src, dst, k, device()),
                )
            )
            self.free, self.k = self.free + 1, self.k + 1

    def add(self):
        total = self.slots[self.now]
        for slot, k in self.fresh:
            self.copy(slot, slot, k, self.p.sibling()).wait_recv()
            total = total + self.slots[slot]
        self.slots[self.free] = total
        self.now, self.free = self.free, self.free + 1

    def steps(self):
        p = self.p
        stages = [
            [p.sibling],
            [lambda j=j: p.at(b=p.next_b(j)) for j in range(1, p.B)],
            [p.twin],
            [lambda j=j: p.at(a=p.next_a(j)) for j in range(1, p.A)],
        ] + [[functools.partial(p.twin, bit)] for bit in p.bits()]
        out = [lambda: self.exchange(stages[0])]
        for stage in stages[1:]:
            out.append(lambda stage=stage: (self.add(), self.exchange(stage)))
        out.append(self.add)
        return out

    @staticmethod
    def counts(reps, shards):
        wide = max(reps.bit_length() - 2, 0)
        copies = 1 + (shards // 8 - 1) + 1 + 3 + wide
        return copies, 1 + copies + 4 + wide


def dot(lhs, rhs):
    return lax.dot_general(lhs, rhs, (((1,), (0,)), ((), ())), preferred_element_type=F32)


def dot_nt(lhs, rhs):
    return lax.dot_general(lhs, rhs, (((1,), (1,)), ((), ())), preferred_element_type=F32)


def dot_tn(lhs, rhs):
    return lax.dot_general(lhs, rhs, (((0,), (0,)), ((), ())), preferred_element_type=F32)


def iota(shape, axis):
    return lax.broadcasted_iota(jnp.int32, shape, axis)


def mean_last(value):
    return jnp.sum(value, axis=-1, keepdims=True) * (1.0 / value.shape[-1])


def column_sum(value):
    return jnp.sum(value, axis=0, keepdims=True)


def twice(value):
    return jnp.concatenate([value, value], axis=1)


def feature(value):
    return jnp.where(value > 0, value + 1.0, jnp.exp(jnp.minimum(value, 0.0)))


def layer_kernel(reps, shards, length, n):
    p = Place(reps, shards)
    A, B = p.A, p.B
    rows_w = n.w_query.shape[0]
    R = rows_w
    chunks = length // CHUNK
    full, part, smalls, slots, vecs = n.full, n.part, n.smalls, n.slots, n.vecs

    mine = full.at[p.a, p.b, p.c]
    pieces = [
        (ref, mine.at[pl.ds(i * R, R)])
        for i, ref in enumerate((n.w_query, n.w_key, n.w_value, n.w_out))
    ]
    pieces += [
        (n.w_up.at[:, pl.ds(i * WIDTH, WIDTH)], mine.at[pl.ds((4 + i) * R, R)]) for i in range(4)
    ]
    pieces += [(n.w_down, mine.at[pl.ds(8 * R, 4 * R)])]
    pieces += [(n.inputs_far, n.inputs), (n.cotangent_far, n.cotangent)]
    local = [
        pltpu.make_async_copy(src, dst, n.sem_local.at[i]) for i, (src, dst) in enumerate(pieces)
    ]
    for copy in local:
        copy.start()
    smalls[p.a, p.b, p.c] = jnp.zeros((8, 128), F32)
    vectors = (n.b_up, n.b_down, n.gain_attn, n.shift_attn, n.gain_ffn, n.shift_ffn)
    for i, ref in enumerate(vectors):
        size = ref.shape[0]
        smalls[p.a, p.b, p.c, i : i + 1, 0:size] = ref[...].astype(F32).reshape(1, size)
    greet(p.partners())
    for copy in local[:9]:
        copy.wait()

    sends = Sends()
    tiny = SmallGather(p, smalls, n.send0, n.recv0, sends)
    windows = ((0 * R, 3 * R, 0, 512), (3 * R, 5 * R, 0, 512), (8 * R, 4 * R, 0, 512))
    gather_0, gather_1, gather_2 = (
        Gather(p, full, window, n.send1, n.recv1, i * Gather.n_sems(shards), sends)
        for i, window in enumerate(windows)
    )
    bufs = (n.core, n.line_b, n.pair, n.line_a, n.wide, n.done)

    made = []

    def job(lo, rows, at=0, lanes=WIDTH, **more):
        base = sum(one.n_sems() for one in made)
        window = (lo * R, rows * R, at, lanes)
        made.append(Reduce(p, part, bufs, window, (n.send2, n.recv2), base, sends, **more))
        return made[-1]

    up_one = job(4, 2)
    up_two = job(6, 2, pair_first=True)
    down_one = job(8, 4, pair_first=True, span=(0, 2))
    down_two = job(8, 4, span=(2, 4), end=down_one)
    out_all = job(3, 1)
    attn_one = job(0, 3, 0, 256)
    attn_two = job(0, 1, 256, 256)
    attn_three = job(1, 2, 256, 256, pair_first=True)
    assert sum(one.n_sems() for one in made) <= n.recv2.shape[0]
    small_sum = SmallReduce(p, slots, n.send3, n.recv3, sends)
    T = small_sum.steps()

    def rows_of(t, size=CHUNK):
        return pl.ds(pl.multiple_of(t * size, size), size)

    def per_chunk(events, body, down=False, size=CHUNK):
        chunks = length // size

        def step(i, carry):
            body(chunks - 1 - i if down else i)
            for at, calls in enumerate(events):
                if calls:

                    @pl.when(i == at)
                    def _():
                        for call in calls:
                            call()

            return carry

        lax.fori_loop(0, chunks, step, 0)

    gather_0.own()
    tiny.own()
    tiny.second()
    gather_1.own()
    tiny.third()

    seg_row = n.segment_ids[...].astype(F32)
    seg_rows = n.seg_rows
    seg_rows[0:8, :] = jnp.full((8, 128), -1.0, F32)
    seg_rows[pl.ds(8, length), :] = jnp.broadcast_to(seg_row, (128, length)).T
    seg_rows[pl.ds(8 + length, 8), :] = jnp.full((8, 128), -2.0, F32)
    heads, mask, mask_t = n.heads, n.mask, n.mask_t
    for i in range(PER_GROUP):
        heads[i] = jnp.where(iota((CHUNK, GROUP), 1) // HEAD_DIM == i, 1.0, 0.0).astype(BF16)
    same_head = (iota((GROUP, GROUP), 0) // HEAD_DIM) == (iota((GROUP, GROUP), 1) // HEAD_DIM)
    n.ones[...] = jnp.where(same_head, 1.0, 0.0).astype(BF16)
    later_row = iota((CHUNK, CHUNK), 0) >= iota((CHUNK, CHUNK), 1)
    later_col = iota((CHUNK, CHUNK), 0) <= iota((CHUNK, CHUNK), 1)
    for t in range(chunks):
        same = twice(seg_rows[pl.ds(8 + t * CHUNK, CHUNK), :]) == seg_row[
            :, t * CHUNK : (t + 1) * CHUNK
        ]
        mask[t] = jnp.where(same & later_row, 1.0, 0.0).astype(BF16)
        mask_t[t] = jnp.where(same & later_col, 1.0, 0.0).astype(BF16)

    def seg_chunk(t):
        return seg_rows[pl.ds(pl.multiple_of(8 + t * CHUNK, 8), CHUNK), :]

    def seg_at(t, row):
        return seg_rows[pl.ds(8 + t * CHUNK + row, 1), :]

    def flags(one, two):
        return twice(jnp.where(one == two, 1.0, 0.0))

    gather_0.line_a(1)
    tiny.last()
    gather_0.line_a(2)
    gather_0.line_a(0)
    gather_0.line_b(1)
    gather_0.line_b(2)
    gather_0.line_b(0)
    gather_1.line_a(1)
    gather_0.line_b_own()
    gather_1.line_a(2)

    local[9].wait()
    def norm_one(t):
        at = rows_of(t)
        h = n.inputs[at].astype(F32)
        centre = h - mean_last(h)
        scale = lax.rsqrt(mean_last(centre * centre) + epsilon)
        n.normal_one[at] = (centre * scale).astype(BF16)
        n.scale_one[at] = jnp.broadcast_to(scale, (CHUNK, 128))

    per_chunk([], norm_one)
    gather_0.twin(2)
    gather_1.line_a(0)
    gather_0.twin(0)
    gather_0.twin(1)
    gather_2.own()

    blocks = smalls[...].reshape(shards * 8, 128).astype(BF16)
    lane = iota((128, WIDTH), 1)
    row = iota((128, WIDTH), 0)
    block = iota((shards, 8, WIDTH), 0)
    at_lane = iota((shards, 8, WIDTH), 2)
    spread = jnp.where(lane % R == row, 1.0, 0.0).astype(BF16)
    laid = dot(blocks, spread).reshape(shards, 8, WIDTH)
    vecs[0:8] = jnp.sum(jnp.where(at_lane // R == block, laid, 0.0), axis=0)
    spread = jnp.where(lane % (4 * R) == row, 1.0, 0.0).astype(BF16)
    laid = dot(blocks, spread).reshape(shards, 8, WIDTH)
    for i in range(4):
        picked = jnp.where((at_lane + i * WIDTH) // (4 * R) == block, laid, 0.0)
        vecs[8 + i : 9 + i] = jnp.sum(picked, axis=0)[0:1]
    b_down, gain_one, shift_one, gain_two, shift_two = (vecs[i : i + 1] for i in range(1, 6))

    gather_0.rest()
    gather_1.line_b(1)

    def weight(i):
        return full[:, :, :, i * R : (i + 1) * R, :].reshape(WIDTH, WIDTH)

    def weight_down(i):
        return full[i, :, :, 8 * R : 12 * R, :].reshape(WIDTH, WIDTH)

    lanes = [slice(g * GROUP, (g + 1) * GROUP) for g in range(GROUPS)]
    state, state_now, keys_now = n.state, n.state_now, n.keys_now
    state_now[...] = jnp.zeros(state_now.shape, F32)
    keys_now[...] = jnp.zeros(keys_now.shape, F32)
    slots[0] = jnp.zeros(slots.shape[1:], F32)

    def project(t):
        at = rows_of(t, 512)
        normed = (n.normal_one[at].astype(F32) * gain_one + shift_one).astype(BF16)
        n.normed_attn[at] = normed
        n.query[at] = feature(dot(normed, weight(0))).astype(BF16)
        n.key[at] = feature(dot(normed, weight(1))).astype(BF16)
        n.value[at] = dot(normed, weight(2)).astype(BF16)

    def forward(g):
        cut = lanes[g]

        def body(t):
            at = rows_of(t)
            q, k, v = n.query[at, cut], n.key[at, cut], n.value[at, cut]
            seg = seg_chunk(t)
            before = flags(seg, seg_at(t, -1))
            ending = flags(seg, seg_at(t, CHUNK - 1)).astype(BF16)
            carry = flags(seg_at(t, CHUNK - 1), seg_at(t, -1))
            old = state_now[g].astype(BF16)
            state[g, t] = old
            mixed = dot(q * before.astype(BF16), old)
            for i in range(PER_GROUP):
                scores = dot_nt(q * heads[i], k).astype(BF16) * mask[t]
                mixed = mixed + dot(scores, v * heads[i])
            sums = dot(mask[t], k) + before * keys_now[g, 0:1]
            n.key_sums[at, cut] = sums
            totals = dot((q.astype(F32) * sums).astype(BF16), n.ones[...])
            inverse = 1.0 / totals
            n.inverse[at, cut] = inverse
            n.context[at, cut] = (mixed * inverse).astype(BF16)
            ended = k * ending
            state_now[g] = state_now[g] * carry + dot_tn(ended, v) * n.ones[...].astype(F32)
            keys_now[g, 0:1] = keys_now[g, 0:1] * carry + column_sum(ended.astype(F32))

        return body

    per_chunk([[], []], project, size=512)
    gather_1.line_b(2)
    per_chunk([[], [], [(lambda: gather_1.line_b(0))], []], forward(0))
    per_chunk([[gather_2.line_b_own, (lambda: gather_2.line_a(0))], [(lambda: gather_1.twin(1))], [gather_1.line_b_own, (lambda: gather_1.twin(2)), (lambda: gather_1.twin(0)), (lambda: gather_2.line_a(1))], []], forward(1))
    gather_1.rest()

    c0 = 0.7978845608028654
    c1 = c0 * 0.044715

    def norm_two(t):
        at = rows_of(t, 512)
        after = n.inputs[at].astype(F32) + dot(n.context[at], weight(3))
        centre = after - mean_last(after)
        scale = lax.rsqrt(mean_last(centre * centre) + epsilon)
        normal = centre * scale
        n.normal_two[at] = normal.astype(BF16)
        n.scale_two[at] = jnp.broadcast_to(scale, (512, 128))
        n.normed_ffn[at] = (normal * gain_two + shift_two).astype(BF16)
        n.result[at] = after + b_down

    def hidden_units(i):
        cut = slice(i * WIDTH, (i + 1) * WIDTH)
        pre = dot(n.normed_ffn[...], weight(4 + i)) + vecs[8 + i : 9 + i]
        square = pre * pre
        half = 0.5 + 0.5 * jnp.tanh(pre * (c0 + c1 * square))
        hidden = pre * half
        slope = half + hidden * (1.0 - half) * (2.0 * c0 + (6.0 * c1) * square)
        n.hidden[:, cut] = hidden.astype(BF16)
        n.grad_pre[:, cut] = slope.astype(BF16)

    per_chunk([[(lambda: gather_2.line_a(2))], [(lambda: gather_2.line_b(0))]], norm_two, size=512)
    hidden_units(0)
    gather_2.line_b(1)
    hidden_units(1)
    gather_2.line_b(2)
    hidden_units(2)
    hidden_units(3)
    local[10].wait()

    def down_grads(i):
        for m in range(2):
            some = slice(i * WIDTH + m * 256, i * WIDTH + (m + 1) * 256)
            grad = dot_tn(n.hidden[:, some], n.cotangent[...]).astype(BF16)
            part[i, m * B // 2 : (m + 1) * B // 2, :, 8 * R : 12 * R, :] = grad.reshape(
                B // 2, 2, 4 * R, WIDTH
            )

    down_grads(0)
    gather_2.twin(1)
    gather_2.twin(0)
    gather_2.twin(2)
    down_grads(1)
    down_grads(2)
    down_grads(3)
    down_two.start()
    down_one.start()
    gather_2.rest()

    def ffn(i):
        cut = slice(i * WIDTH, (i + 1) * WIDTH)
        grad = dot_nt(n.cotangent[...], weight_down(i)) * n.grad_pre[:, cut].astype(F32)
        grad = grad.astype(BF16)
        n.grad_pre[:, cut] = grad
        slots[0, i : i + 1] += column_sum(grad.astype(F32))

    def up_grads(i):
        cut = slice(i * WIDTH, (i + 1) * WIDTH)
        for m in range(2):
            some = slice(m * 256, (m + 1) * 256)
            grad = dot_tn(n.normed_ffn[:, some], n.grad_pre[:, cut]).astype(BF16)
            part[2 * m : 2 * m + 2, :, :, (4 + i) * R : (5 + i) * R, :] = grad.reshape(
                2, B, 2, R, WIDTH
            )

    ffn(0)
    up_grads(0)
    ffn(1)
    up_grads(1)
    up_one.start()
    down_two.after_core()
    ffn(2)
    up_grads(2)
    ffn(3)
    down_one.after_core()
    up_grads(3)
    up_two.start()

    def norm_two_back(t):
        at = rows_of(t, 512)
        grad = dot_nt(n.grad_pre[at, 0:WIDTH], weight(4))
        for i in range(1, 4):
            grad = grad + dot_nt(n.grad_pre[at, i * WIDTH : (i + 1) * WIDTH], weight(4 + i))
        normal = n.normal_two[at].astype(F32)
        up = n.cotangent[at].astype(F32)
        slots[0, 4:5] += column_sum(up)
        slots[0, 7:8] += column_sum(grad * normal)
        slots[0, 8:9] += column_sum(grad)
        e = grad * gain_two
        back = e - mean_last(e) - normal * mean_last(e * normal)
        after = up + n.scale_two[at][:, 0:1] * back
        n.grad_normed[at] = after
        low = after.astype(BF16)
        n.grad_attn[at] = low
        grad_context = dot_nt(low, weight(3)).astype(BF16).astype(F32)
        inverse = n.inverse[at]
        n.grad_mixed[at] = (grad_context * inverse).astype(BF16)
        turned = (grad_context * n.context[at].astype(F32)).astype(BF16)
        for g in range(GROUPS):
            n.grad_totals[at, lanes[g]] = -dot(turned[:, lanes[g]], n.ones[...]) * inverse[
                :, lanes[g]
            ]

    per_chunk([[up_one.after_core], []], norm_two_back, size=512)
    for m in range(2):
        grad = dot_tn(n.context[:, m * 256 : (m + 1) * 256], n.grad_attn[...]).astype(BF16)
        part[2 * m : 2 * m + 2, :, :, 3 * R : 4 * R, :] = grad.reshape(2, B, 2, R, WIDTH)

    def backward(g):
        state_now[g] = jnp.zeros((GROUP, GROUP), F32)
        keys_now[g] = jnp.zeros((8, GROUP), F32)

        def body(t):
            at = rows_of(t)
            seg = seg_chunk(t)
            before = flags(seg, seg_at(t, -1)).astype(BF16)
            after = flags(seg, seg_at(t, CHUNK))
            opening = flags(seg, seg_at(t, 0)).astype(BF16)
            carry = flags(seg_at(t, 0), seg_at(t, CHUNK))
            q, k, v, gm = (
                ref[at, lanes[g]] for ref in (n.query, n.key, n.value, n.grad_mixed)
            )
            totals = n.grad_totals[at, lanes[g]]
            old = state_now[g].astype(BF16)
            weighted = totals * q.astype(F32)
            gq = dot_nt(gm * before, state[g, t]) + totals * n.key_sums[at, lanes[g]]
            gk = after * (dot_nt(v, old) + keys_now[g, 0:1]) + dot(mask_t[t], weighted.astype(BF16))
            gv = after * dot(k, old)
            for i in range(PER_GROUP):
                head = heads[i]
                gm_head = gm * head
                back = dot_nt(gm_head, v).astype(BF16) * mask[t]
                gq = gq + dot(back, k * head)
                back = dot_nt(v * head, gm).astype(BF16) * mask_t[t]
                gk = gk + dot(back, q * head)
                back = dot_nt(k * head, q).astype(BF16) * mask_t[t]
                gv = gv + dot(back, gm_head)
            n.grad_query[at, lanes[g]] = (gq * jnp.minimum(q.astype(F32), 1.0)).astype(BF16)
            n.grad_key[at, lanes[g]] = (gk * jnp.minimum(k.astype(F32), 1.0)).astype(BF16)
            n.grad_value[at, lanes[g]] = gv.astype(BF16)
            opened = q * opening
            state_now[g] = state_now[g] * carry + dot_tn(opened, gm) * n.ones[...].astype(F32)
            keys_now[g, 0:1] = keys_now[g, 0:1] * carry + column_sum(
                weighted * opening.astype(F32)
            )

        return body

    def weight_grads(g):
        for i, ref in enumerate((n.grad_query, n.grad_key, n.grad_value)):
            grad = dot_tn(n.normed_attn[...], ref[:, lanes[g]]).astype(BF16)
            part[:, :, :, i * R : (i + 1) * R, lanes[g]] = grad.reshape(A, B, 2, R, GROUP)

    per_chunk([[down_two.second, down_one.second], [], [out_all.start, up_two.after_core], []], backward(0), down=True)
    out_all.after_core()
    down_two.third()
    weight_grads(0)
    attn_one.start()
    per_chunk([[down_one.third, attn_one.after_core, up_one.second], [], [out_all.second], []], backward(1), down=True)
    up_two.second()
    weight_grads(1)
    attn_one.second()
    up_one.third()
    attn_three.start()
    attn_two.start()

    def norm_one_back(t):
        at = rows_of(t, 512)
        grad = dot_nt(n.grad_query[at], weight(0))
        grad = grad + dot_nt(n.grad_key[at], weight(1))
        grad = grad + dot_nt(n.grad_value[at], weight(2))
        normal = n.normal_one[at].astype(F32)
        slots[0, 5:6] += column_sum(grad * normal)
        slots[0, 6:7] += column_sum(grad)
        e = grad * gain_one
        back = e - mean_last(e) - normal * mean_last(e * normal)
        n.grad_normed[at] = n.grad_normed[at] + n.scale_one[at][:, 0:1] * back

    per_chunk([[attn_two.after_core, attn_three.after_core, out_all.third], []], norm_one_back, size=512)
    store = pltpu.make_async_copy(n.grad_normed, n.grad_inputs_far, n.sem_local.at[11])
    store.start()
    up_two.third()
    attn_one.third()
    T[0]()
    T[1]()
    down_one.after_a()
    attn_three.second()
    attn_two.second()
    up_one.after_a()

    def outputs(t):
        at = rows_of(t, 512)
        total = n.result[at]
        for i in range(4):
            total = total + dot(n.hidden[at, i * WIDTH : (i + 1) * WIDTH], weight_down(i))
        n.output[at] = total.astype(BF16)

    per_chunk([[attn_two.third, T[2], attn_three.third, up_one.finish, out_all.after_a, T[3], up_two.after_a], []], outputs, size=512)
    store_more = pltpu.make_async_copy(n.output, n.output_far, n.sem_local.at[12])
    store_more.start()
    down_one.finish()
    attn_two.after_a()
    attn_one.after_a()
    out_all.finish()
    attn_three.after_a()
    attn_two.finish()
    attn_three.finish()
    up_two.finish()
    attn_one.finish()
    T[4]()

    total = slots[small_sum.now]
    high = total.astype(BF16)
    low = (total - high.astype(F32)).astype(BF16)
    row, lane = iota((WIDTH, 128), 0), iota((WIDTH, 128), 1)
    pick = jnp.where((row == lane + p.s * R) & (lane < R), 1.0, 0.0).astype(BF16)
    n.tiny_out[0:16] = dot(high, pick) + dot(low, pick)
    picked = jnp.zeros((16, 128), F32)
    for i in range(4):
        wanted = (row + i * WIDTH == lane + p.s * (4 * R)) & (lane < 4 * R)
        pick = jnp.where(wanted, 1.0, 0.0).astype(BF16)
        keep = iota((16, 128), 0) == i
        picked = picked + jnp.where(keep, dot(high, pick) + dot(low, pick), 0.0)
    n.tiny_out[16:17] = column_sum(picked)

    store.wait()
    store_more.wait()
    sends.finish()


PIECES = 2


def final_kernel(output, grad_inputs, done, tiny, *refs):
    outs = refs[:14]
    held_out, held_grad, held_done, held_tiny = refs[14:18]
    held = refs[18:-2]
    sem, more = refs[-2:]
    rows = output.shape[0] // PIECES
    first = [
        pltpu.make_async_copy(done, held_done, more.at[0]),
        pltpu.make_async_copy(tiny, held_tiny, more.at[1]),
    ]
    into, back = [], []
    for i in range(PIECES):
        cut = pl.ds(i * rows, rows)
        for k, (src, mid, dst) in enumerate(
            ((grad_inputs, held_grad, outs[1]), (output, held_out, outs[0]))
        ):
            into.append(pltpu.make_async_copy(src.at[cut], mid.at[cut], sem.at[0, k, i]))
            back.append(pltpu.make_async_copy(mid.at[cut], dst.at[cut], sem.at[1, k, i]))
    for copy in first + into:
        copy.start()
    for copy in first:
        copy.wait()
    R = held[0].shape[0]
    for i in range(4):
        held[i][...] = held_done[i * R : (i + 1) * R].astype(F32)
        held[4][:, i * WIDTH : (i + 1) * WIDTH] = held_done[(4 + i) * R : (5 + i) * R].astype(F32)
    held[5][...] = held_done[8 * R : 12 * R].astype(F32)
    for i in range(6):
        back.append(pltpu.make_async_copy(held[i], outs[2 + i], more.at[2 + i]))
        back[-1].start()
    for ref, row in zip(outs[8:14], (16, 4, 5, 6, 7, 8), strict=True):
        ref[...] = held_tiny[row, : ref.shape[0]]
    for one, two in zip(into, back, strict=False):
        one.wait()
        two.start()
    for copy in back:
        copy.wait()


def final(output, grad_inputs, done, tiny):
    R = done.shape[0] // 12
    vmem, far = pl.BlockSpec(memory_space=pltpu.VMEM), pl.BlockSpec(memory_space=pl.ANY)
    grads = [((R, WIDTH), F32)] * 4 + [((R, 4 * WIDTH), F32), ((4 * R, WIDTH), F32)]
    shapes = [(output.shape, BF16), (grad_inputs.shape, F32)] + grads
    shapes += [((4 * R,), F32)] + [((R,), F32)] * 5
    return pl.pallas_call(
        final_kernel,
        out_shape=tuple(jax.ShapeDtypeStruct(*shape) for shape in shapes),
        in_specs=[far] * 4,
        out_specs=(far,) * 8 + (vmem,) * 6,
        scratch_shapes=[
            pltpu.VMEM(output.shape, BF16),
            pltpu.VMEM(grad_inputs.shape, F32),
            pltpu.VMEM(done.shape, BF16),
            pltpu.VMEM(tiny.shape, F32),
        ]
        + [pltpu.VMEM(*shape) for shape in grads]
        + [pltpu.SemaphoreType.DMA((2, 2, PIECES)), pltpu.SemaphoreType.DMA((8,))],
        name="final",
    )(output, grad_inputs, done, tiny)


def layer(reps, shards, inputs, segment_ids, weights, vectors, cotangent):
    length = inputs.shape[0]
    A, B = 4, shards // 8
    R = weights[0].shape[0]
    rows = 12 * R
    bits = max(reps.bit_length() - 2, 0)
    copies, n_slots = SmallReduce.counts(reps, shards)
    sums = 5 * (2 * B + A + bits) + 3 * (3 * B - 1 + A + bits) + 1 * (3 * B - 1)
    groups = 3
    w_query, w_key, w_value, w_out, w_up, w_down = weights
    b_up, b_down, gain_attn, shift_attn, gain_ffn, shift_ffn = vectors
    far_ins = dict(
        inputs_far=inputs,
        cotangent_far=cotangent,
        w_query=w_query,
        w_key=w_key,
        w_value=w_value,
        w_out=w_out,
        w_up=w_up,
        w_down=w_down,
    )
    ins = dict(
        segment_ids=segment_ids,
        b_up=b_up,
        b_down=b_down,
        gain_attn=gain_attn,
        shift_attn=shift_attn,
        gain_ffn=gain_ffn,
        shift_ffn=shift_ffn,
    )
    far_outs = dict(
        output_far=((length, WIDTH), BF16),
        grad_inputs_far=((length, WIDTH), F32),
    )
    outs = dict(
        done=((rows, WIDTH), BF16),
        tiny_out=((24, 128), F32),
    )
    tall = (length, WIDTH)
    buffers = dict(
        inputs=(tall, BF16),
        cotangent=(tall, BF16),
        result=(tall, F32),
        full=((A, B, 2, rows, WIDTH), BF16),
        part=((A, B, 2, rows, WIDTH), BF16),
        core=((A, B, rows, WIDTH), BF16),
        line_b=((B - 1, A, rows, WIDTH), BF16),
        pair=((A, B, rows, WIDTH), BF16),
        line_a=((A - 1, rows, WIDTH), BF16),
        wide=((max(2 * bits, 1), rows if bits else 16, WIDTH), BF16),
        smalls=((A, B, 2, 8, 128), F32),
        slots=((n_slots, 16, WIDTH), F32),
        vecs=((16, WIDTH), F32),
        seg_rows=((length + 16, 128), F32),
        heads=((PER_GROUP, CHUNK, GROUP), BF16),
        ones=((GROUP, GROUP), BF16),
        mask=((length // CHUNK, CHUNK, CHUNK), BF16),
        mask_t=((length // CHUNK, CHUNK, CHUNK), BF16),
        normal_one=(tall, BF16),
        scale_one=((length, 128), F32),
        normed_attn=(tall, BF16),
        query=(tall, BF16),
        key=(tall, BF16),
        value=(tall, BF16),
        key_sums=(tall, F32),
        inverse=(tall, F32),
        context=(tall, BF16),
        state=((GROUPS, length // CHUNK, GROUP, GROUP), BF16),
        state_now=((GROUPS, GROUP, GROUP), F32),
        keys_now=((GROUPS, 8, GROUP), F32),
        normal_two=(tall, BF16),
        scale_two=((length, 128), F32),
        normed_ffn=(tall, BF16),
        hidden=((length, 4 * WIDTH), BF16),
        grad_pre=((length, 4 * WIDTH), BF16),
        grad_normed=(tall, F32),
        grad_mixed=(tall, BF16),
        grad_totals=(tall, F32),
    )
    sems = dict(
        sem_local=(13,),
        send0=(A + B,),
        recv0=(A + B,),
        send1=(groups * Gather.n_sems(shards),),
        recv1=(groups * Gather.n_sems(shards),),
        send2=(sums,),
        recv2=(sums,),
        send3=(copies,),
        recv3=(copies,),
    )
    names = [*far_ins, *ins, *far_outs, *outs, *buffers, *sems]

    def kernel(*refs):
        n = types.SimpleNamespace(**dict(zip(names, refs, strict=True)))
        n.output, n.grad_attn = n.inputs, n.normed_ffn
        n.grad_query, n.grad_key, n.grad_value = (
            n.grad_pre.at[:, pl.ds(i * WIDTH, WIDTH)] for i in range(3)
        )
        layer_kernel(reps, shards, length, n)

    vmem, far = pl.BlockSpec(memory_space=pltpu.VMEM), pl.BlockSpec(memory_space=pl.ANY)
    flops = 2 * 3 * length * WIDTH * WIDTH * 12 + 20 * length * length * WIDTH
    return pl.pallas_call(
        kernel,
        out_shape=tuple(
            jax.ShapeDtypeStruct(*spec) for spec in [*far_outs.values(), *outs.values()]
        ),
        in_specs=[far] * len(far_ins) + [vmem] * len(ins),
        out_specs=(far,) * len(far_outs) + (vmem,) * len(outs),
        scratch_shapes=[pltpu.VMEM(*spec) for spec in buffers.values()]
        + [pltpu.SemaphoreType.DMA(shape) for shape in sems.values()],
        compiler_params=pltpu.CompilerParams(
            collective_id=1, has_side_effects=True, vmem_limit_bytes=63 << 20
        ),
        cost_estimate=pl.CostEstimate(flops=flops, bytes_accessed=8 << 20, transcendentals=0),
        name="layer",
    )(*far_ins.values(), *ins.values())


def on_device(
    reps,
    shards,
    inputs,
    segment_ids,
    w_query,
    w_key,
    w_value,
    w_out,
    w_up,
    w_down,
    b_up,
    b_down,
    gain_attn,
    shift_attn,
    gain_ffn,
    shift_ffn,
    cotangent,
):
    sequences, length, width = inputs.shape
    output, grad_inputs, done, tiny = layer(
        reps,
        shards,
        inputs.reshape(sequences * length, width),
        segment_ids,
        (w_query, w_key, w_value, w_out, w_up, w_down),
        (b_up, b_down, gain_attn, shift_attn, gain_ffn, shift_ffn),
        cotangent.reshape(sequences * length, width),
    )
    output, grad_inputs, *grads = final(output, grad_inputs, done, tiny)
    return (output.reshape(inputs.shape), grad_inputs.reshape(inputs.shape), *grads)


def solution(mesh):
    reps, shards = mesh.shape["rep"], mesh.shape["shard"]
    token = P(("rep", "shard"), None, None)
    matrix, vector = P("shard", None), P("shard")
    return jax.shard_map(
        functools.partial(on_device, reps, shards),
        mesh=mesh,
        in_specs=(token, P(("rep", "shard"), None)) + (matrix,) * 6 + (vector,) * 6 + (token,),
        out_specs=(token, token) + (matrix,) * 6 + (vector,) * 6,
        check_vma=False,
    )
```
